128 devices in a mesh: dp: 2 (over y_lo), outer: 4 (over z), inner: 16 (over x, y_hi, core).
Axes of the slice: x: 4, y: 4 (y_hi: 2, y_lo: 2; y = y_hi * 2 + y_lo), z: 4, core: 2. Of those that a mesh axis runs over, the one named last changes fastest.
Arguments:
- inputs: bfloat16 [2, 10240, 4096], P('dp', ('outer', 'inner')), may hold values from -6 to 6
- block_order: int32 [2, 128], P('dp'), may hold values from 0 to 127, each once within a row
- w_query: bfloat16 [4096, 512], replicated, may hold values from -0.09375 to 0.09375
- w_key: bfloat16 [4096, 128], replicated, may hold values from -1.875 to 1.875
- w_value: bfloat16 [4096, 128], replicated, may hold values from -0.09375 to 0.09375
- grad_out: bfloat16 [2, 10240, 512], P('dp', ('outer', 'inner')), may hold values from -6 to 6
Outputs:
- grad_w_query: float32 [4096, 512], P(('dp', 'outer', 'inner'))
- grad_w_key: float32 [4096, 128], P(('dp', 'outer', 'inner'))
- grad_w_value: float32 [4096, 128], P(('dp', 'outer', 'inner'))
The draws below stay inside these ranges and needn't reach their ends.
Inputs may be any that keep to these rules, and one draw needn't show every extreme that they name: Each row of block_order is a permutation of the sequence's 128 blocks; block slot b holds rows b * 80 to (b + 1) * 80 - 1 of the stored sequence.
All inputs are finite; a program needn't handle non-finite values.
Results may differ from the reference program's by a relative error of at most 0.012.
The reference program's roundings to bfloat16 on the way count: a program that leaves them out, or rounds other values in their place, can miss the bound.
Values may be sent and summed in bfloat16 or wider, within the bound.
No kernel may reach another device: no remote copies, remote signals or barrier semaphores. Data moves between devices by JAX's collectives and lax.ppermute only.
A program may use at most 192 MiB of HBM per device.

```python
import math
import jax
import jax.numpy as jnp
from jax import lax

D = 4096
GROUP = 4
HEAD = 128
SEQ_LEN = 10240
BLOCKS = 128
SEQS = 2


def shared_query(key):
    values = jax.random.normal(jax.random.fold_in(key, 7), (D, GROUP * HEAD), jnp.float32)
    return jnp.clip(values, -6.0, 6.0) * D ** (-0.5)


def draw_w_query(key, part):
    return shared_query(key).astype(jnp.bfloat16)


def draw_w_key(key, part):
    noise = jnp.clip(jax.random.normal(jax.random.fold_in(key, 9), (D, HEAD), jnp.float32), -6.0, 6.0) * D ** (-0.5)
    return noise.astype(jnp.bfloat16)


def levels(stream_key, dims, split, least, largest):
    factor_of, own = 1.0, jax.random.fold_in(stream_key, 6)
    for position, blocks in split:
        steps = jnp.exp(jax.random.uniform(jax.random.fold_in(own, position), (blocks,), jnp.float32, least / len(split), largest / len(split)))
        factor_of = factor_of * jnp.repeat(steps, dims[position] // blocks).reshape([-1 if axis == position else 1 for axis in range(len(dims))])
    return factor_of


def scatter_about(stream_key, extent, width, most, cuts=(), kind=jnp.bfloat16):
    level = levels(stream_key, extent, cuts, -0.22, 0.18) if cuts else 1.0
    values = jax.random.normal(stream_key, extent, jnp.float32) * width * level
    return jnp.minimum(jnp.maximum(values, -most), most).astype(kind)


def setup_inputs(seed: int = 0) -> dict:
    splits = jax.random.split(jax.random.key(seed), 7)
    return {
        "inputs": scatter_about(splits[0], (SEQS, SEQ_LEN, D), 1.0, 6.0, ((0, 2), (1, 64))),
        "block_order": jax.vmap(lambda own: jax.random.permutation(own, BLOCKS))(jax.random.split(splits[1], SEQS)).reshape((SEQS, BLOCKS)).astype(jnp.int32),
        "w_query": draw_w_query(jax.random.fold_in(splits[6], 71), 0),
        "w_key": draw_w_key(jax.random.fold_in(splits[6], 71), 0),
        "w_value": scatter_about(splits[4], (D, HEAD), D ** -0.5, 0.09375),
        "grad_out": scatter_about(splits[5], (SEQS, SEQ_LEN, GROUP * HEAD), 1.0, 6.0, ((0, 2), (1, 64))),
    }


masked_fill = -1e+30

def rounded(values):
    return lax.optimization_barrier(values.astype(jnp.bfloat16))

def one_sequence(tokens, order, dout_flat, w_query, w_key, w_value):
    length = tokens.shape[0]
    half = length // order.shape[0]
    head_dim = w_key.shape[1]
    heads = w_query.shape[1] // head_dim
    scale = 1.0 / math.sqrt(head_dim)
    block = math.gcd(length, 512)
    count = length // block
    positions = (order[:, None] * half + jnp.arange(half, dtype=jnp.int32)[None, :]).reshape(-1).astype(jnp.int32)
    query = rounded(jnp.dot(tokens, w_query, preferred_element_type=jnp.float32))
    key_all = rounded(jnp.dot(tokens, w_key, preferred_element_type=jnp.float32))
    value_all = rounded(jnp.dot(tokens, w_value, preferred_element_type=jnp.float32))
    key_wide = key_all.astype(jnp.float32)
    value_wide = value_all.astype(jnp.float32)
    query_blocks = query.astype(jnp.float32).reshape(count, block, heads, head_dim)
    dout_blocks = dout_flat.astype(jnp.float32).reshape(count, block, heads, head_dim)
    pos_blocks = positions.reshape(count, block)

    def scores_of(query_rows, row_pos):
        score = jnp.einsum('qhd,kd->hqk', query_rows, key_wide) * scale
        allowed = positions[None, None, :] <= row_pos[None, :, None]
        return (jnp.where(allowed, score, masked_fill), allowed)

    def stats(args):
        query_rows, dout_rows, row_pos = args
        score, allowed = scores_of(query_rows, row_pos)
        row_max = lax.optimization_barrier(jnp.max(score, axis=2))
        weights = jnp.where(allowed, jnp.exp(score - row_max[:, :, None]), 0.0)
        dprob = jnp.einsum('qhd,kd->hqk', dout_rows, value_wide)
        total = lax.optimization_barrier(jnp.sum(weights, axis=2))
        return (row_max + jnp.log(total), lax.optimization_barrier(jnp.sum(weights * dprob, axis=2)) / total)
    lse, delta = lax.map(stats, (query_blocks, dout_blocks, pos_blocks))

    def backward(carry, args):
        grad_key, grad_value = carry
        query_rows, dout_rows, row_pos, lse_rows, delta_rows = args
        score, allowed = scores_of(query_rows, row_pos)
        prob = jnp.where(allowed, jnp.exp(score - lse_rows[:, :, None]), 0.0)
        dprob = jnp.einsum('qhd,kd->hqk', dout_rows, value_wide)
        dscore = rounded(prob * (dprob - delta_rows[:, :, None])).astype(jnp.float32)
        prob_low = rounded(prob).astype(jnp.float32)
        grad_query = jnp.einsum('hqk,kd->qhd', dscore, key_wide) * scale
        grad_key = grad_key + jnp.einsum('hqk,qhd->kd', dscore, query_rows) * scale
        grad_value = grad_value + jnp.einsum('hqk,qhd->kd', prob_low, dout_rows)
        return ((grad_key, grad_value), grad_query.astype(jnp.bfloat16))
    empty = jnp.zeros((length, head_dim), jnp.float32)
    (grad_key, grad_value), grad_query = lax.scan(backward, (empty, empty), (query_blocks, dout_blocks, pos_blocks, lse, delta))
    grads = jnp.concatenate([grad_query.reshape(length, heads * head_dim), grad_key.astype(jnp.bfloat16), grad_value.astype(jnp.bfloat16)], axis=1)
    return lax.dot_general(tokens, grads, (((0,), (0,)), ((), ())), preferred_element_type=jnp.float32)

def reference(inputs, block_order, w_query, w_key, w_value, grad_out):
    summed = one_sequence(inputs[0], block_order[0], grad_out[0], w_query, w_key, w_value)
    for sequence in range(1, inputs.shape[0]):
        summed = summed + one_sequence(inputs[sequence], block_order[sequence], grad_out[sequence], w_query, w_key, w_value)
    query_width = w_query.shape[1]
    head_dim = w_key.shape[1]
    return (summed[:, :query_width], summed[:, query_width:query_width + head_dim], summed[:, query_width + head_dim:])
```

```python
import functools
import math

import jax
import jax.numpy as jnp
import numpy as np
from jax import lax
from jax.experimental import pallas as pl
from jax.experimental.pallas import tpu as pltpu
from jax.sharding import Mesh, PartitionSpec as P

masked_fill = -1e30
HEADS = 4
HEAD = 128
ROWS = 160
HALF = 80
N_OUT = 4
N_X = 4
SLOT = HEADS * ROWS
ALL_ROWS = N_OUT * SLOT
KEYS = 16 * ROWS
KHALF = KEYS // 2
RT = 512
KC = 640
SCALE = 1.0 / math.sqrt(HEAD)
SCALE2 = SCALE * math.log2(math.e)
f32 = jnp.float32
bf16 = jnp.bfloat16
NT = (((1,), (1,)), ((), ()))
NN = (((1,), (0,)), ((), ()))
TN = (((0,), (0,)), ((), ()))


def dot(a, b, dims):
    return lax.dot_general(a, b, dims, preferred_element_type=f32)


def fill_rows(pieces, rows_ref):
    for d in range(N_OUT):
        for h in range(HEADS):
            rows_ref[d * SLOT + h * ROWS : d * SLOT + (h + 1) * ROWS, :] = pieces[d][
                :, h * HEAD : (h + 1) * HEAD
            ]


def masked_scores(key_rows, q, posq, ordk_ref, chunk):
    score = dot(key_rows, q, NT)
    place = lax.broadcasted_iota(jnp.int32, (HALF, RT), 0)
    parts = []
    for b in range(KC // HALF):
        limit = posq - ordk_ref[chunk * (KC // HALF) + b] * HALF
        part = score[b * HALF : (b + 1) * HALF] * SCALE2
        parts.append(jnp.where(place <= limit, part, masked_fill))
    return jnp.concatenate(parts, axis=0)


def stats_kernel(ordk_ref, posq_ref, q0, q1, q2, q3, g0, g1, g2, g3, kva, kvb, out_ref, qr, gr):
    fill_rows((q0, q1, q2, q3), qr)
    fill_rows((g0, g1, g2, g3), gr)

    def row_tile(rt, _):
        r0 = pl.multiple_of(rt * RT, RT)
        q = qr[pl.ds(r0, RT), :]
        g = gr[pl.ds(r0, RT), :]
        posq = posq_ref[:, pl.ds(r0, RT)]
        top = jnp.full((8, RT), masked_fill, f32)
        total = jnp.zeros((8, RT), f32)
        weighted = jnp.zeros((8, RT), f32)
        for chunk in range(KEYS // KC):
            kv = kva if chunk * KC < KHALF else kvb
            k0 = chunk * KC % KHALF
            score = masked_scores(kv[k0 : k0 + KC, :HEAD], q, posq, ordk_ref, chunk)
            dprob = dot(kv[k0 : k0 + KC, HEAD:], g, NT)
            score = score.reshape(KC // 8, 8, RT)
            new_top = jnp.maximum(top, jnp.max(score, axis=0))
            weights = jnp.exp2(score - new_top[None])
            factor = jnp.exp2(top - new_top)
            total = total * factor + jnp.sum(weights, axis=0)
            weighted = weighted * factor + jnp.sum(weights * dprob.reshape(KC // 8, 8, RT), axis=0)
            top = new_top
        row_top = jnp.max(top, axis=0, keepdims=True)
        factor = jnp.exp2(top - row_top)
        out_ref[0:1, pl.ds(r0, RT)] = row_top
        out_ref[1:2, pl.ds(r0, RT)] = jnp.sum(total * factor, axis=0, keepdims=True)
        out_ref[2:3, pl.ds(r0, RT)] = jnp.sum(weighted * factor, axis=0, keepdims=True)
        return 0

    lax.fori_loop(0, ALL_ROWS // RT, row_tile, 0)


def grads_kernel(
    ordk_ref, posq_ref, s0, s1, s2, s3, q0, q1, q2, q3, g0, g1, g2, g3, kva, kvb,
    dq0, dq1, dq2, dq3, dkv_keep, dkv_send, qr, gr, dqr, dkr, dvr, lse_ref, delta_ref,
):
    fill_rows((q0, q1, q2, q3), qr)
    fill_rows((g0, g1, g2, g3), gr)
    stats = (s0, s1, s2, s3)
    for d in range(N_OUT):
        parts = []
        for e in range(N_OUT):
            c0 = (d - e) % N_OUT * SLOT
            parts.append(stats[e][:, c0 : c0 + SLOT])
        row_top = parts[0][0:1]
        for part in parts[1:]:
            row_top = jnp.maximum(row_top, part[0:1])
        total = jnp.zeros_like(row_top)
        weighted = jnp.zeros_like(row_top)
        for part in parts:
            factor = jnp.exp2(part[0:1] - row_top)
            total = total + part[1:2] * factor
            weighted = weighted + part[2:3] * factor
        lse_ref[0:1, d * SLOT : (d + 1) * SLOT] = row_top + jnp.log2(total)
        delta_ref[0:1, d * SLOT : (d + 1) * SLOT] = weighted / total
    dkr[...] = jnp.zeros_like(dkr)
    dvr[...] = jnp.zeros_like(dvr)

    def row_tile(rt, _):
        r0 = pl.multiple_of(rt * RT, RT)
        q = qr[pl.ds(r0, RT), :]
        g = gr[pl.ds(r0, RT), :]
        posq = posq_ref[:, pl.ds(r0, RT)]
        lse = lse_ref[:, pl.ds(r0, RT)]
        delta = delta_ref[:, pl.ds(r0, RT)]
        dq = jnp.zeros((RT, HEAD), f32)
        for chunk in range(KEYS // KC):
            kv = kva if chunk * KC < KHALF else kvb
            k0 = chunk * KC % KHALF
            key_rows = kv[k0 : k0 + KC, :HEAD]
            score = masked_scores(key_rows, q, posq, ordk_ref, chunk)
            prob = jnp.exp2(score - lse)
            dprob = dot(kv[k0 : k0 + KC, HEAD:], g, NT)
            dscore = (prob * (dprob - delta)).astype(bf16)
            prob_low = prob.astype(bf16)
            dvr[chunk * KC : (chunk + 1) * KC, :] += dot(prob_low, g, NN)
            dkr[chunk * KC : (chunk + 1) * KC, :] += dot(dscore, q, NN)
            dq = dq + dot(dscore, key_rows, TN)
        dqr[pl.ds(r0, RT), :] = dq * SCALE
        return 0

    lax.fori_loop(0, ALL_ROWS // RT, row_tile, 0)
    for d, out in enumerate((dq0, dq1, dq2, dq3)):
        for h in range(HEADS):
            out[:, h * HEAD : (h + 1) * HEAD] = dqr[
                d * SLOT + h * ROWS : d * SLOT + (h + 1) * ROWS, :
            ].astype(out.dtype)
    dkv_keep[:, :HEAD] = dkr[:KHALF] * SCALE
    dkv_keep[:, HEAD:] = dvr[:KHALF]
    dkv_send[:, :HEAD] = dkr[KHALF:] * SCALE
    dkv_send[:, HEAD:] = dvr[KHALF:]


smem = pl.BlockSpec(memory_space=pltpu.SMEM)
vmem = pl.BlockSpec(memory_space=pltpu.VMEM)
params = pltpu.CompilerParams(vmem_limit_bytes=50 * 1024 * 1024)


def stats_call(ordk, posq, qs, gs, kva, kvb):
    return pl.pallas_call(
        stats_kernel,
        out_shape=jax.ShapeDtypeStruct((3, ALL_ROWS), f32),
        in_specs=[smem] + [vmem] * 11,
        out_specs=vmem,
        scratch_shapes=[pltpu.VMEM((ALL_ROWS, HEAD), bf16)] * 2,
        compiler_params=params,
        name="stats",
    )(ordk, posq, *qs, *gs, kva, kvb)


def grads_call(ordk, posq, stats, qs, gs, kva, kvb):
    wide = HEADS * HEAD
    return pl.pallas_call(
        grads_kernel,
        out_shape=(
            jax.ShapeDtypeStruct((ROWS, wide), f32),
            jax.ShapeDtypeStruct((ROWS, wide), bf16),
            jax.ShapeDtypeStruct((ROWS, wide), bf16),
            jax.ShapeDtypeStruct((ROWS, wide), bf16),
            jax.ShapeDtypeStruct((KHALF, 2 * HEAD), f32),
            jax.ShapeDtypeStruct((KHALF, 2 * HEAD), f32),
        ),
        in_specs=[smem] + [vmem] * 15,
        out_specs=[vmem] * 6,
        scratch_shapes=[
            pltpu.VMEM((ALL_ROWS, HEAD), bf16),
            pltpu.VMEM((ALL_ROWS, HEAD), bf16),
            pltpu.VMEM((ALL_ROWS, HEAD), f32),
            pltpu.VMEM((KEYS, HEAD), f32),
            pltpu.VMEM((KEYS, HEAD), f32),
            pltpu.VMEM((1, ALL_ROWS), f32),
            pltpu.VMEM((1, ALL_ROWS), f32),
        ],
        compiler_params=params,
        name="grads",
    )(ordk, posq, *stats, *qs, *gs, kva, kvb)


def shift(x, axis, d, n):
    return lax.ppermute(x, axis, [(i, (i + d) % n) for i in range(n)])


def from_behind(x, axis, n):
    return [x] + [shift(x, axis, d, n) for d in range(1, n)]


def per_device(inputs, block_order, w_query, w_key, w_value, grad_out):
    tokens = inputs[0]
    order = block_order[0]
    dout = grad_out[0]
    o, ix, iy, ic = (lax.axis_index(a) for a in ("outer", "x", "yh", "core"))

    gs = from_behind(dout, "outer", N_OUT)
    kv = jnp.concatenate(
        [
            dot(tokens, w_key, NN).astype(bf16),
            dot(tokens, w_value, NN).astype(bf16),
        ],
        axis=1,
    )
    query = dot(tokens, w_query, NN).astype(bf16)

    kv = jnp.concatenate(from_behind(kv, "yh", 2), axis=0)
    qs = from_behind(query, "outer", N_OUT)
    kva = jnp.concatenate(from_behind(kv, "x", N_X), axis=0)
    kvb = shift(kva, "core", 1, 2)

    inner = np.arange(2)[:, None, None, None], np.arange(N_X)[None, :, None, None], np.arange(2)[None, None, :, None]
    step = np.arange(2)[None, None, None, :]
    key_dev = ((o * N_X + (ix - inner[1]) % N_X) * 2 + (iy - inner[2]) % 2) * 2 + (ic - inner[0]) % 2
    key_blocks = (key_dev * 2 + step).reshape(-1)
    query_dev = (((o - np.arange(N_OUT)) % N_OUT * N_X + ix) * 2 + iy) * 2 + ic
    query_blocks = (query_dev[:, None] * 2 + np.arange(2)[None, :]).reshape(-1)

    def look_up(blocks):
        hit = blocks[:, None] == jnp.arange(order.shape[0], dtype=jnp.int32)[None, :]
        return jnp.sum(jnp.where(hit, order[None, :], 0), axis=1)

    ordk = look_up(key_blocks)
    ordq = look_up(query_blocks).reshape(N_OUT, 1, 2, 1)
    posq = ordq * HALF + jnp.arange(HALF, dtype=jnp.int32)
    posq = jnp.broadcast_to(posq, (N_OUT, HEADS, 2, HALF)).reshape(1, ALL_ROWS)

    stats = stats_call(ordk, posq, qs, gs, kva, kvb)
    columns = tokens.reshape(ROWS, 2, N_OUT, -1)
    xs = []
    for d in range(N_OUT):
        part = lax.dynamic_index_in_dim(columns, (o + d) % N_OUT, axis=2, keepdims=False)
        part = part.reshape(ROWS, -1)
        xs.append(part if d == 0 else shift(part, "outer", d, N_OUT))
    all_stats = from_behind(stats, "outer", N_OUT)
    dq0, dq1, dq2, dq3, dkv_keep, dkv_send = grads_call(ordk, posq, all_stats, qs, gs, kva, kvb)

    dkv_got = shift(dkv_send, "core", 1, 2)
    dq = dq0
    for d, part in ((1, dq1), (2, dq2), (3, dq3)):
        dq = dq + shift(part, "outer", -d, N_OUT).astype(f32)
    dq_all = from_behind(dq.astype(bf16), "outer", N_OUT)

    dkv = (dkv_keep + dkv_got).reshape(N_X, 2 * ROWS, 2 * HEAD)
    low = dkv.astype(bf16)
    part = dkv[0]
    for d in range(1, N_X):
        part = part + shift(low[d], "x", -d, N_X).astype(f32)
    dkv = part[:ROWS] + shift(part[ROWS:].astype(bf16), "yh", 1, 2).astype(f32)
    dkv_all = from_behind(dkv.astype(bf16), "outer", N_OUT)

    grads = jnp.concatenate(
        [jnp.concatenate(dq_all, axis=0), jnp.concatenate(dkv_all, axis=0)], axis=1
    )
    dw = dot(jnp.concatenate(xs, axis=0), grads, TN)
    dw = dw.reshape(16, 2, -1, dw.shape[1])
    mine = lax.dynamic_index_in_dim(dw, ic, axis=1, keepdims=False)
    other = lax.dynamic_index_in_dim(dw, 1 - ic, axis=1, keepdims=False)
    dw = (mine + shift(other, "core", 1, 2)).astype(bf16)
    dw = lax.all_to_all(dw, ("dp", "x", "yh"), 0, 0, tiled=True)
    dw = jnp.sum(dw.astype(f32), axis=0)
    wide = HEADS * HEAD
    return dw[:, :wide], dw[:, wide : wide + HEAD], dw[:, wide + HEAD :]


def solution(mesh):
    devices = np.asarray(mesh.devices).reshape(2, N_OUT, N_X, 2, 2)
    fine = Mesh(devices, ("dp", "outer", "x", "yh", "core"))
    seq = ("outer", "x", "yh", "core")
    rows = P(("dp",) + seq, None)
    return jax.shard_map(
        per_device,
        mesh=fine,
        in_specs=(
            P("dp", seq, None),
            P("dp", None),
            P(None, None),
            P(None, None),
            P(None, None),
            P("dp", seq, None),
        ),
        out_specs=(rows, rows, rows),
        check_vma=False,
    )
```

```python
import functools
import math

import jax
import jax.numpy as jnp
import numpy as np
from jax import lax
from jax.experimental import pallas as pl
from jax.experimental.pallas import tpu as pltpu
from jax.sharding import Mesh, PartitionSpec as P

masked_fill = -1e30
HEADS = 4
HEAD = 128
ROWS = 160
HALF = 80
N_OUT = 4
N_X = 4
SLOT = HEADS * ROWS
ALL_ROWS = N_OUT * SLOT
KEYS = 16 * ROWS
KHALF = KEYS // 2
RT = 512
KC = 640
SCALE = 1.0 / math.sqrt(HEAD)
SCALE2 = SCALE * math.log2(math.e)
f32 = jnp.float32
bf16 = jnp.bfloat16
NT = (((1,), (1,)), ((), ()))
NN = (((1,), (0,)), ((), ()))
TN = (((0,), (0,)), ((), ()))


def dot(a, b, dims):
    return lax.dot_general(a, b, dims, preferred_element_type=f32)


def fill_rows(pieces, rows_ref):
    for d in range(N_OUT):
        for h in range(HEADS):
            rows_ref[d * SLOT + h * ROWS : d * SLOT + (h + 1) * ROWS, :] = pieces[d][
                :, h * HEAD : (h + 1) * HEAD
            ]


def masked_scores(key_rows, q, posq, ordk_ref, chunk):
    score = dot(key_rows, q, NT)
    place = lax.broadcasted_iota(jnp.int32, (HALF, RT), 0)
    parts = []
    for b in range(KC // HALF):
        limit = posq - ordk_ref[chunk * (KC // HALF) + b] * HALF
        part = score[b * HALF : (b + 1) * HALF] * SCALE2
        parts.append(jnp.where(place <= limit, part, masked_fill))
    return jnp.concatenate(parts, axis=0)


def stats_kernel(ordk_ref, posq_ref, q0, q1, q2, q3, g0, g1, g2, g3, kva, kvb, out_ref, qr, gr):
    fill_rows((q0, q1, q2, q3), qr)
    fill_rows((g0, g1, g2, g3), gr)

    def row_tile(rt, _):
        r0 = pl.multiple_of(rt * RT, RT)
        q = qr[pl.ds(r0, RT), :]
        g = gr[pl.ds(r0, RT), :]
        posq = posq_ref[:, pl.ds(r0, RT)]
        top = jnp.full((8, RT), masked_fill, f32)
        total = jnp.zeros((8, RT), f32)
        weighted = jnp.zeros((8, RT), f32)
        for chunk in range(KEYS // KC):
            kv = kva if chunk * KC < KHALF else kvb
            k0 = chunk * KC % KHALF
            score = masked_scores(kv[k0 : k0 + KC, :HEAD], q, posq, ordk_ref, chunk)
            dprob = dot(kv[k0 : k0 + KC, HEAD:], g, NT)
            score = score.reshape(KC // 8, 8, RT)
            new_top = jnp.maximum(top, jnp.max(score, axis=0))
            weights = jnp.exp2(score - new_top[None])
            factor = jnp.exp2(top - new_top)
            total = total * factor + jnp.sum(weights, axis=0)
            weighted = weighted * factor + jnp.sum(weights * dprob.reshape(KC // 8, 8, RT), axis=0)
            top = new_top
        row_top = jnp.max(top, axis=0, keepdims=True)
        factor = jnp.exp2(top - row_top)
        out_ref[0:1, pl.ds(r0, RT)] = row_top
        out_ref[1:2, pl.ds(r0, RT)] = jnp.sum(total * factor, axis=0, keepdims=True)
        out_ref[2:3, pl.ds(r0, RT)] = jnp.sum(weighted * factor, axis=0, keepdims=True)
        return 0

    lax.fori_loop(0, ALL_ROWS // RT, row_tile, 0)


def grads_kernel(
    ordk_ref, posq_ref, s0, s1, s2, s3, q0, q1, q2, q3, g0, g1, g2, g3, kva, kvb,
    dq0, dq1, dq2, dq3, dkv_keep, dkv_send, qr, gr, dqr, dkr, dvr, lse_ref, delta_ref,
):
    fill_rows((q0, q1, q2, q3), qr)
    fill_rows((g0, g1, g2, g3), gr)
    stats = (s0, s1, s2, s3)
    for d in range(N_OUT):
        parts = []
        for e in range(N_OUT):
            c0 = (d - e) % N_OUT * SLOT
            parts.append(stats[e][:, c0 : c0 + SLOT])
        row_top = parts[0][0:1]
        for part in parts[1:]:
            row_top = jnp.maximum(row_top, part[0:1])
        total = jnp.zeros_like(row_top)
        weighted = jnp.zeros_like(row_top)
        for part in parts:
            factor = jnp.exp2(part[0:1] - row_top)
            total = total + part[1:2] * factor
            weighted = weighted + part[2:3] * factor
        lse_ref[0:1, d * SLOT : (d + 1) * SLOT] = row_top + jnp.log2(total)
        delta_ref[0:1, d * SLOT : (d + 1) * SLOT] = weighted / total
    dkr[...] = jnp.zeros_like(dkr)
    dvr[...] = jnp.zeros_like(dvr)

    def row_tile(rt, _):
        r0 = pl.multiple_of(rt * RT, RT)
        q = qr[pl.ds(r0, RT), :]
        g = gr[pl.ds(r0, RT), :]
        posq = posq_ref[:, pl.ds(r0, RT)]
        lse = lse_ref[:, pl.ds(r0, RT)]
        delta = delta_ref[:, pl.ds(r0, RT)]
        dq = jnp.zeros((RT, HEAD), f32)
        for chunk in range(KEYS // KC):
            kv = kva if chunk * KC < KHALF else kvb
            k0 = chunk * KC % KHALF
            key_rows = kv[k0 : k0 + KC, :HEAD]
            score = masked_scores(key_rows, q, posq, ordk_ref, chunk)
            prob = jnp.exp2(score - lse)
            dprob = dot(kv[k0 : k0 + KC, HEAD:], g, NT)
            dscore = (prob * (dprob - delta)).astype(bf16)
            prob_low = prob.astype(bf16)
            dvr[chunk * KC : (chunk + 1) * KC, :] += dot(prob_low, g, NN)
            dkr[chunk * KC : (chunk + 1) * KC, :] += dot(dscore, q, NN)
            dq = dq + dot(dscore, key_rows, TN)
        dqr[pl.ds(r0, RT), :] = dq * SCALE
        return 0

    lax.fori_loop(0, ALL_ROWS // RT, row_tile, 0)
    for d, out in enumerate((dq0, dq1, dq2, dq3)):
        for h in range(HEADS):
            out[:, h * HEAD : (h + 1) * HEAD] = dqr[
                d * SLOT + h * ROWS : d * SLOT + (h + 1) * ROWS, :
            ].astype(out.dtype)
    dkv_keep[:, :HEAD] = dkr[:KHALF] * SCALE
    dkv_keep[:, HEAD:] = dvr[:KHALF]
    dkv_send[:, :HEAD] = dkr[KHALF:] * SCALE
    dkv_send[:, HEAD:] = dvr[KHALF:]


def columns_kernel(place_ref, tok, keep, send):
    o = place_ref[0]
    ic = place_ref[1]
    src = lax.broadcasted_iota(jnp.int32, (512, 256), 0)
    dst = lax.broadcasted_iota(jnp.int32, (512, 256), 1)
    home = dst // 32 * 64 + dst % 32
    for out, c in ((keep, ic), (send, 1 - ic)):
        pick = jnp.where(src == home + c * 32, 1.0, 0.0).astype(bf16)
        for d in range(N_OUT):
            base = lax.rem(o + d, N_OUT) * 512
            for p in range(2):
                start = pl.multiple_of(base + p * 2048, 512)
                cols = tok[:, pl.ds(start, 512)]
                out[d, :, p * 256 : (p + 1) * 256] = dot(cols, pick, NN).astype(bf16)


def weights_kernel(keep, got, x1, x2, x3, q0, q1, q2, q3, k0, k1, k2, k3, qo, ko, out, xr, gr):
    wide = HEADS * HEAD
    for d in range(N_OUT):
        rows = slice(d * ROWS, (d + 1) * ROWS)
        other = slice((N_OUT + d) * ROWS, (N_OUT + d + 1) * ROWS)
        if d == 0:
            xr[rows, :] = keep[0]
            xr[other, :] = got[0]
        else:
            x = (x1, x2, x3)[d - 1]
            xr[rows, :] = x[0]
            xr[other, :] = x[1]
        gr[rows, :wide] = (q0, q1, q2, q3)[d][...]
        gr[rows, wide:] = (k0, k1, k2, k3)[d][...]
        gr[other, :wide] = qo[d]
        gr[other, wide:] = ko[d]
    dw = dot(xr[...], gr[...], TN).astype(bf16)
    for p in range(16):
        out[p] = dw[p * 32 : (p + 1) * 32]


smem = pl.BlockSpec(memory_space=pltpu.SMEM)
vmem = pl.BlockSpec(memory_space=pltpu.VMEM)
params = pltpu.CompilerParams(vmem_limit_bytes=50 * 1024 * 1024)


def stats_call(ordk, posq, qs, gs, kva, kvb):
    return pl.pallas_call(
        stats_kernel,
        out_shape=jax.ShapeDtypeStruct((3, ALL_ROWS), f32),
        in_specs=[smem] + [vmem] * 11,
        out_specs=vmem,
        scratch_shapes=[pltpu.VMEM((ALL_ROWS, HEAD), bf16)] * 2,
        compiler_params=params,
        name="stats",
    )(ordk, posq, *qs, *gs, kva, kvb)


def grads_call(ordk, posq, stats, qs, gs, kva, kvb):
    wide = HEADS * HEAD
    return pl.pallas_call(
        grads_kernel,
        out_shape=(
            jax.ShapeDtypeStruct((ROWS, wide), f32),
            jax.ShapeDtypeStruct((ROWS, wide), bf16),
            jax.ShapeDtypeStruct((ROWS, wide), bf16),
            jax.ShapeDtypeStruct((ROWS, wide), bf16),
            jax.ShapeDtypeStruct((KHALF, 2 * HEAD), f32),
            jax.ShapeDtypeStruct((KHALF, 2 * HEAD), f32),
        ),
        in_specs=[smem] + [vmem] * 15,
        out_specs=[vmem] * 6,
        scratch_shapes=[
            pltpu.VMEM((ALL_ROWS, HEAD), bf16),
            pltpu.VMEM((ALL_ROWS, HEAD), bf16),
            pltpu.VMEM((ALL_ROWS, HEAD), f32),
            pltpu.VMEM((KEYS, HEAD), f32),
            pltpu.VMEM((KEYS, HEAD), f32),
            pltpu.VMEM((1, ALL_ROWS), f32),
            pltpu.VMEM((1, ALL_ROWS), f32),
        ],
        compiler_params=params,
        name="grads",
    )(ordk, posq, *stats, *qs, *gs, kva, kvb)


def columns_call(place, tokens):
    shape = jax.ShapeDtypeStruct((N_OUT, ROWS, 512), bf16)
    return pl.pallas_call(
        columns_kernel,
        out_shape=(shape, shape),
        in_specs=[smem, vmem],
        out_specs=[vmem] * 2,
        compiler_params=params,
        name="columns",
    )(place, tokens)


def weights_call(*args):
    return pl.pallas_call(
        weights_kernel,
        out_shape=jax.ShapeDtypeStruct((16, 32, 768), bf16),
        in_specs=[vmem] * len(args),
        out_specs=vmem,
        scratch_shapes=[
            pltpu.VMEM((2 * N_OUT * ROWS, 512), bf16),
            pltpu.VMEM((2 * N_OUT * ROWS, 768), bf16),
        ],
        compiler_params=params,
        name="weights",
    )(*args)


def shift(x, axis, d, n):
    return lax.ppermute(x, axis, [(i, (i + d) % n) for i in range(n)])


def from_behind(x, axis, n):
    return [x] + [shift(x, axis, d, n) for d in range(1, n)]


def per_device(inputs, block_order, w_query, w_key, w_value, grad_out):
    tokens = inputs[0]
    order = block_order[0]
    dout = grad_out[0]
    o, ix, iy, ic = (lax.axis_index(a) for a in ("outer", "x", "yh", "core"))

    kv = jnp.concatenate(
        [
            dot(tokens, w_key, NN).astype(bf16),
            dot(tokens, w_value, NN).astype(bf16),
        ],
        axis=1,
    )
    kv, later, dout = lax.optimization_barrier((kv, tokens, dout))
    pair = jnp.concatenate(from_behind(kv, "yh", 2), axis=0)
    query = dot(later, w_query, NN).astype(bf16)
    qs = from_behind(query, "outer", N_OUT)
    gs = from_behind(dout, "outer", N_OUT)
    keep, send = columns_call(jnp.stack([o, ic]), later)
    kva = jnp.concatenate(from_behind(pair, "x", N_X), axis=0)
    kvb = shift(kva, "core", 1, 2)
    got = shift(send, "core", 1, 2)

    inner = np.arange(2)[:, None, None, None], np.arange(N_X)[None, :, None, None], np.arange(2)[None, None, :, None]
    step = np.arange(2)[None, None, None, :]
    key_dev = ((o * N_X + (ix - inner[1]) % N_X) * 2 + (iy - inner[2]) % 2) * 2 + (ic - inner[0]) % 2
    key_blocks = (key_dev * 2 + step).reshape(-1)
    query_dev = (((o - np.arange(N_OUT)) % N_OUT * N_X + ix) * 2 + iy) * 2 + ic
    query_blocks = (query_dev[:, None] * 2 + np.arange(2)[None, :]).reshape(-1)

    def look_up(blocks):
        hit = blocks[:, None] == jnp.arange(order.shape[0], dtype=jnp.int32)[None, :]
        return jnp.sum(jnp.where(hit, order[None, :], 0), axis=1)

    ordk = look_up(key_blocks)
    ordq = look_up(query_blocks).reshape(N_OUT, 1, 2, 1)
    posq = ordq * HALF + jnp.arange(HALF, dtype=jnp.int32)
    posq = jnp.broadcast_to(posq, (N_OUT, HEADS, 2, HALF)).reshape(1, ALL_ROWS)

    keep, got, kva = lax.optimization_barrier((keep, got, kva))
    xs = [
        shift(jnp.stack([keep[d], got[d]]), "outer", d, N_OUT) for d in range(1, N_OUT)
    ]
    stats = stats_call(ordk, posq, qs, gs, kva, kvb)
    all_stats = from_behind(stats, "outer", N_OUT)
    all_stats, xs = lax.optimization_barrier((all_stats, xs))
    dq0, dq1, dq2, dq3, dkv_keep, dkv_send = grads_call(ordk, posq, all_stats, qs, gs, kva, kvb)

    dkv_got = shift(dkv_send, "core", 1, 2)
    dq = dq0
    for d, part in ((1, dq1), (2, dq2), (3, dq3)):
        dq = dq + shift(part, "outer", -d, N_OUT).astype(f32)
    dq_all = from_behind(dq.astype(bf16), "outer", N_OUT)

    dkv = (dkv_keep + dkv_got).reshape(N_X, 2 * ROWS, 2 * HEAD)
    low = dkv.astype(bf16)
    part = dkv[0]
    for d in range(1, N_X):
        part = part + shift(low[d], "x", -d, N_X).astype(f32)
    dkv = part[:ROWS] + shift(part[ROWS:].astype(bf16), "yh", 1, 2).astype(f32)
    dkv_all = from_behind(dkv.astype(bf16), "outer", N_OUT)

    dq_other = shift(jnp.stack(dq_all), "core", 1, 2)
    dkv_other = shift(jnp.stack(dkv_all), "core", 1, 2)
    dw = weights_call(keep, got, *xs, *dq_all, *dkv_all, dq_other, dkv_other)
    dw = lax.all_to_all(dw, ("dp", "x", "yh"), 0, 0, tiled=True)
    dw = jnp.sum(dw.astype(f32), axis=0)
    wide = HEADS * HEAD
    return dw[:, :wide], dw[:, wide : wide + HEAD], dw[:, wide + HEAD :]


def solution(mesh):
    devices = np.asarray(mesh.devices).reshape(2, N_OUT, N_X, 2, 2)
    fine = Mesh(devices, ("dp", "outer", "x", "yh", "core"))
    seq = ("outer", "x", "yh", "core")
    rows = P(("dp",) + seq, None)
    return jax.shard_map(
        per_device,
        mesh=fine,
        in_specs=(
            P("dp", seq, None),
            P("dp", None),
            P(None, None),
            P(None, None),
            P(None, None),
            P("dp", seq, None),
        ),
        out_specs=(rows, rows, rows),
        check_vma=False,
    )
```

```python
import functools
import math

import jax
import jax.numpy as jnp
import numpy as np
from jax import lax
from jax.experimental import pallas as pl
from jax.experimental.pallas import tpu as pltpu
from jax.sharding import Mesh, PartitionSpec as P

masked_fill = -1e30
HEADS = 4
HEAD = 128
ROWS = 160
HALF = 80
N_OUT = 4
N_X = 4
SLOT = HEADS * ROWS
ALL_ROWS = N_OUT * SLOT
KEYS = 16 * ROWS
KHALF = KEYS // 2
RT = 512
KC = 640
SCALE = 1.0 / math.sqrt(HEAD)
SCALE2 = SCALE * math.log2(math.e)
f32 = jnp.float32
bf16 = jnp.bfloat16
NT = (((1,), (1,)), ((), ()))
NN = (((1,), (0,)), ((), ()))
TN = (((0,), (0,)), ((), ()))


def dot(a, b, dims):
    return lax.dot_general(a, b, dims, preferred_element_type=f32)


def fill_rows(pieces, rows_ref):
    for d in range(N_OUT):
        for h in range(HEADS):
            rows_ref[d * SLOT + h * ROWS : d * SLOT + (h + 1) * ROWS, :] = pieces[d][
                :, h * HEAD : (h + 1) * HEAD
            ]


def masked_scores(key_rows, q, posq, ordk_ref, block):
    score = dot(key_rows, q, NT)
    place = lax.broadcasted_iota(jnp.int32, (HALF, RT), 0)
    parts = []
    for b in range(score.shape[0] // HALF):
        limit = posq - ordk_ref[block + b] * HALF
        part = score[b * HALF : (b + 1) * HALF] * SCALE2
        parts.append(jnp.where(place <= limit, part, masked_fill))
    return jnp.concatenate(parts, axis=0)


def stats_kernel(ordk_ref, posq_ref, q0, q1, q2, q3, g0, g1, g2, g3, kva, kvb, out_ref, qr, gr):
    fill_rows((q0, q1, q2, q3), qr)
    fill_rows((g0, g1, g2, g3), gr)

    def row_tile(rt, _):
        r0 = pl.multiple_of(rt * RT, RT)
        q = qr[pl.ds(r0, RT), :]
        g = gr[pl.ds(r0, RT), :]
        posq = posq_ref[:, pl.ds(r0, RT)]
        top = jnp.full((8, RT), masked_fill, f32)
        total = jnp.zeros((8, RT), f32)
        weighted = jnp.zeros((8, RT), f32)
        for chunk in range(KEYS // KC):
            kv = kva if chunk * KC < KHALF else kvb
            k0 = chunk * KC % KHALF
            score = masked_scores(kv[k0 : k0 + KC, :HEAD], q, posq, ordk_ref, chunk * (KC // HALF))
            dprob = dot(kv[k0 : k0 + KC, HEAD:], g, NT)
            score = score.reshape(KC // 8, 8, RT)
            new_top = jnp.maximum(top, jnp.max(score, axis=0))
            weights = jnp.exp2(score - new_top[None])
            factor = jnp.exp2(top - new_top)
            total = total * factor + jnp.sum(weights, axis=0)
            weighted = weighted * factor + jnp.sum(weights * dprob.reshape(KC // 8, 8, RT), axis=0)
            top = new_top
        row_top = jnp.max(top, axis=0, keepdims=True)
        factor = jnp.exp2(top - row_top)
        out_ref[0:1, pl.ds(r0, RT)] = row_top
        out_ref[1:2, pl.ds(r0, RT)] = jnp.sum(total * factor, axis=0, keepdims=True)
        out_ref[2:3, pl.ds(r0, RT)] = jnp.sum(weighted * factor, axis=0, keepdims=True)
        return 0

    lax.fori_loop(0, ALL_ROWS // RT, row_tile, 0)


def combine_stats(stats, rowstat_ref):
    for d in range(N_OUT):
        parts = []
        for e in range(N_OUT):
            c0 = (d - e) % N_OUT * SLOT
            parts.append(stats[e][:, c0 : c0 + SLOT])
        row_top = parts[0][0:1]
        for part in parts[1:]:
            row_top = jnp.maximum(row_top, part[0:1])
        total = jnp.zeros_like(row_top)
        weighted = jnp.zeros_like(row_top)
        for part in parts:
            factor = jnp.exp2(part[0:1] - row_top)
            total = total + part[1:2] * factor
            weighted = weighted + part[2:3] * factor
        rowstat_ref[0:1, d * SLOT : (d + 1) * SLOT] = row_top + jnp.log2(total)
        rowstat_ref[1:2, d * SLOT : (d + 1) * SLOT] = weighted / total


def grads_pass(segments, ordk_ref, posq_ref, rowstat_ref, kvs, dq_in, dq_out, dkvs, qr, gr):
    for out in dkvs:
        out[...] = jnp.zeros_like(out)

    def row_tile(rt, _):
        r0 = pl.multiple_of(rt * RT, RT)
        q = qr[pl.ds(r0, RT), :]
        g = gr[pl.ds(r0, RT), :]
        posq = posq_ref[:, pl.ds(r0, RT)]
        lse = rowstat_ref[0:1, pl.ds(r0, RT)]
        delta = rowstat_ref[1:2, pl.ds(r0, RT)]
        dq = jnp.zeros((RT, HEAD), f32) if dq_in is None else dq_in[pl.ds(r0, RT), :]
        for which, k0, size, block, to, t0 in segments:
            kv = kvs[which]
            key_rows = kv[k0 : k0 + size, :HEAD]
            score = masked_scores(key_rows, q, posq, ordk_ref, block)
            prob = jnp.exp2(score - lse)
            dprob = dot(kv[k0 : k0 + size, HEAD:], g, NT)
            dscore = (prob * (dprob - delta)).astype(bf16)
            prob_low = prob.astype(bf16)
            dkvs[to][t0 : t0 + size, HEAD:] += dot(prob_low, g, NN)
            dkvs[to][t0 : t0 + size, :HEAD] += dot(dscore, q, NN)
            dq = dq + dot(dscore, key_rows, TN)
        dq_out[pl.ds(r0, RT), :] = dq
        return 0

    lax.fori_loop(0, ALL_ROWS // RT, row_tile, 0)
    for out in dkvs:
        out[:, :HEAD] = out[:, :HEAD] * SCALE


HOME = 2 * ROWS
AWAY = KHALF - HOME


def away_segments(half):
    size = AWAY // 2
    first = half * (KHALF // HALF)
    return [
        (0, HOME + j * size, size, first + (HOME + j * size) // HALF, 0, j * size) for j in range(2)
    ]


def grads_first(ordk, posq, s0, s1, s2, s3, q0, q1, q2, q3, g0, g1, g2, g3, kvb, rowstat, dq, send, qr, gr):
    fill_rows((q0, q1, q2, q3), qr)
    fill_rows((g0, g1, g2, g3), gr)
    combine_stats((s0, s1, s2, s3), rowstat)
    grads_pass(away_segments(1), ordk, posq, rowstat, (kvb,), None, dq, (send,), qr, gr)


def grads_second(ordk, posq, rowstat, q0, q1, q2, q3, g0, g1, g2, g3, kva, dq_in, dq, keep, qr, gr):
    fill_rows((q0, q1, q2, q3), qr)
    fill_rows((g0, g1, g2, g3), gr)
    grads_pass(away_segments(0), ordk, posq, rowstat, (kva,), dq_in, dq, (keep,), qr, gr)


def grads_third(
    ordk, posq, rowstat, q0, q1, q2, q3, g0, g1, g2, g3, kva, kvb, dq_in,
    dq0, dq1, dq2, dq3, keep, send, qr, gr, dqr,
):
    fill_rows((q0, q1, q2, q3), qr)
    fill_rows((g0, g1, g2, g3), gr)
    segments = [(0, 0, HOME, 0, 0, 0), (1, 0, HOME, KHALF // HALF, 1, 0)]
    grads_pass(segments, ordk, posq, rowstat, (kva, kvb), dq_in, dqr, (keep, send), qr, gr)
    for d, out in enumerate((dq0, dq1, dq2, dq3)):
        for h in range(HEADS):
            rows = dqr[d * SLOT + h * ROWS : d * SLOT + (h + 1) * ROWS, :] * SCALE
            out[:, h * HEAD : (h + 1) * HEAD] = rows.astype(out.dtype)


def columns_kernel(place_ref, own, other, out):
    ic = place_ref[1]
    src = lax.broadcasted_iota(jnp.int32, (512, 256), 0)
    dst = lax.broadcasted_iota(jnp.int32, (512, 256), 1)
    home = dst // 32 * 64 + dst % 32 + ic * 32
    pick = jnp.where(src == home, 1.0, 0.0).astype(bf16)
    for t, tok in enumerate((own, other)):
        for o in range(N_OUT):
            for p in range(2):
                start = p * 2048 + o * 512
                cols = tok[:, start : start + 512]
                out[o, t, :, p * 256 : (p + 1) * 256] = dot(cols, pick, NN).astype(bf16)


def weights_kernel(place_ref, x, q0, q1, q2, q3, k0, k1, k2, k3, qo, ko, out, xr, gr):
    wide = HEADS * HEAD
    for d in range(N_OUT):
        rows = slice(d * ROWS, (d + 1) * ROWS)
        other = slice((N_OUT + d) * ROWS, (N_OUT + d + 1) * ROWS)
        source = lax.rem(place_ref[0] + N_OUT - d, N_OUT)
        xr[rows, :] = x[source, 0]
        xr[other, :] = x[source, 1]
        gr[rows, :wide] = (q0, q1, q2, q3)[d][...]
        gr[rows, wide:] = (k0, k1, k2, k3)[d][...]
        gr[other, :wide] = qo[d]
        gr[other, wide:] = ko[d]
    dw = dot(xr[...], gr[...], TN).astype(bf16)
    for p in range(16):
        out[p] = dw[p * 32 : (p + 1) * 32]


smem = pl.BlockSpec(memory_space=pltpu.SMEM)
vmem = pl.BlockSpec(memory_space=pltpu.VMEM)
params = pltpu.CompilerParams(vmem_limit_bytes=50 * 1024 * 1024)


def cost(pairs, matmuls, size):
    return pl.CostEstimate(
        flops=2 * pairs * HEAD * matmuls, transcendentals=pairs, bytes_accessed=size
    )


def kernel_call(body, name, outs, scratch, estimate, aliases, scalars, *args):
    return pl.pallas_call(
        body,
        out_shape=tuple(jax.ShapeDtypeStruct(*o) for o in outs),
        in_specs=[smem] * scalars + [vmem] * (len(args) - scalars),
        out_specs=tuple(vmem for _ in outs),
        scratch_shapes=[pltpu.VMEM(*s) for s in scratch],
        compiler_params=params,
        cost_estimate=estimate,
        input_output_aliases=aliases,
        name=name,
    )(*args)


WIDE = HEADS * HEAD
row_scratch = [((ALL_ROWS, HEAD), bf16)] * 2
acc_rows = ((ALL_ROWS, HEAD), f32)


def shift(x, axis, d, n):
    return lax.ppermute(x, axis, [(i, (i + d) % n) for i in range(n)])


def from_behind(x, axis, n):
    return [x] + [shift(x, axis, d, n) for d in range(1, n)]


def both_ways(x, axis, way):
    behind = shift(x, axis, 1, 4)
    ahead = shift(x, axis, -1, 4)
    far = shift(behind if way == 1 else ahead, axis, way, 4)
    return [x, behind, far, ahead]


def per_device(inputs, block_order, w_query, w_key, w_value, grad_out):
    tokens = inputs[0]
    order = block_order[0]
    dout = grad_out[0]
    o, ix, iy, ic = (lax.axis_index(a) for a in ("outer", "x", "yh", "core"))

    kv = jnp.concatenate(
        [
            dot(tokens, w_key, NN).astype(bf16),
            dot(tokens, w_value, NN).astype(bf16),
        ],
        axis=1,
    )
    kv, later, dout = lax.optimization_barrier((kv, tokens, dout))
    pair = shift(kv, "yh", 1, 2)
    own_x = both_ways(kv, "x", 1)
    pair_x = both_ways(pair, "x", -1)
    query = dot(later, w_query, NN).astype(bf16)
    qs = both_ways(query, "outer", 1)
    gs = both_ways(dout, "outer", -1)
    kva = jnp.concatenate([part for d in range(N_X) for part in (own_x[d], pair_x[d])], axis=0)
    kvb = shift(kva, "core", 1, 2)

    inner = np.arange(2)[:, None, None, None], np.arange(N_X)[None, :, None, None], np.arange(2)[None, None, :, None]
    step = np.arange(2)[None, None, None, :]
    key_dev = ((o * N_X + (ix - inner[1]) % N_X) * 2 + (iy - inner[2]) % 2) * 2 + (ic - inner[0]) % 2
    key_blocks = (key_dev * 2 + step).reshape(-1)
    query_dev = (((o - np.arange(N_OUT)) % N_OUT * N_X + ix) * 2 + iy) * 2 + ic
    query_blocks = (query_dev[:, None] * 2 + np.arange(2)[None, :]).reshape(-1)

    def look_up(blocks):
        hit = blocks[:, None] == jnp.arange(order.shape[0], dtype=jnp.int32)[None, :]
        return jnp.sum(jnp.where(hit, order[None, :], 0), axis=1)

    ordk = look_up(key_blocks)
    ordq = look_up(query_blocks).reshape(N_OUT, 1, 2, 1)
    posq = ordq * HALF + jnp.arange(HALF, dtype=jnp.int32)
    posq = jnp.broadcast_to(posq, (N_OUT, HEADS, 2, HALF)).reshape(1, ALL_ROWS)

    place = jnp.stack([o, ic])
    later, kva = lax.optimization_barrier((later, kva))
    other_tokens = shift(later, "core", 1, 2)
    (stats,) = kernel_call(
        stats_kernel, "stats", [((3, ALL_ROWS), f32)], row_scratch,
        cost(ALL_ROWS * KEYS, 2, 4 << 20), {}, 1, ordk, posq, *qs, *gs, kva, kvb,
    )
    all_stats = from_behind(stats, "outer", N_OUT)
    later, other_tokens, stats = lax.optimization_barrier((later, other_tokens, stats))
    (columns,) = kernel_call(
        columns_kernel, "columns", [((N_OUT, 2, ROWS, 512), bf16)], [],
        cost(ROWS * 4096, 4, 5 << 20), {}, 1, place, later, other_tokens,
    )
    columns = lax.all_to_all(columns, "outer", 0, 0, tiled=True)

    rowstat, dq, send = kernel_call(
        grads_first, "grads_first",
        [((2, ALL_ROWS), f32), acc_rows, ((AWAY, 2 * HEAD), f32)], row_scratch,
        cost(ALL_ROWS * AWAY, 5, 8 << 20), {}, 1, ordk, posq, *all_stats, *qs, *gs, kvb,
    )
    got = shift(send, "core", 1, 2)
    dq, keep = kernel_call(
        grads_second, "grads_second", [acc_rows, ((AWAY, 2 * HEAD), f32)], row_scratch,
        cost(ALL_ROWS * AWAY, 5, 8 << 20), {12: 0}, 1, ordk, posq, rowstat, *qs, *gs, kva, dq,
    )
    away = (keep + got).astype(bf16).reshape(N_X - 1, HOME, 2 * HEAD)
    away, dq = lax.optimization_barrier((away, dq))
    away = [shift(away[d - 1], "x", -d, N_X) for d in range(1, N_X)]
    dq0, dq1, dq2, dq3, keep, send = kernel_call(
        grads_third, "grads_third",
        [((ROWS, WIDE), f32)] + [((ROWS, WIDE), bf16)] * 3 + [((HOME, 2 * HEAD), f32)] * 2,
        row_scratch + [acc_rows],
        cost(ALL_ROWS * 2 * HOME, 5, 8 << 20), {}, 1, ordk, posq, rowstat, *qs, *gs, kva, kvb, dq,
    )
    got = shift(send, "core", 1, 2)
    dq1, dq2, dq3, columns = lax.optimization_barrier((dq1, dq2, dq3, columns))
    dq = dq0
    for d, part in ((1, dq1), (2, dq2), (3, dq3)):
        dq = dq + shift(part, "outer", -d, N_OUT).astype(f32)
    dq_all = from_behind(dq.astype(bf16), "outer", N_OUT)

    part = keep + got
    for arrived in away:
        part = part + arrived.astype(f32)
    dkv = part[:ROWS] + shift(part[ROWS:].astype(bf16), "yh", 1, 2).astype(f32)
    dkv_all = both_ways(dkv.astype(bf16), "outer", 1)

    dq_other = shift(jnp.stack(dq_all), "core", 1, 2)
    dkv_other = shift(jnp.stack(dkv_all), "core", 1, 2)
    (dw,) = kernel_call(
        weights_kernel, "weights", [((16, 32, 768), bf16)],
        [((2 * N_OUT * ROWS, 512), bf16), ((2 * N_OUT * ROWS, 768), bf16)],
        cost(1280 * 512, 6, 4 << 20), {}, 1,
        place, columns, *dq_all, *dkv_all, dq_other, dkv_other,
    )
    dw = lax.all_to_all(dw, ("dp", "x", "yh"), 0, 0, tiled=True)
    dw = jnp.sum(dw.astype(f32), axis=0)
    wide = HEADS * HEAD
    return dw[:, :wide], dw[:, wide : wide + HEAD], dw[:, wide + HEAD :]


def solution(mesh):
    devices = np.asarray(mesh.devices).reshape(2, N_OUT, N_X, 2, 2)
    fine = Mesh(devices, ("dp", "outer", "x", "yh", "core"))
    seq = ("outer", "x", "yh", "core")
    rows = P(("dp",) + seq, None)
    return jax.shard_map(
        per_device,
        mesh=fine,
        in_specs=(
            P("dp", seq, None),
            P("dp", None),
            P(None, None),
            P(None, None),
            P(None, None),
            P("dp", seq, None),
        ),
        out_specs=(rows, rows, rows),
        check_vma=False,
    )
```

```python
import functools
import math

import jax
import jax.numpy as jnp
import numpy as np
from jax import lax
from jax.experimental import pallas as pl
from jax.experimental.pallas import tpu as pltpu
from jax.sharding import Mesh, PartitionSpec as P

masked_fill = -1e30
HEADS = 4
HEAD = 128
ROWS = 160
HALF = 80
N_OUT = 4
N_X = 4
SLOT = HEADS * ROWS
ALL_ROWS = N_OUT * SLOT
KEYS = 16 * ROWS
KHALF = KEYS // 2
RT = 512
KC = 640
SCALE = 1.0 / math.sqrt(HEAD)
SCALE2 = SCALE * math.log2(math.e)
f32 = jnp.float32
bf16 = jnp.bfloat16
NT = (((1,), (1,)), ((), ()))
NN = (((1,), (0,)), ((), ()))
TN = (((0,), (0,)), ((), ()))


def dot(a, b, dims):
    return lax.dot_general(a, b, dims, preferred_element_type=f32)


def slot_start(d):
    return (d - 1) % N_OUT * SLOT


def fill_rows(pieces, q_ref, g_ref):
    for d in range(N_OUT):
        for h in range(HEADS):
            r0 = slot_start(d) + h * ROWS
            q_ref[r0 : r0 + ROWS, :] = pieces[d][:, h * HEAD : (h + 1) * HEAD]
            g_ref[r0 : r0 + ROWS, :] = pieces[d][:, (HEADS + h) * HEAD : (HEADS + h + 1) * HEAD]


def masked_scores(key_rows, q, posq, ordk_ref, block):
    score = dot(key_rows, q, NT)
    place = lax.broadcasted_iota(jnp.int32, (HALF, RT), 0)
    parts = []
    for b in range(score.shape[0] // HALF):
        limit = posq - ordk_ref[block + b] * HALF
        part = score[b * HALF : (b + 1) * HALF] * SCALE2
        parts.append(jnp.where(place <= limit, part, masked_fill))
    return jnp.concatenate(parts, axis=0)


def stats_kernel(ordk_ref, posq_ref, p0, p1, p2, p3, kva, kvb, out_ref, qr, gr):
    fill_rows((p0, p1, p2, p3), qr, gr)

    def row_tile(rt, _):
        r0 = pl.multiple_of(rt * RT, RT)
        q = qr[pl.ds(r0, RT), :]
        g = gr[pl.ds(r0, RT), :]
        posq = posq_ref[:, pl.ds(r0, RT)]
        top = jnp.full((8, RT), masked_fill, f32)
        total = jnp.zeros((8, RT), f32)
        weighted = jnp.zeros((8, RT), f32)
        for chunk in range(KEYS // KC):
            kv = kva if chunk * KC < KHALF else kvb
            k0 = chunk * KC % KHALF
            score = masked_scores(kv[k0 : k0 + KC, :HEAD], q, posq, ordk_ref, chunk * (KC // HALF))
            dprob = dot(kv[k0 : k0 + KC, HEAD:], g, NT)
            score = score.reshape(KC // 8, 8, RT)
            new_top = jnp.maximum(top, jnp.max(score, axis=0))
            weights = jnp.exp2(score - new_top[None])
            factor = jnp.exp2(top - new_top)
            total = total * factor + jnp.sum(weights, axis=0)
            weighted = weighted * factor + jnp.sum(weights * dprob.reshape(KC // 8, 8, RT), axis=0)
            top = new_top
        row_top = jnp.max(top, axis=0, keepdims=True)
        factor = jnp.exp2(top - row_top)
        out_ref[0:1, pl.ds(r0, RT)] = row_top
        out_ref[1:2, pl.ds(r0, RT)] = jnp.sum(total * factor, axis=0, keepdims=True)
        out_ref[2:3, pl.ds(r0, RT)] = jnp.sum(weighted * factor, axis=0, keepdims=True)
        return 0

    lax.fori_loop(0, ALL_ROWS // RT, row_tile, 0)


def combine_stats(stats, rowstat_ref):
    for d in range(N_OUT):
        parts = []
        for e in range(N_OUT):
            c0 = slot_start(d - e)
            parts.append(stats[e][:, c0 : c0 + SLOT])
        row_top = parts[0][0:1]
        for part in parts[1:]:
            row_top = jnp.maximum(row_top, part[0:1])
        total = jnp.zeros_like(row_top)
        weighted = jnp.zeros_like(row_top)
        for part in parts:
            factor = jnp.exp2(part[0:1] - row_top)
            total = total + part[1:2] * factor
            weighted = weighted + part[2:3] * factor
        r0 = slot_start(d)
        rowstat_ref[0:1, r0 : r0 + SLOT] = row_top + jnp.log2(total)
        rowstat_ref[1:2, r0 : r0 + SLOT] = weighted / total


def grads_pass(block, ordk_ref, posq_ref, rowstat_ref, kv, dq_in, dqr, dkv, qr, gr):
    dkv[...] = jnp.zeros_like(dkv)

    def row_tile(rt, _):
        r0 = pl.multiple_of(rt * RT, RT)
        q = qr[pl.ds(r0, RT), :]
        g = gr[pl.ds(r0, RT), :]
        posq = posq_ref[:, pl.ds(r0, RT)]
        lse = rowstat_ref[0:1, pl.ds(r0, RT)]
        delta = rowstat_ref[1:2, pl.ds(r0, RT)]
        dq = jnp.zeros((RT, HEAD), f32) if dq_in is None else dq_in[pl.ds(r0, RT), :]
        for k0 in range(0, KHALF, KC):
            key_rows = kv[k0 : k0 + KC, :HEAD]
            score = masked_scores(key_rows, q, posq, ordk_ref, block + k0 // HALF)
            prob = jnp.exp2(score - lse)
            dprob = dot(kv[k0 : k0 + KC, HEAD:], g, NT)
            dscore = (prob * (dprob - delta)).astype(bf16)
            prob_low = prob.astype(bf16)
            dkv[k0 : k0 + KC, HEAD:] += dot(prob_low, g, NN)
            dkv[k0 : k0 + KC, :HEAD] += dot(dscore, q, NN)
            dq = dq + dot(dscore, key_rows, TN)
        dqr[pl.ds(r0, RT), :] = dq
        return 0

    lax.fori_loop(0, ALL_ROWS // RT, row_tile, 0)
    dkv[:, :HEAD] = dkv[:, :HEAD] * SCALE


def grads_first(ordk, posq, s0, s1, s2, s3, p0, p1, p2, p3, kvb, rowstat, dq, dkvb, qr, gr):
    fill_rows((p0, p1, p2, p3), qr, gr)
    combine_stats((s0, s1, s2, s3), rowstat)
    grads_pass(KHALF // HALF, ordk, posq, rowstat, kvb, None, dq, dkvb, qr, gr)


def grads_second(
    ordk, posq, rowstat, p0, p1, p2, p3, kva, dq_in, dq0, dq1, dq2, dq3, dkva, qr, gr, dqr
):
    fill_rows((p0, p1, p2, p3), qr, gr)
    grads_pass(0, ordk, posq, rowstat, kva, dq_in, dqr, dkva, qr, gr)
    for d, out in enumerate((dq0, dq1, dq2, dq3)):
        for h in range(HEADS):
            r0 = slot_start(d) + h * ROWS
            out[:, h * HEAD : (h + 1) * HEAD] = (dqr[r0 : r0 + ROWS, :] * SCALE).astype(out.dtype)


def columns_kernel(place_ref, own, other, x0, x1, x2, x3):
    ic = place_ref[1]
    src = lax.broadcasted_iota(jnp.int32, (512, 256), 0)
    dst = lax.broadcasted_iota(jnp.int32, (512, 256), 1)
    home = dst // 32 * 64 + dst % 32 + ic * 32
    pick = jnp.where(src == home, 1.0, 0.0).astype(bf16)
    for d, out in enumerate((x0, x1, x2, x3)):
        base = lax.rem(place_ref[0] + d, N_OUT) * 512
        for t, tok in enumerate((own, other)):
            for p in range(2):
                cols = tok[:, pl.ds(pl.multiple_of(base + p * 2048, 512), 512)]
                out[t, :, p * 256 : (p + 1) * 256] = dot(cols, pick, NN).astype(bf16)


def weights_kernel(x0, x1, x2, x3, q0, q1, q2, q3, k0, k1, k2, k3, qo, ko, out, xr, gr):
    wide = HEADS * HEAD
    for d, x in enumerate((x0, x1, x2, x3)):
        rows = slice(d * ROWS, (d + 1) * ROWS)
        other = slice((N_OUT + d) * ROWS, (N_OUT + d + 1) * ROWS)
        xr[rows, :] = x[0]
        xr[other, :] = x[1]
        gr[rows, :wide] = (q0, q1, q2, q3)[d][...]
        gr[rows, wide:] = (k0, k1, k2, k3)[d][...]
        gr[other, :wide] = qo[d]
        gr[other, wide:] = ko[d]
    dw = dot(xr[...], gr[...], TN).astype(bf16)
    for p in range(16):
        out[p] = dw[p * 32 : (p + 1) * 32]


smem = pl.BlockSpec(memory_space=pltpu.SMEM)
vmem = pl.BlockSpec(memory_space=pltpu.VMEM)
params = pltpu.CompilerParams(vmem_limit_bytes=50 * 1024 * 1024)


def cost(pairs, matmuls, size):
    return pl.CostEstimate(
        flops=2 * pairs * HEAD * matmuls, transcendentals=pairs, bytes_accessed=size
    )


def kernel_call(body, name, outs, scratch, estimate, aliases, scalars, *args):
    return pl.pallas_call(
        body,
        out_shape=tuple(jax.ShapeDtypeStruct(*o) for o in outs),
        in_specs=[smem] * scalars + [vmem] * (len(args) - scalars),
        out_specs=tuple(vmem for _ in outs),
        scratch_shapes=[pltpu.VMEM(*s) for s in scratch],
        compiler_params=params,
        cost_estimate=estimate,
        input_output_aliases=aliases,
        name=name,
    )(*args)


WIDE = HEADS * HEAD
row_scratch = [((ALL_ROWS, HEAD), bf16)] * 2
acc_rows = ((ALL_ROWS, HEAD), f32)


def shift(x, axis, d, n):
    return lax.ppermute(x, axis, [(i, (i + d) % n) for i in range(n)])


def from_behind(x, axis, n):
    return [x] + [shift(x, axis, d, n) for d in range(1, n)]


def per_device(inputs, block_order, w_query, w_key, w_value, grad_out):
    tokens = inputs[0]
    order = block_order[0]
    dout = grad_out[0]
    o, ix, iy, ic = (lax.axis_index(a) for a in ("outer", "x", "yh", "core"))

    query = dot(tokens, w_query, NN).astype(bf16)
    ps = from_behind(jnp.concatenate([query, dout], axis=1), "outer", N_OUT)
    kv = jnp.concatenate(
        [
            dot(tokens, w_key, NN).astype(bf16),
            dot(tokens, w_value, NN).astype(bf16),
        ],
        axis=1,
    )
    kva = jnp.broadcast_to(kv[None], (8,) + kv.shape)
    kva = lax.all_to_all(kva, ("x", "yh"), 0, 0, tiled=True).reshape(KHALF, 2 * HEAD)
    kvb = shift(kva, "core", 1, 2)

    key_dev = (o * 8 + np.arange(8)[None, :, None]) * 2 + (ic + np.arange(2)[:, None, None]) % 2
    key_blocks = (key_dev * 2 + np.arange(2)[None, None, :]).reshape(-1)
    query_dev = (((o - np.array([1, 2, 3, 0])) % N_OUT * N_X + ix) * 2 + iy) * 2 + ic
    query_blocks = (query_dev[:, None] * 2 + np.arange(2)[None, :]).reshape(-1)

    def look_up(blocks):
        hit = blocks[:, None] == jnp.arange(order.shape[0], dtype=jnp.int32)[None, :]
        return jnp.sum(jnp.where(hit, order[None, :], 0), axis=1)

    ordk = look_up(key_blocks)
    ordq = look_up(query_blocks).reshape(N_OUT, 1, 2, 1)
    posq = ordq * HALF + jnp.arange(HALF, dtype=jnp.int32)
    posq = jnp.broadcast_to(posq, (N_OUT, HEADS, 2, HALF)).reshape(1, ALL_ROWS)

    place = jnp.stack([o, ic])
    later, kv = lax.optimization_barrier((tokens, kv))
    other_tokens = shift(later, "core", 1, 2)
    xs = kernel_call(
        columns_kernel, "columns", [((2, ROWS, 512), bf16)] * N_OUT, [],
        cost(ROWS * 4096, 4, 5 << 20), {}, 1, place, later, other_tokens,
    )
    xs, ps, kva = lax.optimization_barrier((xs, ps, kva))
    xs = [xs[0]] + [shift(xs[d], "outer", d, N_OUT) for d in range(1, N_OUT)]
    (stats,) = kernel_call(
        stats_kernel, "stats", [((3, ALL_ROWS), f32)], row_scratch,
        cost(ALL_ROWS * KEYS, 2, 4 << 20), {}, 1, ordk, posq, *ps, kva, kvb,
    )
    all_stats = from_behind(stats, "outer", N_OUT)
    all_stats, xs = lax.optimization_barrier((all_stats, xs))

    half = ((KHALF, 2 * HEAD), f32)
    rowstat, dq, dkvb = kernel_call(
        grads_first, "grads_first", [((2, ALL_ROWS), f32), acc_rows, half], row_scratch,
        cost(ALL_ROWS * KHALF, 5, 8 << 20), {}, 1, ordk, posq, *all_stats, *ps, kvb,
    )
    got = shift(dkvb, "core", 1, 2)
    dq0, dq1, dq2, dq3, dkva = kernel_call(
        grads_second, "grads_second",
        [((ROWS, WIDE), f32)] + [((ROWS, WIDE), bf16)] * 3 + [half], row_scratch + [acc_rows],
        cost(ALL_ROWS * KHALF, 5, 8 << 20), {}, 1, ordk, posq, rowstat, *ps, kva, dq,
    )
    dq1, dq2, dq3, got = lax.optimization_barrier((dq1, dq2, dq3, got))
    dq_parts = [shift(part, "outer", -d, N_OUT) for d, part in ((1, dq1), (2, dq2), (3, dq3))]
    dq = dq0
    dkv = (dkva + got).astype(bf16).reshape(8, ROWS, 2 * HEAD)
    dkv = lax.all_to_all(dkv, ("x", "yh"), 0, 0, tiled=True)
    dkv = jnp.sum(dkv.astype(f32), axis=0)
    dkv_all = from_behind(dkv.astype(bf16), "outer", N_OUT)
    for part in dq_parts:
        dq = dq + part.astype(f32)
    dq_all = from_behind(dq.astype(bf16), "outer", N_OUT)

    dq_other = shift(jnp.stack(dq_all), "core", 1, 2)
    dkv_other = shift(jnp.stack(dkv_all), "core", 1, 2)
    (dw,) = kernel_call(
        weights_kernel, "weights", [((16, 32, 768), bf16)],
        [((2 * N_OUT * ROWS, 512), bf16), ((2 * N_OUT * ROWS, 768), bf16)],
        cost(1280 * 512, 6, 4 << 20), {}, 0,
        *xs, *dq_all, *dkv_all, dq_other, dkv_other,
    )
    dw = lax.all_to_all(dw, ("dp", "x", "yh"), 0, 0, tiled=True)
    dw = jnp.sum(dw.astype(f32), axis=0)
    wide = HEADS * HEAD
    return dw[:, :wide], dw[:, wide : wide + HEAD], dw[:, wide + HEAD :]


def solution(mesh):
    devices = np.asarray(mesh.devices).reshape(2, N_OUT, N_X, 2, 2)
    fine = Mesh(devices, ("dp", "outer", "x", "yh", "core"))
    seq = ("outer", "x", "yh", "core")
    rows = P(("dp",) + seq, None)
    return jax.shard_map(
        per_device,
        mesh=fine,
        in_specs=(
            P("dp", seq, None),
            P("dp", None),
            P(None, None),
            P(None, None),
            P(None, None),
            P("dp", seq, None),
        ),
        out_specs=(rows, rows, rows),
        check_vma=False,
    )
```

```python
import functools
import math

import jax
import jax.numpy as jnp
import numpy as np
from jax import lax
from jax.experimental import pallas as pl
from jax.experimental.pallas import tpu as pltpu
from jax.sharding import Mesh, PartitionSpec as P

masked_fill = -1e30
HEADS = 4
HEAD = 128
ROWS = 160
HALF = 80
N_OUT = 4
N_X = 4
SLOT = HEADS * ROWS
ALL_ROWS = N_OUT * SLOT
KEYS = 16 * ROWS
KHALF = KEYS // 2
RT = 1280
KC = 640
KS = 160
SCALE = 1.0 / math.sqrt(HEAD)
SCALE2 = SCALE * math.log2(math.e)
f32 = jnp.float32
bf16 = jnp.bfloat16
NT = (((1,), (1,)), ((), ()))
NN = (((1,), (0,)), ((), ()))
TN = (((0,), (0,)), ((), ()))


def dot(a, b, dims):
    return lax.dot_general(a, b, dims, preferred_element_type=f32)


def slot_start(d):
    return (d - 1) % N_OUT * SLOT


def fill_rows(pieces, q_ref, g_ref):
    for d in range(N_OUT):
        for h in range(HEADS):
            r0 = slot_start(d) + h * ROWS
            q_ref[r0 : r0 + ROWS, :] = pieces[d][:, h * HEAD : (h + 1) * HEAD]
            g_ref[r0 : r0 + ROWS, :] = pieces[d][:, (HEADS + h) * HEAD : (HEADS + h + 1) * HEAD]


def masked_scores(key_rows, q, posq, ordk_ref, block):
    score = dot(key_rows, q, NT)
    place = lax.broadcasted_iota(jnp.int32, (HALF, RT), 0)
    parts = []
    for b in range(score.shape[0] // HALF):
        limit = posq - ordk_ref[block + b] * HALF
        part = score[b * HALF : (b + 1) * HALF] * SCALE2
        parts.append(jnp.where(place <= limit, part, masked_fill))
    return jnp.concatenate(parts, axis=0)


def stats_kernel(ordk_ref, posq_ref, p0, p1, p2, p3, kva, kvb, out_ref, qr, gr):
    fill_rows((p0, p1, p2, p3), qr, gr)

    def row_tile(rt, _):
        r0 = pl.multiple_of(rt * RT, RT)
        q = qr[pl.ds(r0, RT), :]
        g = gr[pl.ds(r0, RT), :]
        posq = posq_ref[:, pl.ds(r0, RT)]
        top = jnp.full((8, RT), masked_fill, f32)
        total = jnp.zeros((8, RT), f32)
        weighted = jnp.zeros((8, RT), f32)
        for chunk in range(KEYS // KS):
            kv = kva if chunk * KS < KHALF else kvb
            k0 = chunk * KS % KHALF
            score = masked_scores(kv[k0 : k0 + KS, :HEAD], q, posq, ordk_ref, chunk * (KS // HALF))
            dprob = dot(kv[k0 : k0 + KS, HEAD:], g, NT)
            score = score.reshape(KS // 8, 8, RT)
            new_top = jnp.maximum(top, jnp.max(score, axis=0))
            weights = jnp.exp2(score - new_top[None])
            factor = jnp.exp2(top - new_top)
            total = total * factor + jnp.sum(weights, axis=0)
            weighted = weighted * factor + jnp.sum(weights * dprob.reshape(KS // 8, 8, RT), axis=0)
            top = new_top
        row_top = jnp.max(top, axis=0, keepdims=True)
        factor = jnp.exp2(top - row_top)
        out_ref[0:1, pl.ds(r0, RT)] = row_top
        out_ref[1:2, pl.ds(r0, RT)] = jnp.sum(total * factor, axis=0, keepdims=True)
        out_ref[2:3, pl.ds(r0, RT)] = jnp.sum(weighted * factor, axis=0, keepdims=True)
        return 0

    lax.fori_loop(0, ALL_ROWS // RT, row_tile, 0)


def combine_stats(stats, rowstat_ref):
    for d in range(N_OUT):
        parts = []
        for e in range(N_OUT):
            c0 = slot_start(d - e)
            parts.append(stats[e][:, c0 : c0 + SLOT])
        row_top = parts[0][0:1]
        for part in parts[1:]:
            row_top = jnp.maximum(row_top, part[0:1])
        total = jnp.zeros_like(row_top)
        weighted = jnp.zeros_like(row_top)
        for part in parts:
            factor = jnp.exp2(part[0:1] - row_top)
            total = total + part[1:2] * factor
            weighted = weighted + part[2:3] * factor
        r0 = slot_start(d)
        rowstat_ref[0:1, r0 : r0 + SLOT] = row_top + jnp.log2(total)
        rowstat_ref[1:2, r0 : r0 + SLOT] = weighted / total


def grads_kernel(
    ordk, posq_ref, s0, s1, s2, s3, p0, p1, p2, p3, kva, kvb,
    dq0, dq1, dq2, dq3, keep, send, qr, gr, rowstat, dqr, dkv,
):
    fill_rows((p0, p1, p2, p3), qr, gr)
    combine_stats((s0, s1, s2, s3), rowstat)
    dkv[...] = jnp.zeros_like(dkv)

    def row_tile(rt, _):
        r0 = pl.multiple_of(rt * RT, RT)
        q = qr[pl.ds(r0, RT), :]
        g = gr[pl.ds(r0, RT), :]
        posq = posq_ref[:, pl.ds(r0, RT)]
        lse = rowstat[0:1, pl.ds(r0, RT)]
        delta = rowstat[1:2, pl.ds(r0, RT)]
        dq = jnp.zeros((RT, HEAD), f32)
        for chunk in range(KEYS // KC):
            kv = kva if chunk * KC < KHALF else kvb
            k0 = chunk * KC % KHALF
            key_rows = kv[k0 : k0 + KC, :HEAD]
            score = masked_scores(key_rows, q, posq, ordk, chunk * (KC // HALF))
            prob = jnp.exp2(score - lse)
            dprob = dot(kv[k0 : k0 + KC, HEAD:], g, NT)
            dscore = (prob * (dprob - delta)).astype(bf16)
            prob_low = prob.astype(bf16)
            dkv[chunk * KC : (chunk + 1) * KC, HEAD:] += dot(prob_low, g, NN)
            dkv[chunk * KC : (chunk + 1) * KC, :HEAD] += dot(dscore, q, NN)
            dq = dq + dot(dscore, key_rows, TN)
        dqr[pl.ds(r0, RT), :] = dq
        return 0

    lax.fori_loop(0, ALL_ROWS // RT, row_tile, 0)
    for d, out in enumerate((dq0, dq1, dq2, dq3)):
        for h in range(HEADS):
            r0 = slot_start(d) + h * ROWS
            out[:, h * HEAD : (h + 1) * HEAD] = (dqr[r0 : r0 + ROWS, :] * SCALE).astype(out.dtype)
    for out, k0 in ((keep, 0), (send, KHALF)):
        out[:, :HEAD] = (dkv[k0 : k0 + KHALF, :HEAD] * SCALE).astype(out.dtype)
        out[:, HEAD:] = dkv[k0 : k0 + KHALF, HEAD:].astype(out.dtype)


def columns_kernel(place_ref, own, other, x0, x1, x2, x3):
    ic = place_ref[1]
    src = lax.broadcasted_iota(jnp.int32, (512, 256), 0)
    dst = lax.broadcasted_iota(jnp.int32, (512, 256), 1)
    home = dst // 32 * 64 + dst % 32 + ic * 32
    pick = jnp.where(src == home, 1.0, 0.0).astype(bf16)
    for d, out in enumerate((x0, x1, x2, x3)):
        base = lax.rem(place_ref[0] + d, N_OUT) * 512
        for t, tok in enumerate((own, other)):
            for p in range(2):
                cols = tok[:, pl.ds(pl.multiple_of(base + p * 2048, 512), 512)]
                out[t, :, p * 256 : (p + 1) * 256] = dot(cols, pick, NN).astype(bf16)


def weights_kernel(x0, x1, x2, x3, q0, q1, q2, q3, k0, k1, k2, k3, qo, ko, out, xr, gr):
    wide = HEADS * HEAD
    for d, x in enumerate((x0, x1, x2, x3)):
        rows = slice(d * ROWS, (d + 1) * ROWS)
        other = slice((N_OUT + d) * ROWS, (N_OUT + d + 1) * ROWS)
        xr[rows, :] = x[0]
        xr[other, :] = x[1]
        gr[rows, :wide] = (q0, q1, q2, q3)[d][...]
        gr[rows, wide:] = (k0, k1, k2, k3)[d][...]
        gr[other, :wide] = qo[d]
        gr[other, wide:] = ko[d]
    dw = dot(xr[...], gr[...], TN).astype(bf16)
    for p in range(16):
        out[p] = dw[p * 32 : (p + 1) * 32]


VM = 24
smem = pl.BlockSpec(memory_space=pltpu.SMEM)
vmem = pl.BlockSpec(memory_space=pltpu.VMEM)
params = pltpu.CompilerParams(vmem_limit_bytes=VM * 1024 * 1024)


def cost(pairs, matmuls, size):
    return pl.CostEstimate(
        flops=2 * pairs * HEAD * matmuls, transcendentals=pairs, bytes_accessed=size
    )


def kernel_call(body, name, outs, scratch, estimate, aliases, scalars, *args):
    return pl.pallas_call(
        body,
        out_shape=tuple(jax.ShapeDtypeStruct(*o) for o in outs),
        in_specs=[smem] * scalars + [vmem] * (len(args) - scalars),
        out_specs=tuple(vmem for _ in outs),
        scratch_shapes=[pltpu.VMEM(*s) for s in scratch],
        compiler_params=params,
        cost_estimate=estimate,
        input_output_aliases=aliases,
        name=name,
    )(*args)


WIDE = HEADS * HEAD
row_scratch = [((ALL_ROWS, HEAD), bf16)] * 2
acc_rows = ((ALL_ROWS, HEAD), f32)


def shift(x, axis, d, n):
    return lax.ppermute(x, axis, [(i, (i + d) % n) for i in range(n)])


def from_behind(x, axis, n):
    return [x] + [shift(x, axis, d, n) for d in range(1, n)]


def per_device(inputs, block_order, w_query, w_key, w_value, grad_out):
    tokens = inputs[0]
    order = block_order[0]
    dout = grad_out[0]
    o, ix, iy, ic = (lax.axis_index(a) for a in ("outer", "x", "yh", "core"))

    query = dot(tokens, w_query, NN).astype(bf16)
    ps = from_behind(jnp.concatenate([query, dout], axis=1), "outer", N_OUT)
    kv = jnp.concatenate(
        [
            dot(tokens, w_key, NN).astype(bf16),
            dot(tokens, w_value, NN).astype(bf16),
        ],
        axis=1,
    )
    kva = jnp.broadcast_to(kv[None], (8,) + kv.shape)
    kva = lax.all_to_all(kva, ("x", "yh"), 0, 0, tiled=True).reshape(KHALF, 2 * HEAD)
    kvb = shift(kva, "core", 1, 2)

    key_dev = (o * 8 + np.arange(8)[None, :, None]) * 2 + (ic + np.arange(2)[:, None, None]) % 2
    key_blocks = (key_dev * 2 + np.arange(2)[None, None, :]).reshape(-1)
    query_dev = (((o - np.array([1, 2, 3, 0])) % N_OUT * N_X + ix) * 2 + iy) * 2 + ic
    query_blocks = (query_dev[:, None] * 2 + np.arange(2)[None, :]).reshape(-1)

    def look_up(blocks):
        hit = blocks[:, None] == jnp.arange(order.shape[0], dtype=jnp.int32)[None, :]
        return jnp.sum(jnp.where(hit, order[None, :], 0), axis=1)

    ordk = look_up(key_blocks)
    ordq = look_up(query_blocks).reshape(N_OUT, 1, 2, 1)
    posq = ordq * HALF + jnp.arange(HALF, dtype=jnp.int32)
    posq = jnp.broadcast_to(posq, (N_OUT, HEADS, 2, HALF)).reshape(1, ALL_ROWS)

    place = jnp.stack([o, ic])
    later, kv = lax.optimization_barrier((tokens, kv))
    other_tokens = shift(later, "core", 1, 2)
    xs = kernel_call(
        columns_kernel, "columns", [((2, ROWS, 512), bf16)] * N_OUT, [],
        cost(ROWS * 4096, 4, 5 << 20), {}, 1, place, later, other_tokens,
    )
    xs, kva = lax.optimization_barrier((xs, kva))
    xs = [xs[0]] + [shift(xs[d], "outer", d, N_OUT) for d in range(1, N_OUT)]
    (stats,) = kernel_call(
        stats_kernel, "stats", [((3, ALL_ROWS), f32)], row_scratch,
        cost(ALL_ROWS * KEYS, 2, 4 << 20), {}, 1, ordk, posq, *ps, kva, kvb,
    )
    all_stats = from_behind(stats, "outer", N_OUT)
    all_stats, xs = lax.optimization_barrier((all_stats, xs))

    half = (KHALF, 2 * HEAD)
    dq, dq1, dq2, dq3, keep, send = kernel_call(
        grads_kernel, "grads",
        [((ROWS, WIDE), f32)] + [((ROWS, WIDE), bf16)] * 3 + [(half, f32), (half, bf16)],
        row_scratch + [((2, ALL_ROWS), f32), acc_rows, ((KEYS, 2 * HEAD), f32)],
        cost(ALL_ROWS * KEYS, 5, 8 << 20), {}, 1,
        ordk, posq, *all_stats, *ps, kva, kvb,
    )
    got = shift(send, "core", 1, 2)
    dq_parts = [shift(part, "outer", -d, N_OUT) for d, part in ((1, dq1), (2, dq2), (3, dq3))]
    dkv = (keep + got.astype(f32)).astype(bf16).reshape(8, ROWS, 2 * HEAD)
    dkv = lax.all_to_all(dkv, ("x", "yh"), 0, 0, tiled=True)
    dkv = jnp.sum(dkv.astype(f32), axis=0)
    dkv_all = from_behind(dkv.astype(bf16), "outer", N_OUT)
    for part in dq_parts:
        dq = dq + part.astype(f32)
    dq_all = from_behind(dq.astype(bf16), "outer", N_OUT)

    dq_other = shift(jnp.stack(dq_all), "core", 1, 2)
    dkv_other = shift(jnp.stack(dkv_all), "core", 1, 2)
    (dw,) = kernel_call(
        weights_kernel, "weights", [((16, 32, 768), bf16)],
        [((2 * N_OUT * ROWS, 512), bf16), ((2 * N_OUT * ROWS, 768), bf16)],
        cost(1280 * 512, 6, 4 << 20), {}, 0,
        *xs, *dq_all, *dkv_all, dq_other, dkv_other,
    )
    dw = lax.all_to_all(dw, ("dp", "x", "yh"), 0, 0, tiled=True)
    dw = jnp.sum(dw.astype(f32), axis=0)
    wide = HEADS * HEAD
    return dw[:, :wide], dw[:, wide : wide + HEAD], dw[:, wide + HEAD :]


def solution(mesh):
    devices = np.asarray(mesh.devices).reshape(2, N_OUT, N_X, 2, 2)
    fine = Mesh(devices, ("dp", "outer", "x", "yh", "core"))
    seq = ("outer", "x", "yh", "core")
    rows = P(("dp",) + seq, None)
    return jax.shard_map(
        per_device,
        mesh=fine,
        in_specs=(
            P("dp", seq, None),
            P("dp", None),
            P(None, None),
            P(None, None),
            P(None, None),
            P("dp", seq, None),
        ),
        out_specs=(rows, rows, rows),
        check_vma=False,
    )
```

```python
import functools
import math

import jax
import jax.numpy as jnp
import numpy as np
from jax import lax
from jax.experimental import pallas as pl
from jax.experimental.pallas import tpu as pltpu
from jax.sharding import Mesh, PartitionSpec as P

masked_fill = -1e30
HEADS = 4
HEAD = 128
ROWS = 160
HALF = 80
N_OUT = 4
N_X = 4
SLOT = HEADS * ROWS
ALL_ROWS = N_OUT * SLOT
KEYS = 16 * ROWS
KHALF = KEYS // 2
RT = 1280
KC = 640
KS = 160
SCALE = 1.0 / math.sqrt(HEAD)
SCALE2 = SCALE * math.log2(math.e)
f32 = jnp.float32
bf16 = jnp.bfloat16
NT = (((1,), (1,)), ((), ()))
NN = (((1,), (0,)), ((), ()))
TN = (((0,), (0,)), ((), ()))


def dot(a, b, dims):
    return lax.dot_general(a, b, dims, preferred_element_type=f32)


def slot_start(d):
    return (d - 1) % N_OUT * SLOT


def fill_rows(pieces, rows_ref):
    for d in range(N_OUT):
        for h in range(HEADS):
            r0 = slot_start(d) + h * ROWS
            rows_ref[r0 : r0 + ROWS, :] = pieces[d][:, h * HEAD : (h + 1) * HEAD]


def masked_scores(key_rows, q, posq, ordk_ref, block):
    score = dot(key_rows, q, NT)
    place = lax.broadcasted_iota(jnp.int32, (HALF, RT), 0)
    parts = []
    for b in range(score.shape[0] // HALF):
        limit = posq - ordk_ref[block + b] * HALF
        part = score[b * HALF : (b + 1) * HALF] * SCALE2
        parts.append(jnp.where(place <= limit, part, masked_fill))
    return jnp.concatenate(parts, axis=0)


def stats_pass(block, ordk_ref, posq_ref, qs, gs, kv, before, out_ref, qr, gr):
    fill_rows(qs, qr)
    fill_rows(gs, gr)

    def row_tile(rt, _):
        r0 = pl.multiple_of(rt * RT, RT)
        q = qr[pl.ds(r0, RT), :]
        g = gr[pl.ds(r0, RT), :]
        posq = posq_ref[:, pl.ds(r0, RT)]
        top = jnp.full((8, RT), masked_fill, f32)
        total = jnp.zeros((8, RT), f32)
        weighted = jnp.zeros((8, RT), f32)
        for k0 in range(0, KHALF, KS):
            score = masked_scores(kv[k0 : k0 + KS, :HEAD], q, posq, ordk_ref, block + k0 // HALF)
            dprob = dot(kv[k0 : k0 + KS, HEAD:], g, NT)
            score = score.reshape(KS // 8, 8, RT)
            new_top = jnp.maximum(top, jnp.max(score, axis=0))
            weights = jnp.exp2(score - new_top[None])
            factor = jnp.exp2(top - new_top)
            total = total * factor + jnp.sum(weights, axis=0)
            weighted = weighted * factor + jnp.sum(weights * dprob.reshape(KS // 8, 8, RT), axis=0)
            top = new_top
        row_top = jnp.max(top, axis=0, keepdims=True)
        if before is not None:
            row_top = jnp.maximum(row_top, before[0:1, pl.ds(r0, RT)])
        factor = jnp.exp2(top - row_top)
        total = jnp.sum(total * factor, axis=0, keepdims=True)
        weighted = jnp.sum(weighted * factor, axis=0, keepdims=True)
        if before is not None:
            factor = jnp.exp2(before[0:1, pl.ds(r0, RT)] - row_top)
            total = total + before[1:2, pl.ds(r0, RT)] * factor
            weighted = weighted + before[2:3, pl.ds(r0, RT)] * factor
        out_ref[0:1, pl.ds(r0, RT)] = row_top
        out_ref[1:2, pl.ds(r0, RT)] = total
        out_ref[2:3, pl.ds(r0, RT)] = weighted
        return 0

    lax.fori_loop(0, ALL_ROWS // RT, row_tile, 0)


def stats_own(ordk, posq, q0, q1, q2, q3, g0, g1, g2, g3, kva, out, qr, gr):
    stats_pass(0, ordk, posq, (q0, q1, q2, q3), (g0, g1, g2, g3), kva, None, out, qr, gr)


def stats_other(ordk, posq, q0, q1, q2, q3, g0, g1, g2, g3, kvb, before, out, qr, gr):
    stats_pass(
        KHALF // HALF, ordk, posq, (q0, q1, q2, q3), (g0, g1, g2, g3), kvb, before, out, qr, gr
    )


def combine_stats(stats, rowstat_ref):
    for d in range(N_OUT):
        parts = []
        for e in range(N_OUT):
            c0 = slot_start(d - e)
            parts.append(stats[e][:, c0 : c0 + SLOT])
        row_top = parts[0][0:1]
        for part in parts[1:]:
            row_top = jnp.maximum(row_top, part[0:1])
        total = jnp.zeros_like(row_top)
        weighted = jnp.zeros_like(row_top)
        for part in parts:
            factor = jnp.exp2(part[0:1] - row_top)
            total = total + part[1:2] * factor
            weighted = weighted + part[2:3] * factor
        r0 = slot_start(d)
        rowstat_ref[0:1, r0 : r0 + SLOT] = row_top + jnp.log2(total)
        rowstat_ref[1:2, r0 : r0 + SLOT] = weighted / total


def grads_kernel(
    ordk, posq_ref, s0, s1, s2, s3, q0, q1, q2, q3, g0, g1, g2, g3, kva, kvb,
    dq0, dq1, dq2, dq3, keep, send, qr, gr, rowstat, dqr, dkv,
):
    fill_rows((q0, q1, q2, q3), qr)
    fill_rows((g0, g1, g2, g3), gr)
    combine_stats((s0, s1, s2, s3), rowstat)
    dkv[...] = jnp.zeros_like(dkv)

    def row_tile(rt, _):
        r0 = pl.multiple_of(rt * RT, RT)
        q = qr[pl.ds(r0, RT), :]
        g = gr[pl.ds(r0, RT), :]
        posq = posq_ref[:, pl.ds(r0, RT)]
        lse = rowstat[0:1, pl.ds(r0, RT)]
        delta = rowstat[1:2, pl.ds(r0, RT)]
        dq = jnp.zeros((RT, HEAD), f32)
        for chunk in range(KEYS // KC):
            kv = kva if chunk * KC < KHALF else kvb
            k0 = chunk * KC % KHALF
            key_rows = kv[k0 : k0 + KC, :HEAD]
            score = masked_scores(key_rows, q, posq, ordk, chunk * (KC // HALF))
            prob = jnp.exp2(score - lse)
            dprob = dot(kv[k0 : k0 + KC, HEAD:], g, NT)
            dscore = (prob * (dprob - delta)).astype(bf16)
            prob_low = prob.astype(bf16)
            dkv[chunk * KC : (chunk + 1) * KC, HEAD:] += dot(prob_low, g, NN)
            dkv[chunk * KC : (chunk + 1) * KC, :HEAD] += dot(dscore, q, NN)
            dq = dq + dot(dscore, key_rows, TN)
        dqr[pl.ds(r0, RT), :] = dq
        return 0

    lax.fori_loop(0, ALL_ROWS // RT, row_tile, 0)
    for d, out in enumerate((dq0, dq1, dq2, dq3)):
        for h in range(HEADS):
            r0 = slot_start(d) + h * ROWS
            out[:, h * HEAD : (h + 1) * HEAD] = (dqr[r0 : r0 + ROWS, :] * SCALE).astype(out.dtype)
    for out, k0 in ((keep, 0), (send, KHALF)):
        out[:, :HEAD] = (dkv[k0 : k0 + KHALF, :HEAD] * SCALE).astype(out.dtype)
        out[:, HEAD:] = dkv[k0 : k0 + KHALF, HEAD:].astype(out.dtype)


def columns_kernel(place_ref, own, other, x0, x1, x2, x3):
    ic = place_ref[1]
    src = lax.broadcasted_iota(jnp.int32, (512, 256), 0)
    dst = lax.broadcasted_iota(jnp.int32, (512, 256), 1)
    home = dst // 32 * 64 + dst % 32 + ic * 32
    pick = jnp.where(src == home, 1.0, 0.0).astype(bf16)
    for d, out in enumerate((x0, x1, x2, x3)):
        base = lax.rem(place_ref[0] + d, N_OUT) * 512
        for t, tok in enumerate((own, other)):
            for p in range(2):
                cols = tok[:, pl.ds(pl.multiple_of(base + p * 2048, 512), 512)]
                out[t, :, p * 256 : (p + 1) * 256] = dot(cols, pick, NN).astype(bf16)


def weights_kernel(x0, x1, x2, x3, q0, q1, q2, q3, k0, k1, k2, k3, qo, ko, out, xr, gr):
    wide = HEADS * HEAD
    for d, x in enumerate((x0, x1, x2, x3)):
        rows = slice(d * ROWS, (d + 1) * ROWS)
        other = slice((N_OUT + d) * ROWS, (N_OUT + d + 1) * ROWS)
        xr[rows, :] = x[0]
        xr[other, :] = x[1]
        gr[rows, :wide] = (q0, q1, q2, q3)[d][...]
        gr[rows, wide:] = (k0, k1, k2, k3)[d][...]
        gr[other, :wide] = qo[d]
        gr[other, wide:] = ko[d]
    dw = dot(xr[...], gr[...], TN).astype(bf16)
    for p in range(16):
        out[p] = dw[p * 32 : (p + 1) * 32]


def last_sum(parts, dwq, dwk, dwv):
    total = jnp.sum(parts[...].astype(f32), axis=0)
    wide = HEADS * HEAD
    dwq[...] = total[:, :wide]
    dwk[...] = total[:, wide : wide + HEAD]
    dwv[...] = total[:, wide + HEAD :]


VM = 24
smem = pl.BlockSpec(memory_space=pltpu.SMEM)
vmem = pl.BlockSpec(memory_space=pltpu.VMEM)
params = pltpu.CompilerParams(vmem_limit_bytes=VM * 1024 * 1024)


def cost(pairs, matmuls, size):
    return pl.CostEstimate(
        flops=2 * pairs * HEAD * matmuls, transcendentals=pairs, bytes_accessed=size
    )


def kernel_call(body, name, outs, scratch, estimate, aliases, scalars, *args):
    return pl.pallas_call(
        body,
        out_shape=tuple(jax.ShapeDtypeStruct(*o) for o in outs),
        in_specs=[smem] * scalars + [vmem] * (len(args) - scalars),
        out_specs=tuple(vmem for _ in outs),
        scratch_shapes=[pltpu.VMEM(*s) for s in scratch],
        compiler_params=params,
        cost_estimate=estimate,
        input_output_aliases=aliases,
        name=name,
    )(*args)


WIDE = HEADS * HEAD
row_scratch = [((ALL_ROWS, HEAD), bf16)] * 2
acc_rows = ((ALL_ROWS, HEAD), f32)


def shift(x, axis, d, n):
    return lax.ppermute(x, axis, [(i, (i + d) % n) for i in range(n)])


def from_behind(x, axis, n):
    return [x] + [shift(x, axis, d, n) for d in range(1, n)]


def per_device(inputs, block_order, w_query, w_key, w_value, grad_out):
    tokens = inputs[0]
    order = block_order[0]
    dout = grad_out[0]
    o, ix, iy, ic = (lax.axis_index(a) for a in ("outer", "x", "yh", "core"))

    query = dot(tokens, w_query, NN).astype(bf16)
    q1, q3 = shift(query, "outer", 1, N_OUT), shift(query, "outer", -1, N_OUT)
    g1, g3 = shift(dout, "outer", 1, N_OUT), shift(dout, "outer", -1, N_OUT)
    qs = [query, q1, shift(q1, "outer", 1, N_OUT), q3]
    gs = [dout, g1, shift(g3, "outer", -1, N_OUT), g3]
    kv = jnp.concatenate(
        [
            dot(tokens, w_key, NN).astype(bf16),
            dot(tokens, w_value, NN).astype(bf16),
        ],
        axis=1,
    )
    place = jnp.stack([o, ic])
    later, kv = lax.optimization_barrier((tokens, kv))
    other_tokens = shift(later, "core", 1, 2)
    xs = kernel_call(
        columns_kernel, "columns", [((2, ROWS, 512), bf16)] * N_OUT, [],
        cost(ROWS * 4096, 4, 5 << 20), {}, 1, place, later, other_tokens,
    )
    kva = jnp.broadcast_to(kv[None], (8,) + kv.shape)
    kva = lax.all_to_all(kva, ("x", "yh"), 0, 0, tiled=True).reshape(KHALF, 2 * HEAD)
    kva, qs, gs, xs = lax.optimization_barrier((kva, qs, gs, xs))
    kvb = shift(kva, "core", 1, 2)

    key_dev = (o * 8 + np.arange(8)[None, :, None]) * 2 + (ic + np.arange(2)[:, None, None]) % 2
    key_blocks = (key_dev * 2 + np.arange(2)[None, None, :]).reshape(-1)
    query_dev = (((o - np.array([1, 2, 3, 0])) % N_OUT * N_X + ix) * 2 + iy) * 2 + ic
    query_blocks = (query_dev[:, None] * 2 + np.arange(2)[None, :]).reshape(-1)

    def look_up(blocks):
        hit = blocks[:, None] == jnp.arange(order.shape[0], dtype=jnp.int32)[None, :]
        return jnp.sum(jnp.where(hit, order[None, :], 0), axis=1)

    ordk = look_up(key_blocks)
    ordq = look_up(query_blocks).reshape(N_OUT, 1, 2, 1)
    posq = ordq * HALF + jnp.arange(HALF, dtype=jnp.int32)
    posq = jnp.broadcast_to(posq, (N_OUT, HEADS, 2, HALF)).reshape(1, ALL_ROWS)

    pairs = cost(ALL_ROWS * KHALF, 2, 4 << 20)
    row_stats = [((3, ALL_ROWS), f32)]
    (stats,) = kernel_call(
        stats_own, "stats_own", row_stats, row_scratch, pairs, {}, 1, ordk, posq, *qs, *gs, kva
    )
    (stats,) = kernel_call(
        stats_other, "stats_other", row_stats, row_scratch, pairs, {}, 1,
        ordk, posq, *qs, *gs, kvb, stats,
    )
    xs, stats = lax.optimization_barrier((xs, stats))
    xs = [xs[0]] + [shift(xs[d], "outer", d, N_OUT) for d in range(1, N_OUT)]
    all_stats = from_behind(stats, "outer", N_OUT)

    half = (KHALF, 2 * HEAD)
    dq, dq1, dq2, dq3, keep, send = kernel_call(
        grads_kernel, "grads",
        [((ROWS, WIDE), f32)] + [((ROWS, WIDE), bf16)] * 3 + [(half, f32), (half, bf16)],
        row_scratch + [((2, ALL_ROWS), f32), acc_rows, ((KEYS, 2 * HEAD), f32)],
        cost(ALL_ROWS * KEYS, 5, 8 << 20), {}, 1,
        ordk, posq, *all_stats, *qs, *gs, kva, kvb,
    )
    send, dq1, dq2, dq3, xs = lax.optimization_barrier((send, dq1, dq2, dq3, xs))
    got = shift(send, "core", 1, 2)
    dq_parts = [shift(part, "outer", -d, N_OUT) for d, part in ((1, dq1), (2, dq2), (3, dq3))]
    dkv = (keep + got.astype(f32)).astype(bf16).reshape(8, ROWS, 2 * HEAD)
    dkv = lax.all_to_all(dkv, ("x", "yh"), 0, 0, tiled=True)
    dkv = jnp.sum(dkv.astype(f32), axis=0).astype(bf16)
    dkv_all = from_behind(dkv, "outer", N_OUT)
    for part in dq_parts:
        dq = dq + part.astype(f32)
    dq_all = from_behind(dq.astype(bf16), "outer", N_OUT)
    dq_all, dkv = lax.optimization_barrier((dq_all, dkv))

    dq_other = shift(jnp.stack(dq_all), "core", 1, 2)
    dkv_other = shift(jnp.stack(dkv_all), "core", 1, 2)
    (dw,) = kernel_call(
        weights_kernel, "weights", [((16, 32, 768), bf16)],
        [((2 * N_OUT * ROWS, 512), bf16), ((2 * N_OUT * ROWS, 768), bf16)],
        cost(1280 * 512, 6, 4 << 20), {}, 0,
        *xs, *dq_all, *dkv_all, dq_other, dkv_other,
    )
    dw = lax.all_to_all(dw, ("dp", "x", "yh"), 0, 0, tiled=True)
    return kernel_call(
        last_sum, "last_sum", [((32, WIDE), f32), ((32, HEAD), f32), ((32, HEAD), f32)], [],
        cost(32 * 16, 3, 1 << 20), {}, 0, dw,
    )


def solution(mesh):
    devices = np.asarray(mesh.devices).reshape(2, N_OUT, N_X, 2, 2)
    fine = Mesh(devices, ("dp", "outer", "x", "yh", "core"))
    seq = ("outer", "x", "yh", "core")
    rows = P(("dp",) + seq, None)
    return jax.shard_map(
        per_device,
        mesh=fine,
        in_specs=(
            P("dp", seq, None),
            P("dp", None),
            P(None, None),
            P(None, None),
            P(None, None),
            P("dp", seq, None),
        ),
        out_specs=(rows, rows, rows),
        check_vma=False,
    )
```

```python
import functools
import math

import jax
import jax.numpy as jnp
import numpy as np
from jax import lax
from jax.experimental import pallas as pl
from jax.experimental.pallas import tpu as pltpu
from jax.sharding import Mesh, PartitionSpec as P

masked_fill = -1e30
HEADS = 4
HEAD = 128
ROWS = 160
HALF = 80
N_OUT = 4
N_X = 4
SLOT = HEADS * ROWS
ALL_ROWS = N_OUT * SLOT
KEYS = 16 * ROWS
KHALF = KEYS // 2
RT = 1280
KC = 640
KS = 160
SCALE = 1.0 / math.sqrt(HEAD)
SCALE2 = SCALE * math.log2(math.e)
f32 = jnp.float32
bf16 = jnp.bfloat16
NT = (((1,), (1,)), ((), ()))
NN = (((1,), (0,)), ((), ()))
TN = (((0,), (0,)), ((), ()))


def dot(a, b, dims):
    return lax.dot_general(a, b, dims, preferred_element_type=f32)


def slot_start(d):
    return (d - 1) % N_OUT * SLOT


def fill_rows(pieces, rows_ref):
    for d in range(N_OUT):
        for h in range(HEADS):
            r0 = slot_start(d) + h * ROWS
            rows_ref[r0 : r0 + ROWS, :] = pieces[d][:, h * HEAD : (h + 1) * HEAD]


def masked_scores(key_rows, q, posq, ordk_ref, block):
    score = dot(key_rows, q, NT)
    place = lax.broadcasted_iota(jnp.int32, (HALF, RT), 0)
    parts = []
    for b in range(score.shape[0] // HALF):
        limit = posq - ordk_ref[block + b] * HALF
        part = score[b * HALF : (b + 1) * HALF] * SCALE2
        parts.append(jnp.where(place <= limit, part, masked_fill))
    return jnp.concatenate(parts, axis=0)


def stats_pass(block, ordk_ref, posq_ref, qr, gr, kv, before, out_ref):
    def row_tile(rt, _):
        r0 = pl.multiple_of(rt * RT, RT)
        q = qr[pl.ds(r0, RT), :]
        g = gr[pl.ds(r0, RT), :]
        posq = posq_ref[:, pl.ds(r0, RT)]
        top = jnp.full((8, RT), masked_fill, f32)
        total = jnp.zeros((8, RT), f32)
        weighted = jnp.zeros((8, RT), f32)
        for k0 in range(0, KHALF, KS):
            score = masked_scores(kv[k0 : k0 + KS, :HEAD], q, posq, ordk_ref, block + k0 // HALF)
            dprob = dot(kv[k0 : k0 + KS, HEAD:], g, NT)
            score = score.reshape(KS // 8, 8, RT)
            new_top = jnp.maximum(top, jnp.max(score, axis=0))
            weights = jnp.exp2(score - new_top[None])
            factor = jnp.exp2(top - new_top)
            total = total * factor + jnp.sum(weights, axis=0)
            weighted = weighted * factor + jnp.sum(weights * dprob.reshape(KS // 8, 8, RT), axis=0)
            top = new_top
        row_top = jnp.max(top, axis=0, keepdims=True)
        if before is not None:
            row_top = jnp.maximum(row_top, before[0:1, pl.ds(r0, RT)])
        factor = jnp.exp2(top - row_top)
        total = jnp.sum(total * factor, axis=0, keepdims=True)
        weighted = jnp.sum(weighted * factor, axis=0, keepdims=True)
        if before is not None:
            factor = jnp.exp2(before[0:1, pl.ds(r0, RT)] - row_top)
            total = total + before[1:2, pl.ds(r0, RT)] * factor
            weighted = weighted + before[2:3, pl.ds(r0, RT)] * factor
        out_ref[0:1, pl.ds(r0, RT)] = row_top
        out_ref[1:2, pl.ds(r0, RT)] = total
        out_ref[2:3, pl.ds(r0, RT)] = weighted
        return 0

    lax.fori_loop(0, ALL_ROWS // RT, row_tile, 0)


def stats_own(ordk, posq, q0, q1, q2, q3, g0, g1, g2, g3, kva, out, qr, gr):
    fill_rows((q0, q1, q2, q3), qr)
    fill_rows((g0, g1, g2, g3), gr)
    stats_pass(0, ordk, posq, qr, gr, kva, None, out)


def stats_other(ordk, posq, qr, gr, kvb, before, out):
    stats_pass(KHALF // HALF, ordk, posq, qr, gr, kvb, before, out)


def combine_stats(stats, rowstat_ref):
    for d in range(N_OUT):
        parts = []
        for e in range(N_OUT):
            c0 = slot_start(d - e)
            parts.append(stats[e][:, c0 : c0 + SLOT])
        row_top = parts[0][0:1]
        for part in parts[1:]:
            row_top = jnp.maximum(row_top, part[0:1])
        total = jnp.zeros_like(row_top)
        weighted = jnp.zeros_like(row_top)
        for part in parts:
            factor = jnp.exp2(part[0:1] - row_top)
            total = total + part[1:2] * factor
            weighted = weighted + part[2:3] * factor
        r0 = slot_start(d)
        rowstat_ref[0:1, r0 : r0 + SLOT] = row_top + jnp.log2(total)
        rowstat_ref[1:2, r0 : r0 + SLOT] = weighted / total


def grads_kernel(
    ordk, posq_ref, s0, s1, s2, s3, qr, gr, kva, kvb,
    dq0, dq1, dq2, dq3, keep, send, rowstat, dqr, dkv,
):
    combine_stats((s0, s1, s2, s3), rowstat)
    dkv[...] = jnp.zeros_like(dkv)

    def row_tile(rt, _):
        r0 = pl.multiple_of(rt * RT, RT)
        q = qr[pl.ds(r0, RT), :]
        g = gr[pl.ds(r0, RT), :]
        posq = posq_ref[:, pl.ds(r0, RT)]
        lse = rowstat[0:1, pl.ds(r0, RT)]
        delta = rowstat[1:2, pl.ds(r0, RT)]
        dq = jnp.zeros((RT, HEAD), f32)
        for chunk in range(KEYS // KC):
            kv = kva if chunk * KC < KHALF else kvb
            k0 = chunk * KC % KHALF
            key_rows = kv[k0 : k0 + KC, :HEAD]
            score = masked_scores(key_rows, q, posq, ordk, chunk * (KC // HALF))
            prob = jnp.exp2(score - lse)
            dprob = dot(kv[k0 : k0 + KC, HEAD:], g, NT)
            dscore = (prob * (dprob - delta)).astype(bf16)
            prob_low = prob.astype(bf16)
            dkv[chunk * KC : (chunk + 1) * KC, HEAD:] += dot(prob_low, g, NN)
            dkv[chunk * KC : (chunk + 1) * KC, :HEAD] += dot(dscore, q, NN)
            dq = dq + dot(dscore, key_rows, TN)
        dqr[pl.ds(r0, RT), :] = dq
        return 0

    lax.fori_loop(0, ALL_ROWS // RT, row_tile, 0)
    for d, out in enumerate((dq0, dq1, dq2, dq3)):
        for h in range(HEADS):
            r0 = slot_start(d) + h * ROWS
            out[:, h * HEAD : (h + 1) * HEAD] = (dqr[r0 : r0 + ROWS, :] * SCALE).astype(out.dtype)
    for out, k0 in ((keep, 0), (send, KHALF)):
        out[:, :HEAD] = (dkv[k0 : k0 + KHALF, :HEAD] * SCALE).astype(out.dtype)
        out[:, HEAD:] = dkv[k0 : k0 + KHALF, HEAD:].astype(out.dtype)


def columns_kernel(place_ref, own, other, x0, x1, x2, x3):
    ic = place_ref[1]
    src = lax.broadcasted_iota(jnp.int32, (512, 256), 0)
    dst = lax.broadcasted_iota(jnp.int32, (512, 256), 1)
    home = dst // 32 * 64 + dst % 32 + ic * 32
    pick = jnp.where(src == home, 1.0, 0.0).astype(bf16)
    for d, out in enumerate((x0, x1, x2, x3)):
        base = lax.rem(place_ref[0] + d, N_OUT) * 512
        for t, tok in enumerate((own, other)):
            for p in range(2):
                cols = tok[:, pl.ds(pl.multiple_of(base + p * 2048, 512), 512)]
                out[t, :, p * 256 : (p + 1) * 256] = dot(cols, pick, NN).astype(bf16)


def weights_kernel(x0, x1, x2, x3, q0, q1, q2, q3, k0, k1, k2, k3, qo, ko, out, xr, gr):
    wide = HEADS * HEAD
    for d, x in enumerate((x0, x1, x2, x3)):
        rows = slice(d * ROWS, (d + 1) * ROWS)
        other = slice((N_OUT + d) * ROWS, (N_OUT + d + 1) * ROWS)
        xr[rows, :] = x[0]
        xr[other, :] = x[1]
        gr[rows, :wide] = (q0, q1, q2, q3)[d][...]
        gr[rows, wide:] = (k0, k1, k2, k3)[d][...]
        gr[other, :wide] = qo[d]
        gr[other, wide:] = ko[d]
    dw = dot(xr[...], gr[...], TN).astype(bf16)
    for p in range(16):
        out[p] = dw[p * 32 : (p + 1) * 32]


def last_sum(parts, dwq, dwk, dwv):
    total = jnp.sum(parts[...].astype(f32), axis=0)
    wide = HEADS * HEAD
    dwq[...] = total[:, :wide]
    dwk[...] = total[:, wide : wide + HEAD]
    dwv[...] = total[:, wide + HEAD :]


VM = 24
smem = pl.BlockSpec(memory_space=pltpu.SMEM)
vmem = pl.BlockSpec(memory_space=pltpu.VMEM)
params = pltpu.CompilerParams(vmem_limit_bytes=VM * 1024 * 1024)


def cost(pairs, matmuls, size):
    return pl.CostEstimate(
        flops=2 * pairs * HEAD * matmuls, transcendentals=pairs, bytes_accessed=size
    )


def kernel_call(body, name, outs, scratch, estimate, spaces, *args):
    return pl.pallas_call(
        body,
        out_shape=tuple(jax.ShapeDtypeStruct(*o) for o in outs),
        in_specs=spaces + [vmem] * (len(args) - len(spaces)),
        out_specs=tuple(vmem for _ in outs),
        scratch_shapes=[pltpu.VMEM(*s) for s in scratch],
        compiler_params=params,
        cost_estimate=estimate,
        name=name,
    )(*args)


WIDE = HEADS * HEAD
acc_rows = ((ALL_ROWS, HEAD), f32)


def shift(x, axis, d, n):
    return lax.ppermute(x, axis, [(i, (i + d) % n) for i in range(n)])


def from_behind(x, axis, n):
    return [x] + [shift(x, axis, d, n) for d in range(1, n)]


def per_device(inputs, block_order, w_query, w_key, w_value, grad_out):
    tokens = inputs[0]
    order = block_order[0]
    dout = grad_out[0]
    o, ix, iy, ic = (lax.axis_index(a) for a in ("outer", "x", "yh", "core"))

    query = dot(tokens, w_query, NN).astype(bf16)
    q1, q3 = shift(query, "outer", 1, N_OUT), shift(query, "outer", -1, N_OUT)
    g1, g3 = shift(dout, "outer", 1, N_OUT), shift(dout, "outer", -1, N_OUT)
    qs = [query, q1, shift(q1, "outer", 1, N_OUT), q3]
    gs = [dout, g1, shift(g3, "outer", -1, N_OUT), g3]
    kv = jnp.concatenate(
        [
            dot(tokens, w_key, NN).astype(bf16),
            dot(tokens, w_value, NN).astype(bf16),
        ],
        axis=1,
    )
    kva = jnp.broadcast_to(kv[None], (8,) + kv.shape)
    kva = lax.all_to_all(kva, ("x", "yh"), 0, 0, tiled=True).reshape(KHALF, 2 * HEAD)
    kva, qs, gs = lax.optimization_barrier((kva, qs, gs))
    kvb = shift(kva, "core", 1, 2)
    later, kva = lax.optimization_barrier((tokens, kva))
    other_tokens = shift(later, "core", 1, 2)

    key_dev = (o * 8 + np.arange(8)[None, :, None]) * 2 + (ic + np.arange(2)[:, None, None]) % 2
    key_blocks = (key_dev * 2 + np.arange(2)[None, None, :]).reshape(-1)
    query_dev = (((o - np.array([1, 2, 3, 0])) % N_OUT * N_X + ix) * 2 + iy) * 2 + ic
    query_blocks = (query_dev[:, None] * 2 + np.arange(2)[None, :]).reshape(-1)

    def look_up(blocks):
        hit = blocks[:, None] == jnp.arange(order.shape[0], dtype=jnp.int32)[None, :]
        return jnp.sum(jnp.where(hit, order[None, :], 0), axis=1)

    ordk = look_up(key_blocks)
    ordq = look_up(query_blocks).reshape(N_OUT, 1, 2, 1)
    posq = ordq * HALF + jnp.arange(HALF, dtype=jnp.int32)
    posq = jnp.broadcast_to(posq, (N_OUT, HEADS, 2, HALF)).reshape(1, ALL_ROWS)

    pairs = cost(ALL_ROWS * KHALF, 2, 4 << 20)
    row_stats = [((3, ALL_ROWS), f32)]
    rows = ((ALL_ROWS, HEAD), bf16)
    stats, qr, gr = kernel_call(
        stats_own, "stats_own", row_stats + [rows, rows], [], pairs, [smem],
        ordk, posq, *qs, *gs, kva,
    )
    (stats,) = kernel_call(
        stats_other, "stats_other", row_stats, [], pairs, [smem], ordk, posq, qr, gr, kvb, stats
    )
    later, other_tokens, stats = lax.optimization_barrier((later, other_tokens, stats))
    xs = kernel_call(
        columns_kernel, "columns", [((2, ROWS, 512), bf16)] * N_OUT, [],
        cost(ROWS * 4096, 4, 5 << 20), [smem], jnp.stack([o, ic]), later, other_tokens,
    )
    xs = [xs[0]] + [shift(xs[d], "outer", d, N_OUT) for d in range(1, N_OUT)]
    all_stats = from_behind(stats, "outer", N_OUT)

    half = (KHALF, 2 * HEAD)
    dq, dq1, dq2, dq3, keep, send = kernel_call(
        grads_kernel, "grads",
        [((ROWS, WIDE), f32)] + [((ROWS, WIDE), bf16)] * 3 + [(half, f32), (half, bf16)],
        [((2, ALL_ROWS), f32), acc_rows, ((KEYS, 2 * HEAD), f32)],
        cost(ALL_ROWS * KEYS, 5, 8 << 20), [smem], ordk, posq, *all_stats, qr, gr, kva, kvb,
    )
    send, dq1, dq2, dq3, xs = lax.optimization_barrier((send, dq1, dq2, dq3, xs))
    got = shift(send, "core", 1, 2)
    dq_parts = [shift(part, "outer", -d, N_OUT) for d, part in ((1, dq1), (2, dq2), (3, dq3))]
    dkv = (keep + got.astype(f32)).astype(bf16).reshape(8, ROWS, 2 * HEAD)
    dkv = lax.all_to_all(dkv, ("x", "yh"), 0, 0, tiled=True)
    dkv = jnp.sum(dkv.astype(f32), axis=0).astype(bf16)
    dkv_all = from_behind(dkv, "outer", N_OUT)
    for part in dq_parts:
        dq = dq + part.astype(f32)
    dq_all = from_behind(dq.astype(bf16), "outer", N_OUT)
    dq_all, dkv = lax.optimization_barrier((dq_all, dkv))

    dq_other = shift(jnp.stack(dq_all), "core", 1, 2)
    dkv_other = shift(jnp.stack(dkv_all), "core", 1, 2)
    (dw,) = kernel_call(
        weights_kernel, "weights", [((16, 32, 768), bf16)],
        [((2 * N_OUT * ROWS, 512), bf16), ((2 * N_OUT * ROWS, 768), bf16)],
        cost(1280 * 512, 6, 4 << 20), [],
        *xs, *dq_all, *dkv_all, dq_other, dkv_other,
    )
    dw = lax.all_to_all(dw, ("dp", "x", "yh"), 0, 0, tiled=True)
    return kernel_call(
        last_sum, "last_sum", [((32, WIDE), f32), ((32, HEAD), f32), ((32, HEAD), f32)], [],
        cost(32 * 16, 3, 1 << 20), [], dw,
    )


def solution(mesh):
    devices = np.asarray(mesh.devices).reshape(2, N_OUT, N_X, 2, 2)
    fine = Mesh(devices, ("dp", "outer", "x", "yh", "core"))
    seq = ("outer", "x", "yh", "core")
    rows = P(("dp",) + seq, None)
    return jax.shard_map(
        per_device,
        mesh=fine,
        in_specs=(
            P("dp", seq, None),
            P("dp", None),
            P(None, None),
            P(None, None),
            P(None, None),
            P("dp", seq, None),
        ),
        out_specs=(rows, rows, rows),
        check_vma=False,
    )
```

```python
import functools
import math

import jax
import jax.numpy as jnp
import numpy as np
from jax import lax
from jax.experimental import pallas as pl
from jax.experimental.pallas import tpu as pltpu
from jax.sharding import Mesh, PartitionSpec as P

masked_fill = -1e30
HEADS = 4
HEAD = 128
ROWS = 160
HALF = 80
N_OUT = 4
N_X = 4
SLOT = HEADS * ROWS
ALL_ROWS = N_OUT * SLOT
KEYS = 16 * ROWS
KHALF = KEYS // 2
RT = 1280
KC = 640
KS = 160
SCALE = 1.0 / math.sqrt(HEAD)
SCALE2 = SCALE * math.log2(math.e)
f32 = jnp.float32
bf16 = jnp.bfloat16
NT = (((1,), (1,)), ((), ()))
NN = (((1,), (0,)), ((), ()))
TN = (((0,), (0,)), ((), ()))


def dot(a, b, dims):
    return lax.dot_general(a, b, dims, preferred_element_type=f32)


def slot_start(d):
    return (d - 1) % N_OUT * SLOT


def fill_rows(pieces, rows_ref):
    for d in range(N_OUT):
        for h in range(HEADS):
            r0 = slot_start(d) + h * ROWS
            rows_ref[r0 : r0 + ROWS, :] = pieces[d][:, h * HEAD : (h + 1) * HEAD]


def masked_scores(key_rows, q, posq, ordk_ref, block):
    score = dot(key_rows, q, NT)
    place = lax.broadcasted_iota(jnp.int32, (HALF, RT), 0)
    parts = []
    for b in range(score.shape[0] // HALF):
        limit = posq - ordk_ref[block + b] * HALF
        part = score[b * HALF : (b + 1) * HALF] * SCALE2
        parts.append(jnp.where(place <= limit, part, masked_fill))
    return jnp.concatenate(parts, axis=0)


def stats_pass(block, ordk_ref, posq_ref, qr, gr, kv, before, out_ref):
    def row_tile(rt, _):
        r0 = pl.multiple_of(rt * RT, RT)
        q = qr[pl.ds(r0, RT), :]
        g = gr[pl.ds(r0, RT), :]
        posq = posq_ref[:, pl.ds(r0, RT)]
        top = jnp.full((8, RT), masked_fill, f32)
        total = jnp.zeros((8, RT), f32)
        weighted = jnp.zeros((8, RT), f32)
        for k0 in range(0, KHALF, KS):
            score = masked_scores(kv[k0 : k0 + KS, :HEAD], q, posq, ordk_ref, block + k0 // HALF)
            dprob = dot(kv[k0 : k0 + KS, HEAD:], g, NT)
            score = score.reshape(KS // 8, 8, RT)
            new_top = jnp.maximum(top, jnp.max(score, axis=0))
            weights = jnp.exp2(score - new_top[None])
            factor = jnp.exp2(top - new_top)
            total = total * factor + jnp.sum(weights, axis=0)
            weighted = weighted * factor + jnp.sum(weights * dprob.reshape(KS // 8, 8, RT), axis=0)
            top = new_top
        row_top = jnp.max(top, axis=0, keepdims=True)
        if before is not None:
            row_top = jnp.maximum(row_top, before[0:1, pl.ds(r0, RT)])
        factor = jnp.exp2(top - row_top)
        total = jnp.sum(total * factor, axis=0, keepdims=True)
        weighted = jnp.sum(weighted * factor, axis=0, keepdims=True)
        if before is not None:
            factor = jnp.exp2(before[0:1, pl.ds(r0, RT)] - row_top)
            total = total + before[1:2, pl.ds(r0, RT)] * factor
            weighted = weighted + before[2:3, pl.ds(r0, RT)] * factor
        out_ref[0:1, pl.ds(r0, RT)] = row_top
        out_ref[1:2, pl.ds(r0, RT)] = total
        out_ref[2:3, pl.ds(r0, RT)] = weighted
        return 0

    lax.fori_loop(0, ALL_ROWS // RT, row_tile, 0)


def stats_own(ordk, posq, q0, q1, q2, q3, g0, g1, g2, g3, kva, out, qr, gr):
    fill_rows((q0, q1, q2, q3), qr)
    fill_rows((g0, g1, g2, g3), gr)
    stats_pass(0, ordk, posq, qr, gr, kva, None, out)


def stats_other(ordk, posq, qr, gr, kvb, before, out):
    stats_pass(KHALF // HALF, ordk, posq, qr, gr, kvb, before, out)


def combine_stats(stats, rowstat_ref):
    for d in range(N_OUT):
        parts = []
        for e in range(N_OUT):
            c0 = slot_start(d - e)
            parts.append(stats[e][:, c0 : c0 + SLOT])
        row_top = parts[0][0:1]
        for part in parts[1:]:
            row_top = jnp.maximum(row_top, part[0:1])
        total = jnp.zeros_like(row_top)
        weighted = jnp.zeros_like(row_top)
        for part in parts:
            factor = jnp.exp2(part[0:1] - row_top)
            total = total + part[1:2] * factor
            weighted = weighted + part[2:3] * factor
        r0 = slot_start(d)
        rowstat_ref[0:1, r0 : r0 + SLOT] = row_top + jnp.log2(total)
        rowstat_ref[1:2, r0 : r0 + SLOT] = weighted / total


def grads_kernel(
    ordk, posq_ref, s0, s1, s2, s3, qr, gr, kva, kvb,
    dq0, dq1, dq2, dq3, keep, send, rowstat, dqr, dkv,
):
    combine_stats((s0, s1, s2, s3), rowstat)
    dkv[...] = jnp.zeros_like(dkv)

    def row_tile(rt, _):
        r0 = pl.multiple_of(rt * RT, RT)
        q = qr[pl.ds(r0, RT), :]
        g = gr[pl.ds(r0, RT), :]
        posq = posq_ref[:, pl.ds(r0, RT)]
        lse = rowstat[0:1, pl.ds(r0, RT)]
        delta = rowstat[1:2, pl.ds(r0, RT)]
        dq = jnp.zeros((RT, HEAD), f32)
        for chunk in range(KEYS // KC):
            kv = kva if chunk * KC < KHALF else kvb
            k0 = chunk * KC % KHALF
            key_rows = kv[k0 : k0 + KC, :HEAD]
            score = masked_scores(key_rows, q, posq, ordk, chunk * (KC // HALF))
            prob = jnp.exp2(score - lse)
            dprob = dot(kv[k0 : k0 + KC, HEAD:], g, NT)
            dscore = (prob * (dprob - delta)).astype(bf16)
            prob_low = prob.astype(bf16)
            dkv[chunk * KC : (chunk + 1) * KC, HEAD:] += dot(prob_low, g, NN)
            dkv[chunk * KC : (chunk + 1) * KC, :HEAD] += dot(dscore, q, NN)
            dq = dq + dot(dscore, key_rows, TN)
        dqr[pl.ds(r0, RT), :] = dq
        return 0

    lax.fori_loop(0, ALL_ROWS // RT, row_tile, 0)
    for d, out in enumerate((dq0, dq1, dq2, dq3)):
        for h in range(HEADS):
            r0 = slot_start(d) + h * ROWS
            out[:, h * HEAD : (h + 1) * HEAD] = (dqr[r0 : r0 + ROWS, :] * SCALE).astype(out.dtype)
    for out, k0 in ((keep, 0), (send, KHALF)):
        out[:, :HEAD] = (dkv[k0 : k0 + KHALF, :HEAD] * SCALE).astype(out.dtype)
        out[:, HEAD:] = dkv[k0 : k0 + KHALF, HEAD:].astype(out.dtype)


def columns_kernel(place_ref, own, other, x0, x1, x2, x3):
    ic = place_ref[1]
    src = lax.broadcasted_iota(jnp.int32, (512, 256), 0)
    dst = lax.broadcasted_iota(jnp.int32, (512, 256), 1)
    home = dst // 32 * 64 + dst % 32 + ic * 32
    pick = jnp.where(src == home, 1.0, 0.0).astype(bf16)
    for d, out in enumerate((x0, x1, x2, x3)):
        base = lax.rem(place_ref[0] + d, N_OUT) * 512
        for t, tok in enumerate((own, other)):
            for p in range(2):
                cols = tok[:, pl.ds(pl.multiple_of(base + p * 2048, 512), 512)]
                out[t, :, p * 256 : (p + 1) * 256] = dot(cols, pick, NN).astype(bf16)


def weights_kernel(x0, x1, x2, x3, q0, q1, q2, q3, k0, k1, k2, k3, grads, out, xr, gr):
    wide = HEADS * HEAD
    for d, x in enumerate((x0, x1, x2, x3)):
        rows = slice(d * ROWS, (d + 1) * ROWS)
        other = slice((N_OUT + d) * ROWS, (N_OUT + d + 1) * ROWS)
        xr[rows, :] = x[0]
        xr[other, :] = x[1]
        gr[rows, :wide] = (q0, q1, q2, q3)[d][...]
        gr[rows, wide:] = (k0, k1, k2, k3)[d][...]
        gr[other, :] = grads[d]
    dw = dot(xr[...], gr[...], TN).astype(bf16)
    for p in range(16):
        out[p] = dw[p * 32 : (p + 1) * 32]


def last_sum(parts, dwq, dwk, dwv):
    total = jnp.sum(parts[...].astype(f32), axis=0)
    wide = HEADS * HEAD
    dwq[...] = total[:, :wide]
    dwk[...] = total[:, wide : wide + HEAD]
    dwv[...] = total[:, wide + HEAD :]


VM = 24
smem = pl.BlockSpec(memory_space=pltpu.SMEM)
vmem = pl.BlockSpec(memory_space=pltpu.VMEM)
params = pltpu.CompilerParams(vmem_limit_bytes=VM * 1024 * 1024)


def cost(pairs, matmuls, size):
    return pl.CostEstimate(
        flops=2 * pairs * HEAD * matmuls, transcendentals=pairs, bytes_accessed=size
    )


def kernel_call(body, name, outs, scratch, estimate, spaces, *args):
    return pl.pallas_call(
        body,
        out_shape=tuple(jax.ShapeDtypeStruct(*o) for o in outs),
        in_specs=spaces + [vmem] * (len(args) - len(spaces)),
        out_specs=tuple(vmem for _ in outs),
        scratch_shapes=[pltpu.VMEM(*s) for s in scratch],
        compiler_params=params,
        cost_estimate=estimate,
        name=name,
    )(*args)


WIDE = HEADS * HEAD
acc_rows = ((ALL_ROWS, HEAD), f32)


def shift(x, axis, d, n):
    return lax.ppermute(x, axis, [(i, (i + d) % n) for i in range(n)])


def from_behind(x, axis, n):
    return [x] + [shift(x, axis, d, n) for d in range(1, n)]


def per_device(inputs, block_order, w_query, w_key, w_value, grad_out):
    tokens = inputs[0]
    order = block_order[0]
    dout = grad_out[0]
    o, ix, iy, ic = (lax.axis_index(a) for a in ("outer", "x", "yh", "core"))

    query = dot(tokens, w_query, NN).astype(bf16)
    q1, q3 = shift(query, "outer", 1, N_OUT), shift(query, "outer", -1, N_OUT)
    g1, g3 = shift(dout, "outer", 1, N_OUT), shift(dout, "outer", -1, N_OUT)
    qs = [query, q1, shift(q1, "outer", 1, N_OUT), q3]
    gs = [dout, g1, shift(g3, "outer", -1, N_OUT), g3]
    kv = jnp.concatenate(
        [
            dot(tokens, w_key, NN).astype(bf16),
            dot(tokens, w_value, NN).astype(bf16),
        ],
        axis=1,
    )
    kva = jnp.broadcast_to(kv[None], (8,) + kv.shape)
    kva = lax.all_to_all(kva, ("x", "yh"), 0, 0, tiled=True).reshape(KHALF, 2 * HEAD)
    other_tokens = shift(tokens, "core", 1, 2)
    later = tokens
    kva, qs, gs, other_tokens = lax.optimization_barrier((kva, qs, gs, other_tokens))
    kvb = shift(kva, "core", 1, 2)

    key_dev = (o * 8 + np.arange(8)[None, :, None]) * 2 + (ic + np.arange(2)[:, None, None]) % 2
    key_blocks = (key_dev * 2 + np.arange(2)[None, None, :]).reshape(-1)
    query_dev = (((o - np.array([1, 2, 3, 0])) % N_OUT * N_X + ix) * 2 + iy) * 2 + ic
    query_blocks = (query_dev[:, None] * 2 + np.arange(2)[None, :]).reshape(-1)

    def look_up(blocks):
        hit = blocks[:, None] == jnp.arange(order.shape[0], dtype=jnp.int32)[None, :]
        return jnp.sum(jnp.where(hit, order[None, :], 0), axis=1)

    ordk = look_up(key_blocks)
    ordq = look_up(query_blocks).reshape(N_OUT, 1, 2, 1)
    posq = ordq * HALF + jnp.arange(HALF, dtype=jnp.int32)
    posq = jnp.broadcast_to(posq, (N_OUT, HEADS, 2, HALF)).reshape(1, ALL_ROWS)

    pairs = cost(ALL_ROWS * KHALF, 2, 4 << 20)
    row_stats = [((3, ALL_ROWS), f32)]
    rows = ((ALL_ROWS, HEAD), bf16)
    stats, qr, gr = kernel_call(
        stats_own, "stats_own", row_stats + [rows, rows], [], pairs, [smem],
        ordk, posq, *qs, *gs, kva,
    )
    (stats,) = kernel_call(
        stats_other, "stats_other", row_stats, [], pairs, [smem], ordk, posq, qr, gr, kvb, stats
    )
    later, other_tokens, stats = lax.optimization_barrier((later, other_tokens, stats))
    xs = kernel_call(
        columns_kernel, "columns", [((2, ROWS, 512), bf16)] * N_OUT, [],
        cost(ROWS * 4096, 4, 5 << 20), [smem], jnp.stack([o, ic]), later, other_tokens,
    )
    xs = [xs[0]] + [shift(xs[d], "outer", d, N_OUT) for d in range(1, N_OUT)]
    all_stats = from_behind(stats, "outer", N_OUT)

    half = (KHALF, 2 * HEAD)
    dq, dq1, dq2, dq3, keep, send = kernel_call(
        grads_kernel, "grads",
        [((ROWS, WIDE), f32)] + [((ROWS, WIDE), bf16)] * 3 + [(half, f32), (half, bf16)],
        [((2, ALL_ROWS), f32), acc_rows, ((KEYS, 2 * HEAD), f32)],
        cost(ALL_ROWS * KEYS, 5, 8 << 20), [smem], ordk, posq, *all_stats, qr, gr, kva, kvb,
    )
    send, dq1, dq2, dq3, xs = lax.optimization_barrier((send, dq1, dq2, dq3, xs))
    got = shift(send, "core", 1, 2)
    dq_parts = [shift(part, "outer", -d, N_OUT) for d, part in ((1, dq1), (2, dq2), (3, dq3))]
    dkv = (keep + got.astype(f32)).astype(bf16).reshape(8, ROWS, 2 * HEAD)
    dkv = lax.all_to_all(dkv, ("x", "yh"), 0, 0, tiled=True)
    dkv = jnp.sum(dkv.astype(f32), axis=0).astype(bf16)
    dkv_all = from_behind(dkv, "outer", N_OUT)
    for part in dq_parts:
        dq = dq + part.astype(f32)
    dq_all = from_behind(dq.astype(bf16), "outer", N_OUT)
    dq_all, dkv_all = lax.optimization_barrier((dq_all, dkv_all))

    grads = [jnp.concatenate(pair, axis=1) for pair in zip(dq_all, dkv_all)]
    other_grads = shift(jnp.stack(grads), "core", 1, 2)
    (dw,) = kernel_call(
        weights_kernel, "weights", [((16, 32, 768), bf16)],
        [((2 * N_OUT * ROWS, 512), bf16), ((2 * N_OUT * ROWS, 768), bf16)],
        cost(1280 * 512, 6, 4 << 20), [],
        *xs, *dq_all, *dkv_all, other_grads,
    )
    dw = lax.all_to_all(dw, ("dp", "x", "yh"), 0, 0, tiled=True)
    return kernel_call(
        last_sum, "last_sum", [((32, WIDE), f32), ((32, HEAD), f32), ((32, HEAD), f32)], [],
        cost(32 * 16, 3, 1 << 20), [], dw,
    )


def solution(mesh):
    devices = np.asarray(mesh.devices).reshape(2, N_OUT, N_X, 2, 2)
    fine = Mesh(devices, ("dp", "outer", "x", "yh", "core"))
    seq = ("outer", "x", "yh", "core")
    rows = P(("dp",) + seq, None)
    return jax.shard_map(
        per_device,
        mesh=fine,
        in_specs=(
            P("dp", seq, None),
            P("dp", None),
            P(None, None),
            P(None, None),
            P(None, None),
            P("dp", seq, None),
        ),
        out_specs=(rows, rows, rows),
        check_vma=False,
    )
```

```python
import functools
import math

import jax
import jax.numpy as jnp
import numpy as np
from jax import lax
from jax.experimental import pallas as pl
from jax.experimental.pallas import tpu as pltpu
from jax.sharding import Mesh, PartitionSpec as P

masked_fill = -1e30
HEADS = 4
HEAD = 128
ROWS = 160
HALF = 80
N_OUT = 4
N_X = 4
SLOT = HEADS * ROWS
ALL_ROWS = N_OUT * SLOT
KEYS = 16 * ROWS
KHALF = KEYS // 2
RT = 1280
KC = 640
KS = 160
SCALE = 1.0 / math.sqrt(HEAD)
SCALE2 = SCALE * math.log2(math.e)
f32 = jnp.float32
bf16 = jnp.bfloat16
NT = (((1,), (1,)), ((), ()))
NN = (((1,), (0,)), ((), ()))
TN = (((0,), (0,)), ((), ()))


def dot(a, b, dims):
    return lax.dot_general(a, b, dims, preferred_element_type=f32)


def slot_start(d):
    return (d - 1) % N_OUT * SLOT


def fill_rows(pieces, rows_ref):
    for d in range(N_OUT):
        for h in range(HEADS):
            r0 = slot_start(d) + h * ROWS
            rows_ref[r0 : r0 + ROWS, :] = pieces[d][:, h * HEAD : (h + 1) * HEAD]


def masked_scores(key_rows, q, posq, ordk_ref, block):
    score = dot(key_rows, q, NT)
    place = lax.broadcasted_iota(jnp.int32, (HALF, RT), 0)
    parts = []
    for b in range(score.shape[0] // HALF):
        limit = posq - ordk_ref[block + b] * HALF
        part = score[b * HALF : (b + 1) * HALF] * SCALE2
        parts.append(jnp.where(place <= limit, part, masked_fill))
    return jnp.concatenate(parts, axis=0)


def stats_pass(block, ordk_ref, posq_ref, qr, gr, kv, before, out_ref):
    def row_tile(rt, _):
        r0 = pl.multiple_of(rt * RT, RT)
        q = qr[pl.ds(r0, RT), :]
        g = gr[pl.ds(r0, RT), :]
        posq = posq_ref[:, pl.ds(r0, RT)]
        def chunk(k0, carry):
            top, total, weighted = carry
            score = masked_scores(kv[pl.ds(k0, KS), :HEAD], q, posq, ordk_ref, block + k0 // HALF)
            dprob = dot(kv[pl.ds(k0, KS), HEAD:], g, NT)
            score = score.reshape(KS // 8, 8, RT)
            new_top = jnp.maximum(top, jnp.max(score, axis=0))
            weights = jnp.exp2(score - new_top[None])
            factor = jnp.exp2(top - new_top)
            total = total * factor + jnp.sum(weights, axis=0)
            weighted = weighted * factor + jnp.sum(weights * dprob.reshape(KS // 8, 8, RT), axis=0)
            return new_top, total, weighted

        def chunks(i, carry):
            for j in range(2):
                carry = chunk(pl.multiple_of((i * 2 + j) * KS, KS), carry)
            return carry

        empty = jnp.zeros((8, RT), f32)
        carry = (jnp.full((8, RT), masked_fill, f32), empty, empty)
        top, total, weighted = lax.fori_loop(0, KHALF // (2 * KS), chunks, carry)
        row_top = jnp.max(top, axis=0, keepdims=True)
        if before is not None:
            row_top = jnp.maximum(row_top, before[0:1, pl.ds(r0, RT)])
        factor = jnp.exp2(top - row_top)
        total = jnp.sum(total * factor, axis=0, keepdims=True)
        weighted = jnp.sum(weighted * factor, axis=0, keepdims=True)
        if before is not None:
            factor = jnp.exp2(before[0:1, pl.ds(r0, RT)] - row_top)
            total = total + before[1:2, pl.ds(r0, RT)] * factor
            weighted = weighted + before[2:3, pl.ds(r0, RT)] * factor
        out_ref[0:1, pl.ds(r0, RT)] = row_top
        out_ref[1:2, pl.ds(r0, RT)] = total
        out_ref[2:3, pl.ds(r0, RT)] = weighted
        return 0

    lax.fori_loop(0, ALL_ROWS // RT, row_tile, 0)


def stats_own(ordk, posq, q0, q1, q2, q3, g0, g1, g2, g3, kva, out, qr, gr):
    fill_rows((q0, q1, q2, q3), qr)
    fill_rows((g0, g1, g2, g3), gr)
    stats_pass(0, ordk, posq, qr, gr, kva, None, out)


def stats_other(ordk, posq, qr, gr, kvb, before, out):
    stats_pass(KHALF // HALF, ordk, posq, qr, gr, kvb, before, out)


def combined_stats(stats, d):
    parts = []
    for e in range(N_OUT):
        c0 = slot_start(d - e)
        parts.append(stats[e][:, c0 : c0 + SLOT])
    row_top = parts[0][0:1]
    for part in parts[1:]:
        row_top = jnp.maximum(row_top, part[0:1])
    total = jnp.zeros_like(row_top)
    weighted = jnp.zeros_like(row_top)
    for part in parts:
        factor = jnp.exp2(part[0:1] - row_top)
        total = total + part[1:2] * factor
        weighted = weighted + part[2:3] * factor
    return row_top + jnp.log2(total), weighted / total


def grads_tile(slots, ordk, posq_ref, stats, qr, gr, kva, kvb, dqs, put):
    r0 = slot_start(slots[0])
    q = qr[r0 : r0 + RT, :]
    g = gr[r0 : r0 + RT, :]
    posq = posq_ref[:, r0 : r0 + RT]
    pairs = [combined_stats(stats, d) for d in slots]
    lse = jnp.concatenate([p[0] for p in pairs], axis=1)
    delta = jnp.concatenate([p[1] for p in pairs], axis=1)
    dq = jnp.zeros((RT, HEAD), f32)
    for chunk in range(KEYS // KC):
        kv = kva if chunk * KC < KHALF else kvb
        k0 = chunk * KC % KHALF
        key_rows = kv[k0 : k0 + KC, :HEAD]
        score = masked_scores(key_rows, q, posq, ordk, chunk * (KC // HALF))
        prob = jnp.exp2(score - lse)
        dprob = dot(kv[k0 : k0 + KC, HEAD:], g, NT)
        dscore = (prob * (dprob - delta)).astype(bf16)
        prob_low = prob.astype(bf16)
        put(chunk, dot(dscore, q, NN), dot(prob_low, g, NN))
        dq = dq + dot(dscore, key_rows, TN)
    for i, out in enumerate(dqs):
        for h in range(HEADS):
            rows = dq[i * SLOT + h * ROWS : i * SLOT + (h + 1) * ROWS, :] * SCALE
            out[:, h * HEAD : (h + 1) * HEAD] = rows.astype(out.dtype)


def grads_first(ordk, posq, s0, s1, s2, s3, qr, gr, kva, kvb, dq1, dq2, acc):
    def put(chunk, dk, dv):
        acc[chunk * KC : (chunk + 1) * KC, :HEAD] = dk
        acc[chunk * KC : (chunk + 1) * KC, HEAD:] = dv

    grads_tile((1, 2), ordk, posq, (s0, s1, s2, s3), qr, gr, kva, kvb, (dq1, dq2), put)


def grads_second(ordk, posq, s0, s1, s2, s3, qr, gr, kva, kvb, acc, dq3, dq0, keep, send):
    def put(chunk, dk, dv):
        k0 = chunk * KC % KHALF
        out = keep if chunk * KC < KHALF else send
        before = acc[chunk * KC : (chunk + 1) * KC, :]
        out[k0 : k0 + KC, :HEAD] = ((before[:, :HEAD] + dk) * SCALE).astype(out.dtype)
        out[k0 : k0 + KC, HEAD:] = (before[:, HEAD:] + dv).astype(out.dtype)

    grads_tile((3, 0), ordk, posq, (s0, s1, s2, s3), qr, gr, kva, kvb, (dq3, dq0), put)


def columns_kernel(place_ref, own, other, x0, x1, x2, x3):
    ic = place_ref[1]
    src = lax.broadcasted_iota(jnp.int32, (512, 256), 0)
    dst = lax.broadcasted_iota(jnp.int32, (512, 256), 1)
    home = dst // 32 * 64 + dst % 32 + ic * 32
    pick = jnp.where(src == home, 1.0, 0.0).astype(bf16)
    for d, out in enumerate((x0, x1, x2, x3)):
        base = lax.rem(place_ref[0] + d, N_OUT) * 512
        for t, tok in enumerate((own, other)):
            for p in range(2):
                cols = tok[:, pl.ds(pl.multiple_of(base + p * 2048, 512), 512)]
                out[t, :, p * 256 : (p + 1) * 256] = dot(cols, pick, NN).astype(bf16)


def weights_kernel(x0, x1, x2, x3, q0, q1, q2, q3, k0, k1, k2, k3, grads, out, xr, gr):
    wide = HEADS * HEAD
    for d, x in enumerate((x0, x1, x2, x3)):
        rows = slice(d * ROWS, (d + 1) * ROWS)
        other = slice((N_OUT + d) * ROWS, (N_OUT + d + 1) * ROWS)
        xr[rows, :] = x[0]
        xr[other, :] = x[1]
        gr[rows, :wide] = (q0, q1, q2, q3)[d][...]
        gr[rows, wide:] = (k0, k1, k2, k3)[d][...]
        gr[other, :] = grads[d]
    dw = dot(xr[...], gr[...], TN).astype(bf16)
    for p in range(16):
        out[p] = dw[p * 32 : (p + 1) * 32]


def last_sum(parts, dwq, dwk, dwv):
    total = jnp.sum(parts[...].astype(f32), axis=0)
    wide = HEADS * HEAD
    dwq[...] = total[:, :wide]
    dwk[...] = total[:, wide : wide + HEAD]
    dwv[...] = total[:, wide + HEAD :]


VM = 24
smem = pl.BlockSpec(memory_space=pltpu.SMEM)
vmem = pl.BlockSpec(memory_space=pltpu.VMEM)
params = pltpu.CompilerParams(vmem_limit_bytes=VM * 1024 * 1024)


def cost(pairs, matmuls, size):
    return pl.CostEstimate(
        flops=2 * pairs * HEAD * matmuls, transcendentals=pairs, bytes_accessed=size
    )


def kernel_call(body, name, outs, scratch, estimate, spaces, *args):
    return pl.pallas_call(
        body,
        out_shape=tuple(jax.ShapeDtypeStruct(*o) for o in outs),
        in_specs=spaces + [vmem] * (len(args) - len(spaces)),
        out_specs=tuple(vmem for _ in outs),
        scratch_shapes=[pltpu.VMEM(*s) for s in scratch],
        compiler_params=params,
        cost_estimate=estimate,
        name=name,
    )(*args)


WIDE = HEADS * HEAD


def shift(x, axis, d, n):
    return lax.ppermute(x, axis, [(i, (i + d) % n) for i in range(n)])


def from_behind(x, axis, n):
    return [x] + [shift(x, axis, d, n) for d in range(1, n)]


def per_device(inputs, block_order, w_query, w_key, w_value, grad_out):
    tokens = inputs[0]
    order = block_order[0]
    dout = grad_out[0]
    o, ix, iy, ic = (lax.axis_index(a) for a in ("outer", "x", "yh", "core"))

    query = dot(tokens, w_query, NN).astype(bf16)
    q1, q3 = shift(query, "outer", 1, N_OUT), shift(query, "outer", -1, N_OUT)
    g1, g3 = shift(dout, "outer", 1, N_OUT), shift(dout, "outer", -1, N_OUT)
    qs = [query, q1, shift(q1, "outer", 1, N_OUT), q3]
    gs = [dout, g1, shift(g3, "outer", -1, N_OUT), g3]
    kv = jnp.concatenate(
        [
            dot(tokens, w_key, NN).astype(bf16),
            dot(tokens, w_value, NN).astype(bf16),
        ],
        axis=1,
    )
    kva = jnp.broadcast_to(kv[None], (8,) + kv.shape)
    kva = lax.all_to_all(kva, ("x", "yh"), 0, 0, tiled=True).reshape(KHALF, 2 * HEAD)
    other_tokens = shift(tokens, "core", 1, 2)
    later = tokens
    kva, qs, gs, other_tokens = lax.optimization_barrier((kva, qs, gs, other_tokens))
    kvb = shift(kva, "core", 1, 2)

    key_dev = (o * 8 + np.arange(8)[None, :, None]) * 2 + (ic + np.arange(2)[:, None, None]) % 2
    key_blocks = (key_dev * 2 + np.arange(2)[None, None, :]).reshape(-1)
    query_dev = (((o - np.array([1, 2, 3, 0])) % N_OUT * N_X + ix) * 2 + iy) * 2 + ic
    query_blocks = (query_dev[:, None] * 2 + np.arange(2)[None, :]).reshape(-1)

    def look_up(blocks):
        hit = blocks[:, None] == jnp.arange(order.shape[0], dtype=jnp.int32)[None, :]
        return jnp.sum(jnp.where(hit, order[None, :], 0), axis=1)

    ordk = look_up(key_blocks)
    ordq = look_up(query_blocks).reshape(N_OUT, 1, 2, 1)
    posq = ordq * HALF + jnp.arange(HALF, dtype=jnp.int32)
    posq = jnp.broadcast_to(posq, (N_OUT, HEADS, 2, HALF)).reshape(1, ALL_ROWS)

    pairs = cost(ALL_ROWS * KHALF, 2, 4 << 20)
    row_stats = [((3, ALL_ROWS), f32)]
    rows = ((ALL_ROWS, HEAD), bf16)
    stats, qr, gr = kernel_call(
        stats_own, "stats_own", row_stats + [rows, rows], [], pairs, [smem],
        ordk, posq, *qs, *gs, kva,
    )
    (stats,) = kernel_call(
        stats_other, "stats_other", row_stats, [], pairs, [smem], ordk, posq, qr, gr, kvb, stats
    )
    later, other_tokens, stats = lax.optimization_barrier((later, other_tokens, stats))
    xs = kernel_call(
        columns_kernel, "columns", [((2, ROWS, 512), bf16)] * N_OUT, [],
        cost(ROWS * 4096, 4, 5 << 20), [smem], jnp.stack([o, ic]), later, other_tokens,
    )
    xs = [xs[0]] + [shift(xs[d], "outer", d, N_OUT) for d in range(1, N_OUT)]
    all_stats = from_behind(stats, "outer", N_OUT)

    half = (KHALF, 2 * HEAD)
    low_rows = ((ROWS, WIDE), bf16)
    pairs = cost(RT * KEYS, 5, 8 << 20)
    dq1, dq2, acc = kernel_call(
        grads_first, "grads_first", [low_rows, low_rows, ((KEYS, 2 * HEAD), f32)], [],
        pairs, [smem], ordk, posq, *all_stats, qr, gr, kva, kvb,
    )
    dq1, dq2 = shift(dq1, "outer", -1, N_OUT), shift(dq2, "outer", -2, N_OUT)
    dq3, dq, keep, send = kernel_call(
        grads_second, "grads_second",
        [low_rows, ((ROWS, WIDE), f32), (half, f32), (half, bf16)], [],
        pairs, [smem], ordk, posq, *all_stats, qr, gr, kva, kvb, acc,
    )
    send, dq1, dq2, dq3, xs = lax.optimization_barrier((send, dq1, dq2, dq3, xs))
    got = shift(send, "core", 1, 2)
    dq_parts = [dq1, dq2, shift(dq3, "outer", -3, N_OUT)]
    dkv = (keep + got.astype(f32)).astype(bf16).reshape(8, ROWS, 2 * HEAD)
    dkv = lax.all_to_all(dkv, ("x", "yh"), 0, 0, tiled=True)
    dkv = jnp.sum(dkv.astype(f32), axis=0).astype(bf16)
    dkv_all = from_behind(dkv, "outer", N_OUT)
    for part in dq_parts:
        dq = dq + part.astype(f32)
    dq_all = from_behind(dq.astype(bf16), "outer", N_OUT)
    dq_all, dkv_all = lax.optimization_barrier((dq_all, dkv_all))

    grads = [jnp.concatenate(pair, axis=1) for pair in zip(dq_all, dkv_all)]
    other_grads = shift(jnp.stack(grads), "core", 1, 2)
    (dw,) = kernel_call(
        weights_kernel, "weights", [((16, 32, 768), bf16)],
        [((2 * N_OUT * ROWS, 512), bf16), ((2 * N_OUT * ROWS, 768), bf16)],
        cost(1280 * 512, 6, 4 << 20), [],
        *xs, *dq_all, *dkv_all, other_grads,
    )
    dw = lax.all_to_all(dw, ("dp", "x", "yh"), 0, 0, tiled=True)
    return kernel_call(
        last_sum, "last_sum", [((32, WIDE), f32), ((32, HEAD), f32), ((32, HEAD), f32)], [],
        cost(32 * 16, 3, 1 << 20), [], dw,
    )


def solution(mesh):
    devices = np.asarray(mesh.devices).reshape(2, N_OUT, N_X, 2, 2)
    fine = Mesh(devices, ("dp", "outer", "x", "yh", "core"))
    seq = ("outer", "x", "yh", "core")
    rows = P(("dp",) + seq, None)
    return jax.shard_map(
        per_device,
        mesh=fine,
        in_specs=(
            P("dp", seq, None),
            P("dp", None),
            P(None, None),
            P(None, None),
            P(None, None),
            P("dp", seq, None),
        ),
        out_specs=(rows, rows, rows),
        check_vma=False,
    )
```

```python
import functools
import math

import jax
import jax.numpy as jnp
import numpy as np
from jax import lax
from jax.experimental import pallas as pl
from jax.experimental.pallas import tpu as pltpu
from jax.sharding import Mesh, PartitionSpec as P

masked_fill = -1e30
HEADS = 4
HEAD = 128
ROWS = 160
HALF = 80
N_OUT = 4
N_X = 4
SLOT = HEADS * ROWS
ALL_ROWS = N_OUT * SLOT
KEYS = 16 * ROWS
KHALF = KEYS // 2
RT = 1280
KC = 640
KS = 160
SCALE = 1.0 / math.sqrt(HEAD)
SCALE2 = SCALE * math.log2(math.e)
f32 = jnp.float32
bf16 = jnp.bfloat16
NT = (((1,), (1,)), ((), ()))
NN = (((1,), (0,)), ((), ()))
TN = (((0,), (0,)), ((), ()))


def dot(a, b, dims):
    return lax.dot_general(a, b, dims, preferred_element_type=f32)


def slot_start(d):
    return (d - 1) % N_OUT * SLOT


def fill_rows(pieces, rows_ref):
    for d in range(N_OUT):
        for h in range(HEADS):
            r0 = slot_start(d) + h * ROWS
            rows_ref[r0 : r0 + ROWS, :] = pieces[d][:, h * HEAD : (h + 1) * HEAD]


def masked_scores(key_rows, q, posq, ordk_ref, block):
    score = dot(key_rows, q, NT)
    place = lax.broadcasted_iota(jnp.int32, (HALF, RT), 0)
    parts = []
    for b in range(score.shape[0] // HALF):
        limit = posq - ordk_ref[block + b] * HALF
        part = score[b * HALF : (b + 1) * HALF] * SCALE2
        parts.append(jnp.where(place <= limit, part, masked_fill))
    return jnp.concatenate(parts, axis=0)


def stats_pass(block, ordk_ref, posq_ref, qr, gr, kv, before, out_ref):
    def row_tile(rt, _):
        r0 = pl.multiple_of(rt * RT, RT)
        q = qr[pl.ds(r0, RT), :]
        g = gr[pl.ds(r0, RT), :]
        posq = posq_ref[:, pl.ds(r0, RT)]
        top = jnp.full((8, RT), masked_fill, f32)
        total = jnp.zeros((8, RT), f32)
        weighted = jnp.zeros((8, RT), f32)
        for k0 in range(0, KHALF, KS):
            score = masked_scores(kv[k0 : k0 + KS, :HEAD], q, posq, ordk_ref, block + k0 // HALF)
            dprob = dot(kv[k0 : k0 + KS, HEAD:], g, NT)
            score = score.reshape(KS // 8, 8, RT)
            new_top = jnp.maximum(top, jnp.max(score, axis=0))
            weights = jnp.exp2(score - new_top[None])
            factor = jnp.exp2(top - new_top)
            total = total * factor + jnp.sum(weights, axis=0)
            weighted = weighted * factor + jnp.sum(weights * dprob.reshape(KS // 8, 8, RT), axis=0)
            top = new_top
        row_top = jnp.max(top, axis=0, keepdims=True)
        if before is not None:
            row_top = jnp.maximum(row_top, before[0:1, pl.ds(r0, RT)])
        factor = jnp.exp2(top - row_top)
        total = jnp.sum(total * factor, axis=0, keepdims=True)
        weighted = jnp.sum(weighted * factor, axis=0, keepdims=True)
        if before is not None:
            factor = jnp.exp2(before[0:1, pl.ds(r0, RT)] - row_top)
            total = total + before[1:2, pl.ds(r0, RT)] * factor
            weighted = weighted + before[2:3, pl.ds(r0, RT)] * factor
        out_ref[0:1, pl.ds(r0, RT)] = row_top
        out_ref[1:2, pl.ds(r0, RT)] = total
        out_ref[2:3, pl.ds(r0, RT)] = weighted
        return 0

    lax.fori_loop(0, ALL_ROWS // RT, row_tile, 0)


def stats_own(ordk, posq, q0, q1, q2, q3, g0, g1, g2, g3, kva, out, qr, gr):
    fill_rows((q0, q1, q2, q3), qr)
    fill_rows((g0, g1, g2, g3), gr)
    stats_pass(0, ordk, posq, qr, gr, kva, None, out)


def stats_other(ordk, posq, qr, gr, kvb, before, out):
    stats_pass(KHALF // HALF, ordk, posq, qr, gr, kvb, before, out)


def combine_stats(stats, rowstat_ref):
    for d in range(N_OUT):
        parts = []
        for e in range(N_OUT):
            c0 = slot_start(d - e)
            parts.append(stats[e][:, c0 : c0 + SLOT])
        row_top = parts[0][0:1]
        for part in parts[1:]:
            row_top = jnp.maximum(row_top, part[0:1])
        total = jnp.zeros_like(row_top)
        weighted = jnp.zeros_like(row_top)
        for part in parts:
            factor = jnp.exp2(part[0:1] - row_top)
            total = total + part[1:2] * factor
            weighted = weighted + part[2:3] * factor
        r0 = slot_start(d)
        rowstat_ref[0:1, r0 : r0 + SLOT] = row_top + jnp.log2(total)
        rowstat_ref[1:2, r0 : r0 + SLOT] = weighted / total


def grads_kernel(
    ordk, posq_ref, s0, s1, s2, s3, qr, gr, kva, kvb,
    dq0, dq1, dq2, dq3, keep, send, rowstat, dqr, dkv,
):
    combine_stats((s0, s1, s2, s3), rowstat)
    dkv[...] = jnp.zeros_like(dkv)

    def row_tile(rt, _):
        r0 = pl.multiple_of(rt * RT, RT)
        q = qr[pl.ds(r0, RT), :]
        g = gr[pl.ds(r0, RT), :]
        posq = posq_ref[:, pl.ds(r0, RT)]
        lse = rowstat[0:1, pl.ds(r0, RT)]
        delta = rowstat[1:2, pl.ds(r0, RT)]
        dq = jnp.zeros((RT, HEAD), f32)
        for chunk in range(KEYS // KC):
            kv = kva if chunk * KC < KHALF else kvb
            k0 = chunk * KC % KHALF
            key_rows = kv[k0 : k0 + KC, :HEAD]
            score = masked_scores(key_rows, q, posq, ordk, chunk * (KC // HALF))
            prob = jnp.exp2(score - lse)
            dprob = dot(kv[k0 : k0 + KC, HEAD:], g, NT)
            dscore = (prob * (dprob - delta)).astype(bf16)
            prob_low = prob.astype(bf16)
            dkv[chunk * KC : (chunk + 1) * KC, HEAD:] += dot(prob_low, g, NN)
            dkv[chunk * KC : (chunk + 1) * KC, :HEAD] += dot(dscore, q, NN)
            dq = dq + dot(dscore, key_rows, TN)
        dqr[pl.ds(r0, RT), :] = dq
        return 0

    lax.fori_loop(0, ALL_ROWS // RT, row_tile, 0)
    for d, out in enumerate((dq0, dq1, dq2, dq3)):
        for h in range(HEADS):
            r0 = slot_start(d) + h * ROWS
            out[:, h * HEAD : (h + 1) * HEAD] = (dqr[r0 : r0 + ROWS, :] * SCALE).astype(out.dtype)
    for out, k0 in ((keep, 0), (send, KHALF)):
        out[:, :HEAD] = (dkv[k0 : k0 + KHALF, :HEAD] * SCALE).astype(out.dtype)
        out[:, HEAD:] = dkv[k0 : k0 + KHALF, HEAD:].astype(out.dtype)


def columns_kernel(place_ref, own, other, x0, x1, x2, x3):
    ic = place_ref[1]
    src = lax.broadcasted_iota(jnp.int32, (512, 256), 0)
    dst = lax.broadcasted_iota(jnp.int32, (512, 256), 1)
    home = dst // 32 * 64 + dst % 32 + ic * 32
    pick = jnp.where(src == home, 1.0, 0.0).astype(bf16)
    for d, out in enumerate((x0, x1, x2, x3)):
        base = lax.rem(place_ref[0] + d, N_OUT) * 512
        for t, tok in enumerate((own, other)):
            for p in range(2):
                cols = tok[:, pl.ds(pl.multiple_of(base + p * 2048, 512), 512)]
                out[t, :, p * 256 : (p + 1) * 256] = dot(cols, pick, NN).astype(bf16)


def weights_kernel(x0, x1, x2, x3, q0, q1, q2, q3, k0, k1, k2, k3, grads, out, xr, gr):
    wide = HEADS * HEAD
    for d, x in enumerate((x0, x1, x2, x3)):
        rows = slice(d * ROWS, (d + 1) * ROWS)
        other = slice((N_OUT + d) * ROWS, (N_OUT + d + 1) * ROWS)
        xr[rows, :] = x[0]
        xr[other, :] = x[1]
        gr[rows, :wide] = (q0, q1, q2, q3)[d][...]
        gr[rows, wide:] = (k0, k1, k2, k3)[d][...]
        gr[other, :] = grads[d]
    dw = dot(xr[...], gr[...], TN).astype(bf16)
    for p in range(16):
        out[p] = dw[p * 32 : (p + 1) * 32]


def last_sum(parts, dwq, dwk, dwv):
    total = jnp.sum(parts[...].astype(f32), axis=0)
    wide = HEADS * HEAD
    dwq[...] = total[:, :wide]
    dwk[...] = total[:, wide : wide + HEAD]
    dwv[...] = total[:, wide + HEAD :]


VM = 24
smem = pl.BlockSpec(memory_space=pltpu.SMEM)
vmem = pl.BlockSpec(memory_space=pltpu.VMEM)
params = pltpu.CompilerParams(vmem_limit_bytes=VM * 1024 * 1024)


def cost(pairs, matmuls, size):
    return pl.CostEstimate(
        flops=2 * pairs * HEAD * matmuls, transcendentals=pairs, bytes_accessed=size
    )


def kernel_call(body, name, outs, scratch, estimate, spaces, *args):
    return pl.pallas_call(
        body,
        out_shape=tuple(jax.ShapeDtypeStruct(*o) for o in outs),
        in_specs=spaces + [vmem] * (len(args) - len(spaces)),
        out_specs=tuple(vmem for _ in outs),
        scratch_shapes=[pltpu.VMEM(*s) for s in scratch],
        compiler_params=params,
        cost_estimate=estimate,
        name=name,
    )(*args)


WIDE = HEADS * HEAD
acc_rows = ((ALL_ROWS, HEAD), f32)


def shift(x, axis, d, n):
    return lax.ppermute(x, axis, [(i, (i + d) % n) for i in range(n)])


def from_behind(x, axis, n):
    return [x] + [shift(x, axis, d, n) for d in range(1, n)]


def per_device(inputs, block_order, w_query, w_key, w_value, grad_out):
    tokens = inputs[0]
    order = block_order[0]
    dout = grad_out[0]
    o, ix, iy, ic = (lax.axis_index(a) for a in ("outer", "x", "yh", "core"))

    query = dot(tokens, w_query, NN).astype(bf16)
    q1, q3 = shift(query, "outer", 1, N_OUT), shift(query, "outer", -1, N_OUT)
    g1, g3 = shift(dout, "outer", 1, N_OUT), shift(dout, "outer", -1, N_OUT)
    qs = [query, q1, shift(q1, "outer", 1, N_OUT), q3]
    gs = [dout, g1, shift(g3, "outer", -1, N_OUT), g3]
    kv = jnp.concatenate(
        [
            dot(tokens, w_key, NN).astype(bf16),
            dot(tokens, w_value, NN).astype(bf16),
        ],
        axis=1,
    )
    other_tokens = shift(tokens, "core", 1, 2)
    later = tokens
    kva = jnp.broadcast_to(kv[None], (8,) + kv.shape)
    kva, other_tokens = lax.optimization_barrier((kva, other_tokens))
    kva = lax.all_to_all(kva, ("x", "yh"), 0, 0, tiled=True).reshape(KHALF, 2 * HEAD)
    kva, qs, gs = lax.optimization_barrier((kva, qs, gs))
    kvb = shift(kva, "core", 1, 2)

    key_dev = (o * 8 + np.arange(8)[None, :, None]) * 2 + (ic + np.arange(2)[:, None, None]) % 2
    key_blocks = (key_dev * 2 + np.arange(2)[None, None, :]).reshape(-1)
    query_dev = (((o - np.array([1, 2, 3, 0])) % N_OUT * N_X + ix) * 2 + iy) * 2 + ic
    query_blocks = (query_dev[:, None] * 2 + np.arange(2)[None, :]).reshape(-1)

    def look_up(blocks):
        hit = blocks[:, None] == jnp.arange(order.shape[0], dtype=jnp.int32)[None, :]
        return jnp.sum(jnp.where(hit, order[None, :], 0), axis=1)

    ordk = look_up(key_blocks)
    ordq = look_up(query_blocks).reshape(N_OUT, 1, 2, 1)
    posq = ordq * HALF + jnp.arange(HALF, dtype=jnp.int32)
    posq = jnp.broadcast_to(posq, (N_OUT, HEADS, 2, HALF)).reshape(1, ALL_ROWS)

    pairs = cost(ALL_ROWS * KHALF, 2, 4 << 20)
    row_stats = [((3, ALL_ROWS), f32)]
    rows = ((ALL_ROWS, HEAD), bf16)
    stats, qr, gr = kernel_call(
        stats_own, "stats_own", row_stats + [rows, rows], [], pairs, [smem],
        ordk, posq, *qs, *gs, kva,
    )
    (stats,) = kernel_call(
        stats_other, "stats_other", row_stats, [], pairs, [smem], ordk, posq, qr, gr, kvb, stats
    )
    later, other_tokens, stats = lax.optimization_barrier((later, other_tokens, stats))
    xs = kernel_call(
        columns_kernel, "columns", [((2, ROWS, 512), bf16)] * N_OUT, [],
        cost(ROWS * 4096, 4, 5 << 20), [smem], jnp.stack([o, ic]), later, other_tokens,
    )
    xs = [xs[0]] + [shift(xs[d], "outer", d, N_OUT) for d in range(1, N_OUT)]
    all_stats = from_behind(stats, "outer", N_OUT)

    half = (KHALF, 2 * HEAD)
    dq, dq1, dq2, dq3, keep, send = kernel_call(
        grads_kernel, "grads",
        [((ROWS, WIDE), f32)] + [((ROWS, WIDE), bf16)] * 3 + [(half, f32), (half, bf16)],
        [((2, ALL_ROWS), f32), acc_rows, ((KEYS, 2 * HEAD), f32)],
        cost(ALL_ROWS * KEYS, 5, 8 << 20), [smem], ordk, posq, *all_stats, qr, gr, kva, kvb,
    )
    send, dq1, dq2, dq3, xs = lax.optimization_barrier((send, dq1, dq2, dq3, xs))
    got = shift(send, "core", 1, 2)
    dq_parts = [shift(part, "outer", -d, N_OUT) for d, part in ((1, dq1), (2, dq2), (3, dq3))]
    dkv = (keep + got.astype(f32)).astype(bf16).reshape(8, ROWS, 2 * HEAD)
    dkv = lax.all_to_all(dkv, ("x", "yh"), 0, 0, tiled=True)
    dkv = jnp.sum(dkv.astype(f32), axis=0).astype(bf16)
    dkv_all = from_behind(dkv, "outer", N_OUT)
    for part in dq_parts:
        dq = dq + part.astype(f32)
    dq_all = from_behind(dq.astype(bf16), "outer", N_OUT)
    dq_all, dkv_all = lax.optimization_barrier((dq_all, dkv_all))

    grads = [jnp.concatenate(pair, axis=1) for pair in zip(dq_all, dkv_all)]
    other_grads = shift(jnp.stack(grads), "core", 1, 2)
    (dw,) = kernel_call(
        weights_kernel, "weights", [((16, 32, 768), bf16)],
        [((2 * N_OUT * ROWS, 512), bf16), ((2 * N_OUT * ROWS, 768), bf16)],
        cost(1280 * 512, 6, 4 << 20), [],
        *xs, *dq_all, *dkv_all, other_grads,
    )
    dw = lax.all_to_all(dw, ("dp", "x", "yh"), 0, 0, tiled=True)
    return kernel_call(
        last_sum, "last_sum", [((32, WIDE), f32), ((32, HEAD), f32), ((32, HEAD), f32)], [],
        cost(32 * 16, 3, 1 << 20), [], dw,
    )


def solution(mesh):
    devices = np.asarray(mesh.devices).reshape(2, N_OUT, N_X, 2, 2)
    fine = Mesh(devices, ("dp", "outer", "x", "yh", "core"))
    seq = ("outer", "x", "yh", "core")
    rows = P(("dp",) + seq, None)
    return jax.shard_map(
        per_device,
        mesh=fine,
        in_specs=(
            P("dp", seq, None),
            P("dp", None),
            P(None, None),
            P(None, None),
            P(None, None),
            P("dp", seq, None),
        ),
        out_specs=(rows, rows, rows),
        check_vma=False,
    )
```

```python
import functools
import math

import jax
import jax.numpy as jnp
import numpy as np
from jax import lax
from jax.experimental import pallas as pl
from jax.experimental.pallas import tpu as pltpu
from jax.sharding import Mesh, PartitionSpec as P

masked_fill = -1e30
HEADS = 4
HEAD = 128
ROWS = 160
HALF = 80
N_OUT = 4
N_X = 4
SLOT = HEADS * ROWS
ALL_ROWS = N_OUT * SLOT
KEYS = 16 * ROWS
KHALF = KEYS // 2
RT = 1280
KC = 640
KS = 160
SCALE = 1.0 / math.sqrt(HEAD)
SCALE2 = SCALE * math.log2(math.e)
f32 = jnp.float32
bf16 = jnp.bfloat16
NT = (((1,), (1,)), ((), ()))
NN = (((1,), (0,)), ((), ()))
TN = (((0,), (0,)), ((), ()))


def dot(a, b, dims):
    return lax.dot_general(a, b, dims, preferred_element_type=f32)


def slot_start(d):
    return (d - 1) % N_OUT * SLOT


def fill_rows(pieces, rows_ref):
    for d in range(N_OUT):
        for h in range(HEADS):
            r0 = slot_start(d) + h * ROWS
            rows_ref[r0 : r0 + ROWS, :] = pieces[d][:, h * HEAD : (h + 1) * HEAD]


def masked_scores(key_rows, q, posq, ordk_ref, block):
    score = dot(key_rows, q, NT)
    place = lax.broadcasted_iota(jnp.int32, (HALF, RT), 0)
    parts = []
    for b in range(score.shape[0] // HALF):
        limit = posq - ordk_ref[block + b] * HALF
        part = score[b * HALF : (b + 1) * HALF] * SCALE2
        parts.append(jnp.where(place <= limit, part, masked_fill))
    return jnp.concatenate(parts, axis=0)


def stats_pass(block, ordk_ref, posq_ref, qr, gr, kv, before, out_ref):
    def row_tile(rt, _):
        r0 = pl.multiple_of(rt * RT, RT)
        q = qr[pl.ds(r0, RT), :]
        g = gr[pl.ds(r0, RT), :]
        posq = posq_ref[:, pl.ds(r0, RT)]
        top = jnp.full((8, RT), masked_fill, f32)
        total = jnp.zeros((8, RT), f32)
        weighted = jnp.zeros((8, RT), f32)
        for k0 in range(0, KHALF, KS):
            score = masked_scores(kv[k0 : k0 + KS, :HEAD], q, posq, ordk_ref, block + k0 // HALF)
            dprob = dot(kv[k0 : k0 + KS, HEAD:], g, NT)
            score = score.reshape(KS // 8, 8, RT)
            new_top = jnp.maximum(top, jnp.max(score, axis=0))
            weights = jnp.exp2(score - new_top[None])
            factor = jnp.exp2(top - new_top)
            total = total * factor + jnp.sum(weights, axis=0)
            weighted = weighted * factor + jnp.sum(weights * dprob.reshape(KS // 8, 8, RT), axis=0)
            top = new_top
        row_top = jnp.max(top, axis=0, keepdims=True)
        if before is not None:
            row_top = jnp.maximum(row_top, before[0:1, pl.ds(r0, RT)])
        factor = jnp.exp2(top - row_top)
        total = jnp.sum(total * factor, axis=0, keepdims=True)
        weighted = jnp.sum(weighted * factor, axis=0, keepdims=True)
        if before is not None:
            factor = jnp.exp2(before[0:1, pl.ds(r0, RT)] - row_top)
            total = total + before[1:2, pl.ds(r0, RT)] * factor
            weighted = weighted + before[2:3, pl.ds(r0, RT)] * factor
        out_ref[0:1, pl.ds(r0, RT)] = row_top
        out_ref[1:2, pl.ds(r0, RT)] = total
        out_ref[2:3, pl.ds(r0, RT)] = weighted
        return 0

    lax.fori_loop(0, ALL_ROWS // RT, row_tile, 0)


def stats_own(ordk, posq, q0, q1, q2, q3, g0, g1, g2, g3, kva, out, qr, gr):
    fill_rows((q0, q1, q2, q3), qr)
    fill_rows((g0, g1, g2, g3), gr)
    stats_pass(0, ordk, posq, qr, gr, kva, None, out)


def stats_other(ordk, posq, qr, gr, kvb, before, out):
    stats_pass(KHALF // HALF, ordk, posq, qr, gr, kvb, before, out)


def combine_stats(stats, rowstat_ref):
    for d in range(N_OUT):
        parts = []
        for e in range(N_OUT):
            c0 = slot_start(d - e)
            parts.append(stats[e][:, c0 : c0 + SLOT])
        row_top = parts[0][0:1]
        for part in parts[1:]:
            row_top = jnp.maximum(row_top, part[0:1])
        total = jnp.zeros_like(row_top)
        weighted = jnp.zeros_like(row_top)
        for part in parts:
            factor = jnp.exp2(part[0:1] - row_top)
            total = total + part[1:2] * factor
            weighted = weighted + part[2:3] * factor
        r0 = slot_start(d)
        rowstat_ref[0:1, r0 : r0 + SLOT] = row_top + jnp.log2(total)
        rowstat_ref[1:2, r0 : r0 + SLOT] = weighted / total


def grads_kernel(
    ordk, posq_ref, s0, s1, s2, s3, qr, gr, kva, kvb,
    dq0, dq1, dq2, dq3, keep, send, rowstat, dqr, dkv,
):
    combine_stats((s0, s1, s2, s3), rowstat)
    dkv[...] = jnp.zeros_like(dkv)

    def row_tile(rt, _):
        r0 = pl.multiple_of(rt * RT, RT)
        q = qr[pl.ds(r0, RT), :]
        g = gr[pl.ds(r0, RT), :]
        posq = posq_ref[:, pl.ds(r0, RT)]
        lse = rowstat[0:1, pl.ds(r0, RT)]
        delta = rowstat[1:2, pl.ds(r0, RT)]
        dq = jnp.zeros((RT, HEAD), f32)
        for chunk in range(KEYS // KC):
            kv = kva if chunk * KC < KHALF else kvb
            k0 = chunk * KC % KHALF
            key_rows = kv[k0 : k0 + KC, :HEAD]
            score = masked_scores(key_rows, q, posq, ordk, chunk * (KC // HALF))
            prob = jnp.exp2(score - lse)
            dprob = dot(kv[k0 : k0 + KC, HEAD:], g, NT)
            dscore = (prob * (dprob - delta)).astype(bf16)
            prob_low = prob.astype(bf16)
            dkv[chunk * KC : (chunk + 1) * KC, HEAD:] += dot(prob_low, g, NN)
            dkv[chunk * KC : (chunk + 1) * KC, :HEAD] += dot(dscore, q, NN)
            dq = dq + dot(dscore, key_rows, TN)
        dqr[pl.ds(r0, RT), :] = dq
        return 0

    lax.fori_loop(0, ALL_ROWS // RT, row_tile, 0)
    for d, out in enumerate((dq0, dq1, dq2, dq3)):
        for h in range(HEADS):
            r0 = slot_start(d) + h * ROWS
            out[:, h * HEAD : (h + 1) * HEAD] = (dqr[r0 : r0 + ROWS, :] * SCALE).astype(out.dtype)
    for out, k0 in ((keep, 0), (send, KHALF)):
        out[:, :HEAD] = (dkv[k0 : k0 + KHALF, :HEAD] * SCALE).astype(out.dtype)
        out[:, HEAD:] = dkv[k0 : k0 + KHALF, HEAD:].astype(out.dtype)


def columns_kernel(place_ref, own, other, x0, x1, x2, x3):
    ic = place_ref[1]
    src = lax.broadcasted_iota(jnp.int32, (512, 256), 0)
    dst = lax.broadcasted_iota(jnp.int32, (512, 256), 1)
    home = dst // 32 * 64 + dst % 32 + ic * 32
    pick = jnp.where(src == home, 1.0, 0.0).astype(bf16)
    for d, out in enumerate((x0, x1, x2, x3)):
        base = lax.rem(place_ref[0] + d, N_OUT) * 512
        for t, tok in enumerate((own, other)):
            for p in range(2):
                cols = tok[:, pl.ds(pl.multiple_of(base + p * 2048, 512), 512)]
                out[t, :, p * 256 : (p + 1) * 256] = dot(cols, pick, NN).astype(bf16)


def weights_kernel(x0, x1, x2, x3, q0, q1, q2, q3, k0, k1, k2, k3, grads, out, xr, gr):
    wide = HEADS * HEAD
    for d, x in enumerate((x0, x1, x2, x3)):
        rows = slice(d * ROWS, (d + 1) * ROWS)
        other = slice((N_OUT + d) * ROWS, (N_OUT + d + 1) * ROWS)
        xr[rows, :] = x[0]
        xr[other, :] = x[1]
        gr[rows, :wide] = (q0, q1, q2, q3)[d][...]
        gr[rows, wide:] = (k0, k1, k2, k3)[d][...]
        gr[other, :] = grads[d]
    dw = dot(xr[...], gr[...], TN).astype(bf16)
    for p in range(16):
        out[p] = dw[p * 32 : (p + 1) * 32]


def last_sum(parts, dwq, dwk, dwv):
    total = jnp.sum(parts[...].astype(f32), axis=0)
    wide = HEADS * HEAD
    dwq[...] = total[:, :wide]
    dwk[...] = total[:, wide : wide + HEAD]
    dwv[...] = total[:, wide + HEAD :]


def project_kernel(tok, wq, wk, wv, query, kv, acc):
    step = pl.program_id(0)

    @pl.when(step == 0)
    def _():
        acc[...] = jnp.zeros_like(acc)

    wide = HEADS * HEAD
    for out, w in ((slice(0, wide), wq), (slice(wide, wide + HEAD), wk), (slice(wide + HEAD, wide + 2 * HEAD), wv)):
        acc[:, out] += dot(tok[...], w[...], NN)

    @pl.when(step == pl.num_programs(0) - 1)
    def _():
        query[...] = acc[:, :wide].astype(bf16)
        for i in range(8):
            kv[i] = acc[:, wide:].astype(bf16)


VM = 24
smem = pl.BlockSpec(memory_space=pltpu.SMEM)
vmem = pl.BlockSpec(memory_space=pltpu.VMEM)
params = pltpu.CompilerParams(vmem_limit_bytes=VM * 1024 * 1024)


def cost(pairs, matmuls, size):
    return pl.CostEstimate(
        flops=2 * pairs * HEAD * matmuls, transcendentals=pairs, bytes_accessed=size
    )


def kernel_call(body, name, outs, scratch, estimate, spaces, *args):
    return pl.pallas_call(
        body,
        out_shape=tuple(jax.ShapeDtypeStruct(*o) for o in outs),
        in_specs=spaces + [vmem] * (len(args) - len(spaces)),
        out_specs=tuple(vmem for _ in outs),
        scratch_shapes=[pltpu.VMEM(*s) for s in scratch],
        compiler_params=params,
        cost_estimate=estimate,
        name=name,
    )(*args)


WIDE = HEADS * HEAD
acc_rows = ((ALL_ROWS, HEAD), f32)


def project_call(tokens, w_query, w_key, w_value):
    depth = 1024
    return pl.pallas_call(
        project_kernel,
        grid=(tokens.shape[1] // depth,),
        out_shape=(
            jax.ShapeDtypeStruct((ROWS, WIDE), bf16),
            jax.ShapeDtypeStruct((8, ROWS, 2 * HEAD), bf16),
        ),
        in_specs=[
            pl.BlockSpec((ROWS, depth), lambda i: (0, i)),
            pl.BlockSpec((depth, WIDE), lambda i: (i, 0)),
            pl.BlockSpec((depth, HEAD), lambda i: (i, 0)),
            pl.BlockSpec((depth, HEAD), lambda i: (i, 0)),
        ],
        out_specs=(
            pl.BlockSpec((ROWS, WIDE), lambda i: (0, 0)),
            pl.BlockSpec((8, ROWS, 2 * HEAD), lambda i: (0, 0, 0)),
        ),
        scratch_shapes=[pltpu.VMEM((ROWS, WIDE + 2 * HEAD), f32)],
        compiler_params=params,
        cost_estimate=cost(ROWS * 4096, 6, 8 << 20),
        name="project",
    )(tokens, w_query, w_key, w_value)


def shift(x, axis, d, n):
    return lax.ppermute(x, axis, [(i, (i + d) % n) for i in range(n)])


def from_behind(x, axis, n):
    return [x] + [shift(x, axis, d, n) for d in range(1, n)]


def per_device(inputs, block_order, w_query, w_key, w_value, grad_out):
    tokens = inputs[0]
    order = block_order[0]
    dout = grad_out[0]
    o, ix, iy, ic = (lax.axis_index(a) for a in ("outer", "x", "yh", "core"))

    query, kva = project_call(tokens, w_query, w_key, w_value)
    q1, q3 = shift(query, "outer", 1, N_OUT), shift(query, "outer", -1, N_OUT)
    g1, g3 = shift(dout, "outer", 1, N_OUT), shift(dout, "outer", -1, N_OUT)
    qs = [query, q1, shift(q1, "outer", 1, N_OUT), q3]
    gs = [dout, g1, shift(g3, "outer", -1, N_OUT), g3]
    kva = lax.all_to_all(kva, ("x", "yh"), 0, 0, tiled=True).reshape(KHALF, 2 * HEAD)
    other_tokens = shift(tokens, "core", 1, 2)
    later = tokens
    kva, qs, gs, other_tokens = lax.optimization_barrier((kva, qs, gs, other_tokens))
    kvb = shift(kva, "core", 1, 2)

    key_dev = (o * 8 + np.arange(8)[None, :, None]) * 2 + (ic + np.arange(2)[:, None, None]) % 2
    key_blocks = (key_dev * 2 + np.arange(2)[None, None, :]).reshape(-1)
    query_dev = (((o - np.array([1, 2, 3, 0])) % N_OUT * N_X + ix) * 2 + iy) * 2 + ic
    query_blocks = (query_dev[:, None] * 2 + np.arange(2)[None, :]).reshape(-1)

    def look_up(blocks):
        hit = blocks[:, None] == jnp.arange(order.shape[0], dtype=jnp.int32)[None, :]
        return jnp.sum(jnp.where(hit, order[None, :], 0), axis=1)

    ordk = look_up(key_blocks)
    ordq = look_up(query_blocks).reshape(N_OUT, 1, 2, 1)
    posq = ordq * HALF + jnp.arange(HALF, dtype=jnp.int32)
    posq = jnp.broadcast_to(posq, (N_OUT, HEADS, 2, HALF)).reshape(1, ALL_ROWS)

    pairs = cost(ALL_ROWS * KHALF, 2, 4 << 20)
    row_stats = [((3, ALL_ROWS), f32)]
    rows = ((ALL_ROWS, HEAD), bf16)
    stats, qr, gr = kernel_call(
        stats_own, "stats_own", row_stats + [rows, rows], [], pairs, [smem],
        ordk, posq, *qs, *gs, kva,
    )
    (stats,) = kernel_call(
        stats_other, "stats_other", row_stats, [], pairs, [smem], ordk, posq, qr, gr, kvb, stats
    )
    later, other_tokens, stats = lax.optimization_barrier((later, other_tokens, stats))
    xs = kernel_call(
        columns_kernel, "columns", [((2, ROWS, 512), bf16)] * N_OUT, [],
        cost(ROWS * 4096, 4, 5 << 20), [smem], jnp.stack([o, ic]), later, other_tokens,
    )
    xs = [xs[0]] + [shift(xs[d], "outer", d, N_OUT) for d in range(1, N_OUT)]
    all_stats = from_behind(stats, "outer", N_OUT)

    half = (KHALF, 2 * HEAD)
    dq, dq1, dq2, dq3, keep, send = kernel_call(
        grads_kernel, "grads",
        [((ROWS, WIDE), f32)] + [((ROWS, WIDE), bf16)] * 3 + [(half, f32), (half, bf16)],
        [((2, ALL_ROWS), f32), acc_rows, ((KEYS, 2 * HEAD), f32)],
        cost(ALL_ROWS * KEYS, 5, 8 << 20), [smem], ordk, posq, *all_stats, qr, gr, kva, kvb,
    )
    send, dq1, dq2, dq3, xs = lax.optimization_barrier((send, dq1, dq2, dq3, xs))
    got = shift(send, "core", 1, 2)
    dq_parts = [shift(part, "outer", -d, N_OUT) for d, part in ((1, dq1), (2, dq2), (3, dq3))]
    dkv = (keep + got.astype(f32)).astype(bf16).reshape(8, ROWS, 2 * HEAD)
    dkv = lax.all_to_all(dkv, ("x", "yh"), 0, 0, tiled=True)
    dkv = jnp.sum(dkv.astype(f32), axis=0).astype(bf16)
    dkv_all = from_behind(dkv, "outer", N_OUT)
    for part in dq_parts:
        dq = dq + part.astype(f32)
    dq_all = from_behind(dq.astype(bf16), "outer", N_OUT)
    dq_all, dkv_all = lax.optimization_barrier((dq_all, dkv_all))

    grads = [jnp.concatenate(pair, axis=1) for pair in zip(dq_all, dkv_all)]
    other_grads = shift(jnp.stack(grads), "core", 1, 2)
    (dw,) = kernel_call(
        weights_kernel, "weights", [((16, 32, 768), bf16)],
        [((2 * N_OUT * ROWS, 512), bf16), ((2 * N_OUT * ROWS, 768), bf16)],
        cost(1280 * 512, 6, 4 << 20), [],
        *xs, *dq_all, *dkv_all, other_grads,
    )
    dw = lax.all_to_all(dw, ("dp", "x", "yh"), 0, 0, tiled=True)
    return kernel_call(
        last_sum, "last_sum", [((32, WIDE), f32), ((32, HEAD), f32), ((32, HEAD), f32)], [],
        cost(32 * 16, 3, 1 << 20), [], dw,
    )


def solution(mesh):
    devices = np.asarray(mesh.devices).reshape(2, N_OUT, N_X, 2, 2)
    fine = Mesh(devices, ("dp", "outer", "x", "yh", "core"))
    seq = ("outer", "x", "yh", "core")
    rows = P(("dp",) + seq, None)
    return jax.shard_map(
        per_device,
        mesh=fine,
        in_specs=(
            P("dp", seq, None),
            P("dp", None),
            P(None, None),
            P(None, None),
            P(None, None),
            P("dp", seq, None),
        ),
        out_specs=(rows, rows, rows),
        check_vma=False,
    )
```

```python
import functools
import math

import jax
import jax.numpy as jnp
import numpy as np
from jax import lax
from jax.experimental import pallas as pl
from jax.experimental.pallas import tpu as pltpu
from jax.sharding import Mesh, PartitionSpec as P

masked_fill = -1e30
HEADS = 4
HEAD = 128
ROWS = 160
HALF = 80
N_OUT = 4
N_X = 4
SLOT = HEADS * ROWS
ALL_ROWS = N_OUT * SLOT
KEYS = 16 * ROWS
KHALF = KEYS // 2
RT = 1280
KC = 640
KS = 160
SCALE = 1.0 / math.sqrt(HEAD)
SCALE2 = SCALE * math.log2(math.e)
f32 = jnp.float32
bf16 = jnp.bfloat16
NT = (((1,), (1,)), ((), ()))
NN = (((1,), (0,)), ((), ()))
TN = (((0,), (0,)), ((), ()))


def dot(a, b, dims):
    return lax.dot_general(a, b, dims, preferred_element_type=f32)


def slot_start(d):
    return (d - 1) % N_OUT * SLOT


def fill_rows(pieces, rows_ref):
    for d in range(N_OUT):
        for h in range(HEADS):
            r0 = slot_start(d) + h * ROWS
            rows_ref[r0 : r0 + ROWS, :] = pieces[d][:, h * HEAD : (h + 1) * HEAD]


def masked_scores(key_rows, q, posq, ordk_ref, block):
    score = dot(key_rows, q, NT)
    place = lax.broadcasted_iota(jnp.int32, (HALF, RT), 0)
    parts = []
    for b in range(score.shape[0] // HALF):
        limit = posq - ordk_ref[block + b] * HALF
        part = score[b * HALF : (b + 1) * HALF] * SCALE2
        parts.append(jnp.where(place <= limit, part, masked_fill))
    return jnp.concatenate(parts, axis=0)


def stats_pass(block, ordk_ref, posq_ref, qr, gr, kv, before, out_ref):
    def row_tile(rt, _):
        r0 = pl.multiple_of(rt * RT, RT)
        q = qr[pl.ds(r0, RT), :]
        g = gr[pl.ds(r0, RT), :]
        posq = posq_ref[:, pl.ds(r0, RT)]
        top = jnp.full((8, RT), masked_fill, f32)
        total = jnp.zeros((8, RT), f32)
        weighted = jnp.zeros((8, RT), f32)
        for k0 in range(0, KHALF, KS):
            score = masked_scores(kv[k0 : k0 + KS, :HEAD], q, posq, ordk_ref, block + k0 // HALF)
            dprob = dot(kv[k0 : k0 + KS, HEAD:], g, NT)
            score = score.reshape(KS // 8, 8, RT)
            new_top = jnp.maximum(top, jnp.max(score, axis=0))
            weights = jnp.exp2(score - new_top[None])
            factor = jnp.exp2(top - new_top)
            total = total * factor + jnp.sum(weights, axis=0)
            weighted = weighted * factor + jnp.sum(weights * dprob.reshape(KS // 8, 8, RT), axis=0)
            top = new_top
        row_top = jnp.max(top, axis=0, keepdims=True)
        if before is not None:
            row_top = jnp.maximum(row_top, before[0:1, pl.ds(r0, RT)])
        factor = jnp.exp2(top - row_top)
        total = jnp.sum(total * factor, axis=0, keepdims=True)
        weighted = jnp.sum(weighted * factor, axis=0, keepdims=True)
        if before is not None:
            factor = jnp.exp2(before[0:1, pl.ds(r0, RT)] - row_top)
            total = total + before[1:2, pl.ds(r0, RT)] * factor
            weighted = weighted + before[2:3, pl.ds(r0, RT)] * factor
        out_ref[0:1, pl.ds(r0, RT)] = row_top
        out_ref[1:2, pl.ds(r0, RT)] = total
        out_ref[2:3, pl.ds(r0, RT)] = weighted
        return 0

    lax.fori_loop(0, ALL_ROWS // RT, row_tile, 0)


def stats_own(ordk, posq, q0, q1, q2, q3, g0, g1, g2, g3, kva, out, qr, gr):
    fill_rows((q0, q1, q2, q3), qr)
    fill_rows((g0, g1, g2, g3), gr)
    stats_pass(0, ordk, posq, qr, gr, kva, None, out)


def pick_columns(place_ref, own, other, xs):
    ic = place_ref[1]
    src = lax.broadcasted_iota(jnp.int32, (512, 256), 0)
    dst = lax.broadcasted_iota(jnp.int32, (512, 256), 1)
    home = dst // 32 * 64 + dst % 32 + ic * 32
    pick = jnp.where(src == home, 1.0, 0.0).astype(bf16)
    for d, out in enumerate(xs):
        base = lax.rem(place_ref[0] + d, N_OUT) * 512
        for t, tok in enumerate((own, other)):
            for p in range(2):
                cols = tok[:, pl.ds(pl.multiple_of(base + p * 2048, 512), 512)]
                out[t, :, p * 256 : (p + 1) * 256] = dot(cols, pick, NN).astype(bf16)


def stats_other(
    ordk, place, posq, qr, gr, kvb, before, own, other, out, x0, x1, x2, x3
):
    stats_pass(KHALF // HALF, ordk, posq, qr, gr, kvb, before, out)
    pick_columns(place, own, other, (x0, x1, x2, x3))


def combine_stats(stats, rowstat_ref):
    for d in range(N_OUT):
        parts = []
        for e in range(N_OUT):
            c0 = slot_start(d - e)
            parts.append(stats[e][:, c0 : c0 + SLOT])
        row_top = parts[0][0:1]
        for part in parts[1:]:
            row_top = jnp.maximum(row_top, part[0:1])
        total = jnp.zeros_like(row_top)
        weighted = jnp.zeros_like(row_top)
        for part in parts:
            factor = jnp.exp2(part[0:1] - row_top)
            total = total + part[1:2] * factor
            weighted = weighted + part[2:3] * factor
        r0 = slot_start(d)
        rowstat_ref[0:1, r0 : r0 + SLOT] = row_top + jnp.log2(total)
        rowstat_ref[1:2, r0 : r0 + SLOT] = weighted / total


def grads_kernel(
    ordk, posq_ref, s0, s1, s2, s3, qr, gr, kva, kvb,
    dq0, dq1, dq2, dq3, keep, send, rowstat, dqr, dkv,
):
    combine_stats((s0, s1, s2, s3), rowstat)
    dkv[...] = jnp.zeros_like(dkv)

    def row_tile(rt, _):
        r0 = pl.multiple_of(rt * RT, RT)
        q = qr[pl.ds(r0, RT), :]
        g = gr[pl.ds(r0, RT), :]
        posq = posq_ref[:, pl.ds(r0, RT)]
        lse = rowstat[0:1, pl.ds(r0, RT)]
        delta = rowstat[1:2, pl.ds(r0, RT)]
        dq = jnp.zeros((RT, HEAD), f32)
        for chunk in range(KEYS // KC):
            kv = kva if chunk * KC < KHALF else kvb
            k0 = chunk * KC % KHALF
            key_rows = kv[k0 : k0 + KC, :HEAD]
            score = masked_scores(key_rows, q, posq, ordk, chunk * (KC // HALF))
            prob = jnp.exp2(score - lse)
            dprob = dot(kv[k0 : k0 + KC, HEAD:], g, NT)
            dscore = (prob * (dprob - delta)).astype(bf16)
            prob_low = prob.astype(bf16)
            dkv[chunk * KC : (chunk + 1) * KC, HEAD:] += dot(prob_low, g, NN)
            dkv[chunk * KC : (chunk + 1) * KC, :HEAD] += dot(dscore, q, NN)
            dq = dq + dot(dscore, key_rows, TN)
        dqr[pl.ds(r0, RT), :] = dq
        return 0

    lax.fori_loop(0, ALL_ROWS // RT, row_tile, 0)
    for d, out in enumerate((dq0, dq1, dq2, dq3)):
        for h in range(HEADS):
            r0 = slot_start(d) + h * ROWS
            out[:, h * HEAD : (h + 1) * HEAD] = (dqr[r0 : r0 + ROWS, :] * SCALE).astype(out.dtype)
    for out, k0 in ((keep, 0), (send, KHALF)):
        out[:, :HEAD] = (dkv[k0 : k0 + KHALF, :HEAD] * SCALE).astype(out.dtype)
        out[:, HEAD:] = dkv[k0 : k0 + KHALF, HEAD:].astype(out.dtype)


def weights_kernel(x0, x1, x2, x3, q0, q1, q2, q3, k0, k1, k2, k3, grads, out, xr, gr):
    wide = HEADS * HEAD
    for d, x in enumerate((x0, x1, x2, x3)):
        rows = slice(d * ROWS, (d + 1) * ROWS)
        other = slice((N_OUT + d) * ROWS, (N_OUT + d + 1) * ROWS)
        xr[rows, :] = x[0]
        xr[other, :] = x[1]
        gr[rows, :wide] = (q0, q1, q2, q3)[d][...]
        gr[rows, wide:] = (k0, k1, k2, k3)[d][...]
        gr[other, :] = grads[d]
    dw = dot(xr[...], gr[...], TN).astype(bf16)
    for p in range(16):
        out[p] = dw[p * 32 : (p + 1) * 32]


def last_sum(parts, dwq, dwk, dwv):
    total = jnp.sum(parts[...].astype(f32), axis=0)
    wide = HEADS * HEAD
    dwq[...] = total[:, :wide]
    dwk[...] = total[:, wide : wide + HEAD]
    dwv[...] = total[:, wide + HEAD :]


VM = 24
smem = pl.BlockSpec(memory_space=pltpu.SMEM)
vmem = pl.BlockSpec(memory_space=pltpu.VMEM)
params = pltpu.CompilerParams(vmem_limit_bytes=VM * 1024 * 1024)


def cost(pairs, matmuls, size):
    return pl.CostEstimate(
        flops=2 * pairs * HEAD * matmuls, transcendentals=pairs, bytes_accessed=size
    )


def kernel_call(body, name, outs, scratch, estimate, spaces, *args):
    return pl.pallas_call(
        body,
        out_shape=tuple(jax.ShapeDtypeStruct(*o) for o in outs),
        in_specs=spaces + [vmem] * (len(args) - len(spaces)),
        out_specs=tuple(vmem for _ in outs),
        scratch_shapes=[pltpu.VMEM(*s) for s in scratch],
        compiler_params=params,
        cost_estimate=estimate,
        name=name,
    )(*args)


WIDE = HEADS * HEAD
acc_rows = ((ALL_ROWS, HEAD), f32)


def shift(x, axis, d, n):
    return lax.ppermute(x, axis, [(i, (i + d) % n) for i in range(n)])


def from_behind(x, axis, n):
    return [x] + [shift(x, axis, d, n) for d in range(1, n)]


def per_device(inputs, block_order, w_query, w_key, w_value, grad_out):
    tokens = inputs[0]
    order = block_order[0]
    dout = grad_out[0]
    o, ix, iy, ic = (lax.axis_index(a) for a in ("outer", "x", "yh", "core"))

    query = dot(tokens, w_query, NN).astype(bf16)
    q1, q3 = shift(query, "outer", 1, N_OUT), shift(query, "outer", -1, N_OUT)
    g1, g3 = shift(dout, "outer", 1, N_OUT), shift(dout, "outer", -1, N_OUT)
    qs = [query, q1, shift(q1, "outer", 1, N_OUT), q3]
    gs = [dout, g1, shift(g3, "outer", -1, N_OUT), g3]
    kv = jnp.concatenate(
        [
            dot(tokens, w_key, NN).astype(bf16),
            dot(tokens, w_value, NN).astype(bf16),
        ],
        axis=1,
    )
    kva = jnp.broadcast_to(kv[None], (8,) + kv.shape)
    kva = lax.all_to_all(kva, ("x", "yh"), 0, 0, tiled=True).reshape(KHALF, 2 * HEAD)
    other_tokens = shift(tokens, "core", 1, 2)
    kva, qs, gs, other_tokens = lax.optimization_barrier((kva, qs, gs, other_tokens))
    kvb = shift(kva, "core", 1, 2)

    key_dev = (o * 8 + np.arange(8)[None, :, None]) * 2 + (ic + np.arange(2)[:, None, None]) % 2
    key_blocks = (key_dev * 2 + np.arange(2)[None, None, :]).reshape(-1)
    query_dev = (((o - np.array([1, 2, 3, 0])) % N_OUT * N_X + ix) * 2 + iy) * 2 + ic
    query_blocks = (query_dev[:, None] * 2 + np.arange(2)[None, :]).reshape(-1)

    def look_up(blocks):
        hit = blocks[:, None] == jnp.arange(order.shape[0], dtype=jnp.int32)[None, :]
        return jnp.sum(jnp.where(hit, order[None, :], 0), axis=1)

    ordk = look_up(key_blocks)
    ordq = look_up(query_blocks).reshape(N_OUT, 1, 2, 1)
    posq = ordq * HALF + jnp.arange(HALF, dtype=jnp.int32)
    posq = jnp.broadcast_to(posq, (N_OUT, HEADS, 2, HALF)).reshape(1, ALL_ROWS)

    pairs = cost(ALL_ROWS * KHALF, 2, 4 << 20)
    row_stats = [((3, ALL_ROWS), f32)]
    rows = ((ALL_ROWS, HEAD), bf16)
    stats, qr, gr = kernel_call(
        stats_own, "stats_own", row_stats + [rows, rows], [], pairs, [smem],
        ordk, posq, *qs, *gs, kva,
    )
    stats, *xs = kernel_call(
        stats_other, "stats_other", row_stats + [((2, ROWS, 512), bf16)] * N_OUT, [], pairs,
        [smem, smem],
        ordk, jnp.stack([o, ic]), posq, qr, gr, kvb, stats, tokens, other_tokens,
    )
    xs = [xs[0]] + [shift(xs[d], "outer", d, N_OUT) for d in range(1, N_OUT)]
    all_stats = from_behind(stats, "outer", N_OUT)

    half = (KHALF, 2 * HEAD)
    dq, dq1, dq2, dq3, keep, send = kernel_call(
        grads_kernel, "grads",
        [((ROWS, WIDE), f32)] + [((ROWS, WIDE), bf16)] * 3 + [(half, f32), (half, bf16)],
        [((2, ALL_ROWS), f32), acc_rows, ((KEYS, 2 * HEAD), f32)],
        cost(ALL_ROWS * KEYS, 5, 8 << 20), [smem], ordk, posq, *all_stats, qr, gr, kva, kvb,
    )
    send, dq1, dq2, dq3, xs = lax.optimization_barrier((send, dq1, dq2, dq3, xs))
    got = shift(send, "core", 1, 2)
    dq_parts = [shift(part, "outer", -d, N_OUT) for d, part in ((1, dq1), (2, dq2), (3, dq3))]
    dkv = (keep + got.astype(f32)).astype(bf16).reshape(8, ROWS, 2 * HEAD)
    dkv = lax.all_to_all(dkv, ("x", "yh"), 0, 0, tiled=True)
    dkv = jnp.sum(dkv.astype(f32), axis=0).astype(bf16)
    dkv_all = from_behind(dkv, "outer", N_OUT)
    for part in dq_parts:
        dq = dq + part.astype(f32)
    dq_all = from_behind(dq.astype(bf16), "outer", N_OUT)
    dq_all, dkv_all = lax.optimization_barrier((dq_all, dkv_all))

    grads = [jnp.concatenate(pair, axis=1) for pair in zip(dq_all, dkv_all)]
    other_grads = shift(jnp.stack(grads), "core", 1, 2)
    (dw,) = kernel_call(
        weights_kernel, "weights", [((16, 32, 768), bf16)],
        [((2 * N_OUT * ROWS, 512), bf16), ((2 * N_OUT * ROWS, 768), bf16)],
        cost(1280 * 512, 6, 4 << 20), [],
        *xs, *dq_all, *dkv_all, other_grads,
    )
    dw = lax.all_to_all(dw, ("dp", "x", "yh"), 0, 0, tiled=True)
    return kernel_call(
        last_sum, "last_sum", [((32, WIDE), f32), ((32, HEAD), f32), ((32, HEAD), f32)], [],
        cost(32 * 16, 3, 1 << 20), [], dw,
    )


def solution(mesh):
    devices = np.asarray(mesh.devices).reshape(2, N_OUT, N_X, 2, 2)
    fine = Mesh(devices, ("dp", "outer", "x", "yh", "core"))
    seq = ("outer", "x", "yh", "core")
    rows = P(("dp",) + seq, None)
    return jax.shard_map(
        per_device,
        mesh=fine,
        in_specs=(
            P("dp", seq, None),
            P("dp", None),
            P(None, None),
            P(None, None),
            P(None, None),
            P("dp", seq, None),
        ),
        out_specs=(rows, rows, rows),
        check_vma=False,
    )
```

```python
import functools
import math

import jax
import jax.numpy as jnp
import numpy as np
from jax import lax
from jax.experimental import pallas as pl
from jax.experimental.pallas import tpu as pltpu
from jax.sharding import Mesh, PartitionSpec as P

masked_fill = -1e30
HEADS = 4
HEAD = 128
ROWS = 160
HALF = 80
N_OUT = 4
N_X = 4
SLOT = HEADS * ROWS
ALL_ROWS = N_OUT * SLOT
KEYS = 16 * ROWS
KHALF = KEYS // 2
RT = 1280
KC = 640
KS = 160
SCALE = 1.0 / math.sqrt(HEAD)
SCALE2 = SCALE * math.log2(math.e)
f32 = jnp.float32
bf16 = jnp.bfloat16
NT = (((1,), (1,)), ((), ()))
NN = (((1,), (0,)), ((), ()))
TN = (((0,), (0,)), ((), ()))


def dot(a, b, dims):
    return lax.dot_general(a, b, dims, preferred_element_type=f32)


def slot_start(d):
    return (d - 1) % N_OUT * SLOT


def fill_rows(pieces, rows_ref):
    for d in range(N_OUT):
        for h in range(HEADS):
            r0 = slot_start(d) + h * ROWS
            rows_ref[r0 : r0 + ROWS, :] = pieces[d][:, h * HEAD : (h + 1) * HEAD]


def masked_scores(key_rows, q, posq, ordk_ref, block):
    score = dot(key_rows, q, NT)
    place = lax.broadcasted_iota(jnp.int32, (HALF, RT), 0)
    parts = []
    for b in range(score.shape[0] // HALF):
        limit = posq - ordk_ref[block + b] * HALF
        part = score[b * HALF : (b + 1) * HALF] * SCALE2
        parts.append(jnp.where(place <= limit, part, masked_fill))
    return jnp.concatenate(parts, axis=0)


def stats_pass(block, ordk_ref, posq_ref, qr, gr, kv, before, out_ref):
    def row_tile(rt, _):
        r0 = pl.multiple_of(rt * RT, RT)
        q = qr[pl.ds(r0, RT), :]
        g = gr[pl.ds(r0, RT), :]
        posq = posq_ref[:, pl.ds(r0, RT)]
        top = jnp.full((8, RT), masked_fill, f32)
        total = jnp.zeros((8, RT), f32)
        weighted = jnp.zeros((8, RT), f32)
        for k0 in range(0, KHALF, KS):
            score = masked_scores(kv[k0 : k0 + KS, :HEAD], q, posq, ordk_ref, block + k0 // HALF)
            dprob = dot(kv[k0 : k0 + KS, HEAD:], g, NT)
            score = score.reshape(KS // 8, 8, RT)
            new_top = jnp.maximum(top, jnp.max(score, axis=0))
            weights = jnp.exp2(score - new_top[None])
            factor = jnp.exp2(top - new_top)
            total = total * factor + jnp.sum(weights, axis=0)
            weighted = weighted * factor + jnp.sum(weights * dprob.reshape(KS // 8, 8, RT), axis=0)
            top = new_top
        row_top = jnp.max(top, axis=0, keepdims=True)
        if before is not None:
            row_top = jnp.maximum(row_top, before[0:1, pl.ds(r0, RT)])
        factor = jnp.exp2(top - row_top)
        total = jnp.sum(total * factor, axis=0, keepdims=True)
        weighted = jnp.sum(weighted * factor, axis=0, keepdims=True)
        if before is not None:
            factor = jnp.exp2(before[0:1, pl.ds(r0, RT)] - row_top)
            total = total + before[1:2, pl.ds(r0, RT)] * factor
            weighted = weighted + before[2:3, pl.ds(r0, RT)] * factor
        out_ref[0:1, pl.ds(r0, RT)] = row_top
        out_ref[1:2, pl.ds(r0, RT)] = total
        out_ref[2:3, pl.ds(r0, RT)] = weighted
        return 0

    lax.fori_loop(0, ALL_ROWS // RT, row_tile, 0)


def stats_own(ordk, posq, q0, q1, q2, q3, g0, g1, g2, g3, kva, out, qr, gr):
    fill_rows((q0, q1, q2, q3), qr)
    fill_rows((g0, g1, g2, g3), gr)
    stats_pass(0, ordk, posq, qr, gr, kva, None, out)


def pick_columns(place_ref, own, other, xs):
    ic = place_ref[1]
    src = lax.broadcasted_iota(jnp.int32, (512, 256), 0)
    dst = lax.broadcasted_iota(jnp.int32, (512, 256), 1)
    home = dst // 32 * 64 + dst % 32 + ic * 32
    pick = jnp.where(src == home, 1.0, 0.0).astype(bf16)
    for d, out in enumerate(xs):
        base = lax.rem(place_ref[0] + d, N_OUT) * 512
        for t, tok in enumerate((own, other)):
            for p in range(2):
                cols = tok[:, pl.ds(pl.multiple_of(base + p * 2048, 512), 512)]
                out[t, :, p * 256 : (p + 1) * 256] = dot(cols, pick, NN).astype(bf16)


def stats_other(
    ordk, place, posq, qr, gr, kvb, before, own, other, out, x0, x1, x2, x3
):
    stats_pass(KHALF // HALF, ordk, posq, qr, gr, kvb, before, out)
    pick_columns(place, own, other, (x0, x1, x2, x3))


def combine_stats(stats, rowstat_ref):
    for d in range(N_OUT):
        parts = []
        for e in range(N_OUT):
            c0 = slot_start(d - e)
            parts.append(stats[e][:, c0 : c0 + SLOT])
        row_top = parts[0][0:1]
        for part in parts[1:]:
            row_top = jnp.maximum(row_top, part[0:1])
        total = jnp.zeros_like(row_top)
        weighted = jnp.zeros_like(row_top)
        for part in parts:
            factor = jnp.exp2(part[0:1] - row_top)
            total = total + part[1:2] * factor
            weighted = weighted + part[2:3] * factor
        r0 = slot_start(d)
        rowstat_ref[0:1, r0 : r0 + SLOT] = row_top + jnp.log2(total)
        rowstat_ref[1:2, r0 : r0 + SLOT] = weighted / total


def grads_kernel(
    ordk, posq_ref, s0, s1, s2, s3, qr, gr, kva, kvb,
    dq0, dq1, dq2, dq3, keep, send, rowstat, dqr, dkv,
):
    combine_stats((s0, s1, s2, s3), rowstat)
    dkv[...] = jnp.zeros_like(dkv)

    def row_tile(rt, _):
        r0 = pl.multiple_of(rt * RT, RT)
        q = qr[pl.ds(r0, RT), :]
        g = gr[pl.ds(r0, RT), :]
        posq = posq_ref[:, pl.ds(r0, RT)]
        lse = rowstat[0:1, pl.ds(r0, RT)]
        delta = rowstat[1:2, pl.ds(r0, RT)]
        dq = jnp.zeros((RT, HEAD), f32)
        for chunk in range(KEYS // KC):
            kv = kva if chunk * KC < KHALF else kvb
            k0 = chunk * KC % KHALF
            key_rows = kv[k0 : k0 + KC, :HEAD]
            score = masked_scores(key_rows, q, posq, ordk, chunk * (KC // HALF))
            prob = jnp.exp2(score - lse)
            dprob = dot(kv[k0 : k0 + KC, HEAD:], g, NT)
            dscore = (prob * (dprob - delta)).astype(bf16)
            prob_low = prob.astype(bf16)
            dkv[chunk * KC : (chunk + 1) * KC, HEAD:] += dot(prob_low, g, NN)
            dkv[chunk * KC : (chunk + 1) * KC, :HEAD] += dot(dscore, q, NN)
            dq = dq + dot(dscore, key_rows, TN)
        dqr[pl.ds(r0, RT), :] = dq
        return 0

    lax.fori_loop(0, ALL_ROWS // RT, row_tile, 0)
    for d, out in enumerate((dq0, dq1, dq2, dq3)):
        for h in range(HEADS):
            r0 = slot_start(d) + h * ROWS
            out[:, h * HEAD : (h + 1) * HEAD] = (dqr[r0 : r0 + ROWS, :] * SCALE).astype(out.dtype)
    for out, k0 in ((keep, 0), (send, KHALF)):
        out[:, :HEAD] = (dkv[k0 : k0 + KHALF, :HEAD] * SCALE).astype(out.dtype)
        out[:, HEAD:] = dkv[k0 : k0 + KHALF, HEAD:].astype(out.dtype)


def weights_kernel(x0, x1, x2, x3, q0, q1, q2, q3, k0, k1, k2, k3, grads, out, xr, gr):
    wide = HEADS * HEAD
    for d, x in enumerate((x0, x1, x2, x3)):
        rows = slice(d * ROWS, (d + 1) * ROWS)
        other = slice((N_OUT + d) * ROWS, (N_OUT + d + 1) * ROWS)
        xr[rows, :] = x[0]
        xr[other, :] = x[1]
        gr[rows, :wide] = (q0, q1, q2, q3)[d][...]
        gr[rows, wide:] = (k0, k1, k2, k3)[d][...]
        gr[other, :] = grads[d]
    dw = dot(xr[...], gr[...], TN).astype(bf16)
    for p in range(16):
        out[p] = dw[p * 32 : (p + 1) * 32]


def last_sum(parts, dwq, dwk, dwv):
    total = jnp.sum(parts[...].astype(f32), axis=0)
    wide = HEADS * HEAD
    dwq[...] = total[:, :wide]
    dwk[...] = total[:, wide : wide + HEAD]
    dwv[...] = total[:, wide + HEAD :]


VM = 24
smem = pl.BlockSpec(memory_space=pltpu.SMEM)
vmem = pl.BlockSpec(memory_space=pltpu.VMEM)
params = pltpu.CompilerParams(vmem_limit_bytes=VM * 1024 * 1024)


def cost(pairs, matmuls, size):
    return pl.CostEstimate(
        flops=2 * pairs * HEAD * matmuls, transcendentals=pairs, bytes_accessed=size
    )


def kernel_call(body, name, outs, scratch, estimate, spaces, *args):
    return pl.pallas_call(
        body,
        out_shape=tuple(jax.ShapeDtypeStruct(*o) for o in outs),
        in_specs=spaces + [vmem] * (len(args) - len(spaces)),
        out_specs=tuple(vmem for _ in outs),
        scratch_shapes=[pltpu.VMEM(*s) for s in scratch],
        compiler_params=params,
        cost_estimate=estimate,
        name=name,
    )(*args)


WIDE = HEADS * HEAD
acc_rows = ((ALL_ROWS, HEAD), f32)


def shift(x, axis, d, n):
    return lax.ppermute(x, axis, [(i, (i + d) % n) for i in range(n)])


def from_behind(x, axis, n):
    return [x] + [shift(x, axis, d, n) for d in range(1, n)]


def per_device(inputs, block_order, w_query, w_key, w_value, grad_out):
    tokens = inputs[0]
    order = block_order[0]
    dout = grad_out[0]
    o, ix, iy, ic = (lax.axis_index(a) for a in ("outer", "x", "yh", "core"))

    query = dot(tokens, w_query, NN).astype(bf16)
    q1, q3 = shift(query, "outer", 1, N_OUT), shift(query, "outer", -1, N_OUT)
    g1, g3 = shift(dout, "outer", 1, N_OUT), shift(dout, "outer", -1, N_OUT)
    qs = [query, q1, shift(q1, "outer", 1, N_OUT), q3]
    gs = [dout, g1, shift(g3, "outer", -1, N_OUT), g3]
    kv = jnp.concatenate(
        [
            dot(tokens, w_key, NN).astype(bf16),
            dot(tokens, w_value, NN).astype(bf16),
        ],
        axis=1,
    )
    kva = jnp.broadcast_to(kv[None], (8,) + kv.shape)
    kva = lax.all_to_all(kva, ("x", "yh"), 0, 0, tiled=True).reshape(KHALF, 2 * HEAD)
    later, _ = lax.optimization_barrier((tokens, (qs[2], gs[2])))
    other_tokens = shift(later, "core", 1, 2)
    kva, qs, gs = lax.optimization_barrier((kva, qs, gs))
    kvb = shift(kva, "core", 1, 2)

    key_dev = (o * 8 + np.arange(8)[None, :, None]) * 2 + (ic + np.arange(2)[:, None, None]) % 2
    key_blocks = (key_dev * 2 + np.arange(2)[None, None, :]).reshape(-1)
    query_dev = (((o - np.array([1, 2, 3, 0])) % N_OUT * N_X + ix) * 2 + iy) * 2 + ic
    query_blocks = (query_dev[:, None] * 2 + np.arange(2)[None, :]).reshape(-1)

    def look_up(blocks):
        hit = blocks[:, None] == jnp.arange(order.shape[0], dtype=jnp.int32)[None, :]
        return jnp.sum(jnp.where(hit, order[None, :], 0), axis=1)

    ordk = look_up(key_blocks)
    ordq = look_up(query_blocks).reshape(N_OUT, 1, 2, 1)
    posq = ordq * HALF + jnp.arange(HALF, dtype=jnp.int32)
    posq = jnp.broadcast_to(posq, (N_OUT, HEADS, 2, HALF)).reshape(1, ALL_ROWS)

    pairs = cost(ALL_ROWS * KHALF, 2, 4 << 20)
    row_stats = [((3, ALL_ROWS), f32)]
    rows = ((ALL_ROWS, HEAD), bf16)
    stats, qr, gr = kernel_call(
        stats_own, "stats_own", row_stats + [rows, rows], [], pairs, [smem],
        ordk, posq, *qs, *gs, kva,
    )
    stats, *xs = kernel_call(
        stats_other, "stats_other", row_stats + [((2, ROWS, 512), bf16)] * N_OUT, [], pairs,
        [smem, smem],
        ordk, jnp.stack([o, ic]), posq, qr, gr, kvb, stats, tokens, other_tokens,
    )
    xs = [xs[0]] + [shift(xs[d], "outer", d, N_OUT) for d in range(1, N_OUT)]
    all_stats = from_behind(stats, "outer", N_OUT)

    half = (KHALF, 2 * HEAD)
    dq, dq1, dq2, dq3, keep, send = kernel_call(
        grads_kernel, "grads",
        [((ROWS, WIDE), f32)] + [((ROWS, WIDE), bf16)] * 3 + [(half, f32), (half, bf16)],
        [((2, ALL_ROWS), f32), acc_rows, ((KEYS, 2 * HEAD), f32)],
        cost(ALL_ROWS * KEYS, 5, 8 << 20), [smem], ordk, posq, *all_stats, qr, gr, kva, kvb,
    )
    send, dq1, dq2, dq3, xs = lax.optimization_barrier((send, dq1, dq2, dq3, xs))
    got = shift(send, "core", 1, 2)
    dq_parts = [shift(part, "outer", -d, N_OUT) for d, part in ((1, dq1), (2, dq2), (3, dq3))]
    dkv = (keep + got.astype(f32)).astype(bf16).reshape(8, ROWS, 2 * HEAD)
    dkv = lax.all_to_all(dkv, ("x", "yh"), 0, 0, tiled=True)
    dkv = jnp.sum(dkv.astype(f32), axis=0).astype(bf16)
    dkv_all = from_behind(dkv, "outer", N_OUT)
    for part in dq_parts:
        dq = dq + part.astype(f32)
    dq_all = from_behind(dq.astype(bf16), "outer", N_OUT)
    dq_all, dkv_all = lax.optimization_barrier((dq_all, dkv_all))

    grads = [jnp.concatenate(pair, axis=1) for pair in zip(dq_all, dkv_all)]
    other_grads = shift(jnp.stack(grads), "core", 1, 2)
    (dw,) = kernel_call(
        weights_kernel, "weights", [((16, 32, 768), bf16)],
        [((2 * N_OUT * ROWS, 512), bf16), ((2 * N_OUT * ROWS, 768), bf16)],
        cost(1280 * 512, 6, 4 << 20), [],
        *xs, *dq_all, *dkv_all, other_grads,
    )
    dw = lax.all_to_all(dw, ("dp", "x", "yh"), 0, 0, tiled=True)
    return kernel_call(
        last_sum, "last_sum", [((32, WIDE), f32), ((32, HEAD), f32), ((32, HEAD), f32)], [],
        cost(32 * 16, 3, 1 << 20), [], dw,
    )


def solution(mesh):
    devices = np.asarray(mesh.devices).reshape(2, N_OUT, N_X, 2, 2)
    fine = Mesh(devices, ("dp", "outer", "x", "yh", "core"))
    seq = ("outer", "x", "yh", "core")
    rows = P(("dp",) + seq, None)
    return jax.shard_map(
        per_device,
        mesh=fine,
        in_specs=(
            P("dp", seq, None),
            P("dp", None),
            P(None, None),
            P(None, None),
            P(None, None),
            P("dp", seq, None),
        ),
        out_specs=(rows, rows, rows),
        check_vma=False,
    )
```

```python
import functools
import math

import jax
import jax.numpy as jnp
import numpy as np
from jax import lax
from jax.experimental import pallas as pl
from jax.experimental.pallas import tpu as pltpu
from jax.sharding import Mesh, PartitionSpec as P

masked_fill = -1e30
HEADS = 4
HEAD = 128
ROWS = 160
HALF = 80
N_OUT = 4
N_X = 4
SLOT = HEADS * ROWS
ALL_ROWS = N_OUT * SLOT
KEYS = 16 * ROWS
KHALF = KEYS // 2
RT = 1280
KC = 640
KS = 640
SCALE = 1.0 / math.sqrt(HEAD)
SCALE2 = SCALE * math.log2(math.e)
f32 = jnp.float32
bf16 = jnp.bfloat16
NT = (((1,), (1,)), ((), ()))
NN = (((1,), (0,)), ((), ()))
TN = (((0,), (0,)), ((), ()))


def dot(a, b, dims):
    return lax.dot_general(a, b, dims, preferred_element_type=f32)


def slot_start(d):
    return (d - 1) % N_OUT * SLOT


def fill_rows(pieces, rows_ref):
    for d in range(N_OUT):
        for h in range(HEADS):
            r0 = slot_start(d) + h * ROWS
            rows_ref[r0 : r0 + ROWS, :] = pieces[d][:, h * HEAD : (h + 1) * HEAD]


def masked_scores(key_rows, q, posq, ordk_ref, block):
    score = dot(key_rows, q, NT)
    place = lax.broadcasted_iota(jnp.int32, (HALF, RT), 0)
    parts = []
    for b in range(score.shape[0] // HALF):
        limit = posq - ordk_ref[block + b] * HALF
        part = score[b * HALF : (b + 1) * HALF] * SCALE2
        parts.append(jnp.where(place <= limit, part, masked_fill))
    return jnp.concatenate(parts, axis=0)


def stats_pass(block, ordk_ref, posq_ref, qr, gr, kv, before, out_ref):
    def row_tile(rt, _):
        r0 = pl.multiple_of(rt * RT, RT)
        q = qr[pl.ds(r0, RT), :]
        g = gr[pl.ds(r0, RT), :]
        posq = posq_ref[:, pl.ds(r0, RT)]
        top = jnp.full((8, RT), masked_fill, f32)
        total = jnp.zeros((8, RT), f32)
        weighted = jnp.zeros((8, RT), f32)
        for k0 in range(0, KHALF, KS):
            score = masked_scores(kv[k0 : k0 + KS, :HEAD], q, posq, ordk_ref, block + k0 // HALF)
            dprob = dot(kv[k0 : k0 + KS, HEAD:], g, NT)
            score = score.reshape(KS // 8, 8, RT)
            new_top = jnp.maximum(top, jnp.max(score, axis=0))
            weights = jnp.exp2(score - new_top[None])
            factor = jnp.exp2(top - new_top)
            total = total * factor + jnp.sum(weights, axis=0)
            weighted = weighted * factor + jnp.sum(weights * dprob.reshape(KS // 8, 8, RT), axis=0)
            top = new_top
        row_top = jnp.max(top, axis=0, keepdims=True)
        if before is not None:
            row_top = jnp.maximum(row_top, before[0:1, pl.ds(r0, RT)])
        factor = jnp.exp2(top - row_top)
        total = jnp.sum(total * factor, axis=0, keepdims=True)
        weighted = jnp.sum(weighted * factor, axis=0, keepdims=True)
        if before is not None:
            factor = jnp.exp2(before[0:1, pl.ds(r0, RT)] - row_top)
            total = total + before[1:2, pl.ds(r0, RT)] * factor
            weighted = weighted + before[2:3, pl.ds(r0, RT)] * factor
        out_ref[0:1, pl.ds(r0, RT)] = row_top
        out_ref[1:2, pl.ds(r0, RT)] = total
        out_ref[2:3, pl.ds(r0, RT)] = weighted
        return 0

    lax.fori_loop(0, ALL_ROWS // RT, row_tile, 0)


def stats_own(ordk, posq, q0, q1, q2, q3, g0, g1, g2, g3, kva, out, qr, gr):
    fill_rows((q0, q1, q2, q3), qr)
    fill_rows((g0, g1, g2, g3), gr)
    stats_pass(0, ordk, posq, qr, gr, kva, None, out)


def pick_columns(place_ref, own, other, xs):
    ic = place_ref[1]
    src = lax.broadcasted_iota(jnp.int32, (512, 256), 0)
    dst = lax.broadcasted_iota(jnp.int32, (512, 256), 1)
    home = dst // 32 * 64 + dst % 32 + ic * 32
    pick = jnp.where(src == home, 1.0, 0.0).astype(bf16)
    for d, out in enumerate(xs):
        base = lax.rem(place_ref[0] + d, N_OUT) * 512
        for t, tok in enumerate((own, other)):
            for p in range(2):
                cols = tok[:, pl.ds(pl.multiple_of(base + p * 2048, 512), 512)]
                out[t, :, p * 256 : (p + 1) * 256] = dot(cols, pick, NN).astype(bf16)


def stats_other(
    ordk, place, posq, qr, gr, kvb, before, own, other, out, x0, x1, x2, x3
):
    stats_pass(KHALF // HALF, ordk, posq, qr, gr, kvb, before, out)
    pick_columns(place, own, other, (x0, x1, x2, x3))


def combine_stats(stats, rowstat_ref):
    for d in range(N_OUT):
        parts = []
        for e in range(N_OUT):
            c0 = slot_start(d - e)
            parts.append(stats[e][:, c0 : c0 + SLOT])
        row_top = parts[0][0:1]
        for part in parts[1:]:
            row_top = jnp.maximum(row_top, part[0:1])
        total = jnp.zeros_like(row_top)
        weighted = jnp.zeros_like(row_top)
        for part in parts:
            factor = jnp.exp2(part[0:1] - row_top)
            total = total + part[1:2] * factor
            weighted = weighted + part[2:3] * factor
        r0 = slot_start(d)
        rowstat_ref[0:1, r0 : r0 + SLOT] = row_top + jnp.log2(total)
        rowstat_ref[1:2, r0 : r0 + SLOT] = weighted / total


def grads_kernel(
    ordk, posq_ref, s0, s1, s2, s3, qr, gr, kva, kvb,
    dq0, dq1, dq2, dq3, keep, send, rowstat, dqr, dkv,
):
    combine_stats((s0, s1, s2, s3), rowstat)
    dkv[...] = jnp.zeros_like(dkv)

    def row_tile(rt, _):
        r0 = pl.multiple_of(rt * RT, RT)
        q = qr[pl.ds(r0, RT), :]
        g = gr[pl.ds(r0, RT), :]
        posq = posq_ref[:, pl.ds(r0, RT)]
        lse = rowstat[0:1, pl.ds(r0, RT)]
        delta = rowstat[1:2, pl.ds(r0, RT)]
        dq = jnp.zeros((RT, HEAD), f32)
        for chunk in range(KEYS // KC):
            kv = kva if chunk * KC < KHALF else kvb
            k0 = chunk * KC % KHALF
            key_rows = kv[k0 : k0 + KC, :HEAD]
            score = masked_scores(key_rows, q, posq, ordk, chunk * (KC // HALF))
            prob = jnp.exp2(score - lse)
            dprob = dot(kv[k0 : k0 + KC, HEAD:], g, NT)
            dscore = (prob * (dprob - delta)).astype(bf16)
            prob_low = prob.astype(bf16)
            dkv[chunk * KC : (chunk + 1) * KC, HEAD:] += dot(prob_low, g, NN)
            dkv[chunk * KC : (chunk + 1) * KC, :HEAD] += dot(dscore, q, NN)
            dq = dq + dot(dscore, key_rows, TN)
        dqr[pl.ds(r0, RT), :] = dq
        return 0

    lax.fori_loop(0, ALL_ROWS // RT, row_tile, 0)
    for d, out in enumerate((dq0, dq1, dq2, dq3)):
        for h in range(HEADS):
            r0 = slot_start(d) + h * ROWS
            out[:, h * HEAD : (h + 1) * HEAD] = (dqr[r0 : r0 + ROWS, :] * SCALE).astype(out.dtype)
    for out, k0 in ((keep, 0), (send, KHALF)):
        out[:, :HEAD] = (dkv[k0 : k0 + KHALF, :HEAD] * SCALE).astype(out.dtype)
        out[:, HEAD:] = dkv[k0 : k0 + KHALF, HEAD:].astype(out.dtype)


def weights_kernel(x0, x1, x2, x3, q0, q1, q2, q3, k0, k1, k2, k3, grads, out, xr, gr):
    wide = HEADS * HEAD
    for d, x in enumerate((x0, x1, x2, x3)):
        rows = slice(d * ROWS, (d + 1) * ROWS)
        other = slice((N_OUT + d) * ROWS, (N_OUT + d + 1) * ROWS)
        xr[rows, :] = x[0]
        xr[other, :] = x[1]
        gr[rows, :wide] = (q0, q1, q2, q3)[d][...]
        gr[rows, wide:] = (k0, k1, k2, k3)[d][...]
        gr[other, :] = grads[d]
    dw = dot(xr[...], gr[...], TN).astype(bf16)
    for p in range(16):
        out[p] = dw[p * 32 : (p + 1) * 32]


def last_sum(parts, dwq, dwk, dwv):
    total = jnp.sum(parts[...].astype(f32), axis=0)
    wide = HEADS * HEAD
    dwq[...] = total[:, :wide]
    dwk[...] = total[:, wide : wide + HEAD]
    dwv[...] = total[:, wide + HEAD :]


VM = 24
smem = pl.BlockSpec(memory_space=pltpu.SMEM)
vmem = pl.BlockSpec(memory_space=pltpu.VMEM)
params = pltpu.CompilerParams(vmem_limit_bytes=VM * 1024 * 1024)


def cost(pairs, matmuls, size):
    return pl.CostEstimate(
        flops=2 * pairs * HEAD * matmuls, transcendentals=pairs, bytes_accessed=size
    )


def kernel_call(body, name, outs, scratch, estimate, spaces, *args):
    return pl.pallas_call(
        body,
        out_shape=tuple(jax.ShapeDtypeStruct(*o) for o in outs),
        in_specs=spaces + [vmem] * (len(args) - len(spaces)),
        out_specs=tuple(vmem for _ in outs),
        scratch_shapes=[pltpu.VMEM(*s) for s in scratch],
        compiler_params=params,
        cost_estimate=estimate,
        name=name,
    )(*args)


WIDE = HEADS * HEAD
acc_rows = ((ALL_ROWS, HEAD), f32)


def shift(x, axis, d, n):
    return lax.ppermute(x, axis, [(i, (i + d) % n) for i in range(n)])


def from_behind(x, axis, n):
    return [x] + [shift(x, axis, d, n) for d in range(1, n)]


def per_device(inputs, block_order, w_query, w_key, w_value, grad_out):
    tokens = inputs[0]
    order = block_order[0]
    dout = grad_out[0]
    o, ix, iy, ic = (lax.axis_index(a) for a in ("outer", "x", "yh", "core"))

    query = dot(tokens, w_query, NN).astype(bf16)
    q1, q3 = shift(query, "outer", 1, N_OUT), shift(query, "outer", -1, N_OUT)
    g1, g3 = shift(dout, "outer", 1, N_OUT), shift(dout, "outer", -1, N_OUT)
    qs = [query, q1, shift(q1, "outer", 1, N_OUT), q3]
    gs = [dout, g1, shift(g3, "outer", -1, N_OUT), g3]
    kv = jnp.concatenate(
        [
            dot(tokens, w_key, NN).astype(bf16),
            dot(tokens, w_value, NN).astype(bf16),
        ],
        axis=1,
    )
    kva = jnp.broadcast_to(kv[None], (8,) + kv.shape)
    kva = lax.all_to_all(kva, ("x", "yh"), 0, 0, tiled=True).reshape(KHALF, 2 * HEAD)
    later, _ = lax.optimization_barrier((tokens, (qs[2], gs[2])))
    other_tokens = shift(later, "core", 1, 2)
    kva, qs, gs = lax.optimization_barrier((kva, qs, gs))
    kvb = shift(kva, "core", 1, 2)

    key_dev = (o * 8 + np.arange(8)[None, :, None]) * 2 + (ic + np.arange(2)[:, None, None]) % 2
    key_blocks = (key_dev * 2 + np.arange(2)[None, None, :]).reshape(-1)
    query_dev = (((o - np.array([1, 2, 3, 0])) % N_OUT * N_X + ix) * 2 + iy) * 2 + ic
    query_blocks = (query_dev[:, None] * 2 + np.arange(2)[None, :]).reshape(-1)

    def look_up(blocks):
        hit = blocks[:, None] == jnp.arange(order.shape[0], dtype=jnp.int32)[None, :]
        return jnp.sum(jnp.where(hit, order[None, :], 0), axis=1)

    ordk = look_up(key_blocks)
    ordq = look_up(query_blocks).reshape(N_OUT, 1, 2, 1)
    posq = ordq * HALF + jnp.arange(HALF, dtype=jnp.int32)
    posq = jnp.broadcast_to(posq, (N_OUT, HEADS, 2, HALF)).reshape(1, ALL_ROWS)

    pairs = cost(ALL_ROWS * KHALF, 2, 4 << 20)
    row_stats = [((3, ALL_ROWS), f32)]
    rows = ((ALL_ROWS, HEAD), bf16)
    stats, qr, gr = kernel_call(
        stats_own, "stats_own", row_stats + [rows, rows], [], pairs, [smem],
        ordk, posq, *qs, *gs, kva,
    )
    stats, *xs = kernel_call(
        stats_other, "stats_other", row_stats + [((2, ROWS, 512), bf16)] * N_OUT, [], pairs,
        [smem, smem],
        ordk, jnp.stack([o, ic]), posq, qr, gr, kvb, stats, tokens, other_tokens,
    )
    xs = [xs[0]] + [shift(xs[d], "outer", d, N_OUT) for d in range(1, N_OUT)]
    all_stats = from_behind(stats, "outer", N_OUT)

    half = (KHALF, 2 * HEAD)
    dq, dq1, dq2, dq3, keep, send = kernel_call(
        grads_kernel, "grads",
        [((ROWS, WIDE), f32)] + [((ROWS, WIDE), bf16)] * 3 + [(half, f32), (half, bf16)],
        [((2, ALL_ROWS), f32), acc_rows, ((KEYS, 2 * HEAD), f32)],
        cost(ALL_ROWS * KEYS, 5, 8 << 20), [smem], ordk, posq, *all_stats, qr, gr, kva, kvb,
    )
    send, dq1, dq2, dq3, xs = lax.optimization_barrier((send, dq1, dq2, dq3, xs))
    got = shift(send, "core", 1, 2)
    dq_parts = [shift(part, "outer", -d, N_OUT) for d, part in ((1, dq1), (2, dq2), (3, dq3))]
    dkv = (keep + got.astype(f32)).astype(bf16).reshape(8, ROWS, 2 * HEAD)
    dkv = lax.all_to_all(dkv, ("x", "yh"), 0, 0, tiled=True)
    dkv = jnp.sum(dkv.astype(f32), axis=0).astype(bf16)
    dkv_all = from_behind(dkv, "outer", N_OUT)
    for part in dq_parts:
        dq = dq + part.astype(f32)
    dq_all = from_behind(dq.astype(bf16), "outer", N_OUT)
    dq_all, dkv_all = lax.optimization_barrier((dq_all, dkv_all))

    grads = [jnp.concatenate(pair, axis=1) for pair in zip(dq_all, dkv_all)]
    other_grads = shift(jnp.stack(grads), "core", 1, 2)
    (dw,) = kernel_call(
        weights_kernel, "weights", [((16, 32, 768), bf16)],
        [((2 * N_OUT * ROWS, 512), bf16), ((2 * N_OUT * ROWS, 768), bf16)],
        cost(1280 * 512, 6, 4 << 20), [],
        *xs, *dq_all, *dkv_all, other_grads,
    )
    dw = lax.all_to_all(dw, ("dp", "x", "yh"), 0, 0, tiled=True)
    return kernel_call(
        last_sum, "last_sum", [((32, WIDE), f32), ((32, HEAD), f32), ((32, HEAD), f32)], [],
        cost(32 * 16, 3, 1 << 20), [], dw,
    )


def solution(mesh):
    devices = np.asarray(mesh.devices).reshape(2, N_OUT, N_X, 2, 2)
    fine = Mesh(devices, ("dp", "outer", "x", "yh", "core"))
    seq = ("outer", "x", "yh", "core")
    rows = P(("dp",) + seq, None)
    return jax.shard_map(
        per_device,
        mesh=fine,
        in_specs=(
            P("dp", seq, None),
            P("dp", None),
            P(None, None),
            P(None, None),
            P(None, None),
            P("dp", seq, None),
        ),
        out_specs=(rows, rows, rows),
        check_vma=False,
    )
```
